128 devices in a mesh: seq: 32 (over z, x, core), mp: 4 (over y).
Axes of the slice: x: 4, y: 4, z: 4, core: 2. Of those that a mesh axis runs over, the one named last changes fastest.
Arguments:
- scan_points: bfloat16 [65536, 512], P('seq'), may hold values from -6 to 6
- send_order: int32 [65536], P('seq'), may hold values from 0 to 2047, as said below
- arrive_order: int32 [65536], P('seq'), may hold values from 0 to 2047, as said below
- qkv_weight: bfloat16 [512, 3, 512], P(None, None, 'mp')
- out_weight: bfloat16 [512, 512], P(None, 'mp'), may hold values from -0.25 to 0.25
- voxel_grads: bfloat16 [65536, 512], P('seq'), may hold values from -6 to 6
- voxel_shard: int32 [65536, 1], P('seq'), may hold values from 0 to 31; in each aligned block of 2048 rows (0 to 2047, 2048 to 4095, ...) at most 128 rows name the same one
- voxel_point: int32 [65536], P('seq'), may hold values from 0 to 2047
Outputs:
- d_points: float32 [65536, 512], P('seq', 'mp')
- grad_qkv: float32 [512, 3, 512], P('seq', None, 'mp')
- grad_out: float32 [512, 512], P('seq', 'mp')
The draws below stay inside these ranges and needn't reach their ends.
Inputs may be any that keep to these rules, and one draw needn't show every extreme that they name: `send_order`: each aligned block of 2048 entries is a permutation of the numbers 0 to 2047. `arrive_order`: each aligned block of 2048 entries is a permutation of the numbers 0 to 2047. `voxel_shard`: among the rows of one device, at most 128 name the same shard.
All inputs are finite; a program needn't handle non-finite values.
Results may differ from the reference program's by a relative error of at most 0.035.
The reference program's roundings to bfloat16 on the way (of `points`, `hidden`, `projected`, `d_out`, `d_attended`, `attended` and `d_projected`) count: a program that leaves them out, or rounds other values in their place, can miss the bound.
Values may be sent and summed in bfloat16 or wider, within the bound.
A program may use at most 192 MiB of HBM per device.

```python
import math
import jax
import jax.numpy as jnp
import numpy as np
from jax import lax

D = 512
HD = 16
PATCH = 1024
P_DEV = 2048
V_DEV = 2048
POINTS = 65536
VOXELS = 65536
N_SEQ = 32
N_MP = 4


def block_permutation(subkey):
    return jax.random.permutation(subkey, P_DEV)


def draw_send_order(key, part):
    subkeys = jax.random.split(jax.random.fold_in(key, 11), POINTS // P_DEV)
    return jax.vmap(block_permutation)(subkeys).reshape(-1).astype(jnp.int32)


def draw_arrive_order(key, part):
    subkeys = jax.random.split(jax.random.fold_in(key, 23), POINTS // P_DEV)
    return jax.vmap(block_permutation)(subkeys).reshape(-1).astype(jnp.int32)


def draw_qkv_weight(key, part):
    base = jax.random.normal(jax.random.fold_in(key, 37), (D, 3, D), jnp.float32) * D ** (-0.5)
    return base.astype(jnp.bfloat16)


def with_ends(result, own_key, low, high):
    longest = result.shape.index(max(result.shape))
    spots = []
    for shift in (0, 1):
        where = [jax.random.randint(jax.random.fold_in(own_key, axis), (), 0, length) for axis, length in enumerate(result.shape)]
        where[longest] = (where[longest] + shift) % result.shape[longest]
        spots.append(tuple(where))
    return result.at[spots[0]].set(low).at[spots[1]].set(high)


def levels(stream_key, dims, pieces, low, high):
    def one(position, shards_of):
        draws = jax.random.uniform(jax.random.fold_in(jax.random.fold_in(stream_key, 6), position), (shards_of,), jnp.float32, low / len(pieces), high / len(pieces))
        return jnp.repeat(jnp.exp(draws), dims[position] // shards_of).reshape((-1,) + (1,) * (len(dims) - position - 1))

    factor_of = one(*pieces[0])
    for cut in pieces[1:]:
        factor_of = factor_of * one(*cut)
    return factor_of


def assign_block(rng, own, number, rows, count, top, most, skew):
    order = jax.random.permutation(rng, count)
    heavy_load, usual = portions_of(count, rows * top, most, skew, True), portions_of(count, rows * top, most, skew, False)
    places = jnp.arange(count)

    def named(lengths, turn):
        used = int((lengths > 0).sum())
        fixed = max(1, used // 4)
        moved = fixed + (places - fixed + turn * (used - fixed)) % max(1, count - fixed)
        return jnp.zeros((count,), jnp.int32).at[order[jnp.where(places < fixed, places, moved)]].set(jnp.asarray(lengths, jnp.int32))

    lengths = jnp.where(number % 4 == 0, named(heavy_load, number // 4), named(usual, number - number // 4 - 1))
    mixed = jax.random.permutation(jax.random.fold_in(own, 3), count)
    source_of, receiver = mixed[0:count // 2 * 2:2], mixed[1:count // 2 * 2:2]
    room = jnp.minimum(lengths[source_of] - 1, most - lengths[receiver]) // 2
    room = jnp.where((source_of == order[0]) | (receiver == order[0]) | (lengths[receiver] == 0), 0, jnp.maximum(room, 0))
    moved = jax.random.randint(jax.random.fold_in(own, 4), (count // 2,), 0, 1 << 20) % (room + 1)
    lengths = lengths.at[source_of].add(-moved).at[receiver].add(moved)
    items = jnp.searchsorted(jnp.cumsum(lengths), jnp.arange(rows * top), side="right").astype(jnp.int32)
    table = items.reshape(top, rows).T
    table = table[jax.random.permutation(jax.random.fold_in(own, 1), rows)]
    turn = jax.random.randint(jax.random.fold_in(own, 2), (rows, 1), 0, top)
    return jnp.take_along_axis(table, (jnp.arange(top)[None, :] + turn) % top, axis=1)


def portions_of(amount, total, reach, slope, full):
    loads = [(1 << 20) // math.isqrt(rank ** slope) + 1 for rank in range(1, amount + 1)]
    largest = reach if full else min(reach, max(-(-total // amount), total * loads[0] // sum(loads)))
    least = 1 if total - largest >= amount - 1 else 0
    given, spare = [largest] + [least] * (amount - 1), total - largest - least * (amount - 1)
    while spare > 0:
        free = [i for i in range(1, amount) if given[i] < largest] or [i for i in range(1, amount) if given[i] < reach]
        pool, budget = sum([loads[i] for i in free]), spare
        for i in free:
            extra = min(reach - given[i], max(1, budget * loads[i] // pool), spare)
            given[i] = given[i] + extra
            spare = spare - extra
    return np.array(given)


def normal_values(rng, dims, width, most, cuts=(), dtype=jnp.bfloat16):
    entries = width * jax.random.normal(rng, dims, jnp.float32)
    if cuts:
        entries = entries * levels(rng, dims, cuts, -0.22, 0.18)
    return jnp.clip(entries, -most, most).astype(dtype)


def setup_inputs(seed: int = 0) -> dict:
    arg_keys = jax.random.split(jax.random.key(seed), 9)
    scan_points = normal_values(arg_keys[0], (POINTS, D), 1.0, 6.0, ((0, 32),))
    send_order = draw_send_order(jax.random.fold_in(arg_keys[8], 71), 0)
    arrive_order = draw_arrive_order(jax.random.fold_in(arg_keys[8], 71), 0)
    qkv_weight = draw_qkv_weight(jax.random.fold_in(arg_keys[8], 71), 0)
    out_weight = normal_values(arg_keys[4], (D, D), D ** -0.5, 0.25, ((1, 4),))
    voxel_grads = normal_values(arg_keys[5], (VOXELS, D), 1.0, 6.0, ((0, 32),))
    voxel_shard_keys = jax.random.split(jax.random.fold_in(arg_keys[6], 1), VOXELS // V_DEV)
    voxel_shard_turns = jax.random.permutation(jax.random.fold_in(arg_keys[6], 3), VOXELS // V_DEV)
    voxel_shard = jax.vmap(lambda own, number: assign_block(jax.random.fold_in(arg_keys[6], 2), own, number, V_DEV, N_SEQ, 1, 2 * V_DEV // N_SEQ, 2))(voxel_shard_keys, voxel_shard_turns).reshape((VOXELS, 1))
    voxel_point = with_ends(jax.random.randint(arg_keys[7], (VOXELS,), 0, P_DEV), jax.random.fold_in(arg_keys[7], 1), 0, P_DEV - 1).astype(jnp.int32)
    return {"scan_points": scan_points, "send_order": send_order, "arrive_order": arrive_order, "qkv_weight": qkv_weight, "out_weight": out_weight, "voxel_grads": voxel_grads, "voxel_shard": voxel_shard, "voxel_point": voxel_point}


score_scale = 0.25
epsilon = 1e-05

def patch_pass(queries, key_rows, values, d_attended):
    row_count = queries.shape[0]
    head_count = queries.shape[1] // HD
    query_heads = queries.reshape(row_count, head_count, HD).astype(jnp.float32)
    key_heads = key_rows.reshape(row_count, head_count, HD).astype(jnp.float32)
    value_heads = values.reshape(row_count, head_count, HD).astype(jnp.float32)
    scores = jnp.einsum('qhc,khc->hqk', query_heads, key_heads) * score_scale
    row_max = lax.optimization_barrier(jnp.max(scores, axis=2, keepdims=True))
    weights_exp = jnp.exp(scores - row_max)
    probabilities = weights_exp / lax.optimization_barrier(jnp.sum(weights_exp, axis=2, keepdims=True))
    prob_rounded = probabilities.astype(jnp.bfloat16).astype(jnp.float32)
    attended = jnp.einsum('hqk,khc->qhc', prob_rounded, value_heads).astype(jnp.bfloat16)
    grad_heads = d_attended.reshape(row_count, head_count, HD).astype(jnp.float32)
    d_probabilities = jnp.einsum('qhc,khc->hqk', grad_heads, value_heads)
    d_values = jnp.einsum('hqk,qhc->khc', prob_rounded, grad_heads).astype(jnp.bfloat16)
    row_delta = lax.optimization_barrier(jnp.sum(grad_heads * attended.astype(jnp.float32), axis=2))
    d_scores = (probabilities * (d_probabilities - row_delta.T[:, :, None]) * score_scale).astype(jnp.bfloat16).astype(jnp.float32)
    d_query = jnp.einsum('hqk,khc->qhc', d_scores, key_heads).astype(jnp.bfloat16)
    d_keys = jnp.einsum('hqk,qhc->khc', d_scores, query_heads).astype(jnp.bfloat16)
    stacked = jnp.stack([d_query, d_keys, d_values], axis=1).reshape(row_count, 3, head_count * HD)
    return (attended.reshape(row_count, head_count * HD), stacked)

def take_rows(block, order):
    return block[order]

def reference(scan_points, send_order, arrive_order, qkv_weight, out_weight, voxel_grads, voxel_shard, voxel_point):
    shards = N_SEQ
    bucket = P_DEV // shards
    total = P_DEV * shards
    blocks = scan_points.reshape(shards, P_DEV, D)
    picked = jax.vmap(take_rows)(blocks, send_order.reshape(shards, P_DEV).astype(jnp.int32))
    picked = picked.reshape(shards, shards, bucket, D).transpose(1, 0, 2, 3).reshape(shards, P_DEV, D)
    points = jax.vmap(take_rows)(picked, arrive_order.reshape(shards, P_DEV).astype(jnp.int32)).reshape(total, D)
    point_float = points.astype(jnp.float32)
    row_mean = lax.optimization_barrier(jnp.mean(point_float, axis=1, keepdims=True))
    centered = point_float - row_mean
    row_var = lax.optimization_barrier(jnp.mean(centered * centered, axis=1, keepdims=True))
    inv_scale = lax.rsqrt(row_var + epsilon)
    normed = centered * inv_scale
    hidden = normed.astype(jnp.bfloat16)
    projected = jnp.einsum('pd,dtc->ptc', hidden.astype(jnp.float32), qkv_weight.astype(jnp.float32)).astype(jnp.bfloat16)
    global_row = (voxel_shard[:, 0] * P_DEV + voxel_point).astype(jnp.int32)
    d_sum = jax.ops.segment_sum(voxel_grads.astype(jnp.float32), global_row, num_segments=total)
    d_out = d_sum.astype(jnp.bfloat16)
    d_attended = jnp.dot(d_out, out_weight, preferred_element_type=jnp.float32).astype(jnp.bfloat16)
    patches = total // PATCH

    def one_patch(operands):
        proj_patch, grad_patch = operands
        return patch_pass(proj_patch[:, 0], proj_patch[:, 1], proj_patch[:, 2], grad_patch)
    attended, d_projected = lax.map(one_patch, (projected.reshape(patches, PATCH, 3, D), d_attended.reshape(patches, PATCH, D)))
    attended = attended.reshape(total, D)
    d_projected = d_projected.reshape(total, 3, D)
    grad_qkv = jnp.einsum('pd,ptc->dtc', hidden.astype(jnp.float32), d_projected.astype(jnp.float32))
    grad_out = jnp.dot(d_out.T, attended, preferred_element_type=jnp.float32)
    group_cols = D // N_MP
    d_hidden = jnp.zeros((total, D), jnp.float32)
    for member in range(N_MP):
        partial_value = jnp.einsum('ptc,dtc->pd', d_projected[:, :, member * group_cols:(member + 1) * group_cols].astype(jnp.float32), qkv_weight[:, :, member * group_cols:(member + 1) * group_cols].astype(jnp.float32))
        partial_value = lax.optimization_barrier(partial_value.astype(jnp.bfloat16)).astype(jnp.float32)
        d_hidden = d_hidden + partial_value
    mean_grad = lax.optimization_barrier(jnp.mean(d_hidden, axis=1, keepdims=True))
    mean_cross = lax.optimization_barrier(jnp.mean(d_hidden * normed, axis=1, keepdims=True))
    d_points = d_out.astype(jnp.float32) + inv_scale * (d_hidden - mean_grad - normed * mean_cross)
    return (d_points, grad_qkv, grad_out)
```

```python
import jax
import jax.numpy as jnp
from jax import lax
from jax.experimental import pallas as pl
from jax.experimental.pallas import tpu as pltpu
from jax.sharding import PartitionSpec as P

HD = 16
PATCH = 1024
LANES = 128
BLK = 256
QB = 256
EPSILON = 1e-05
LOG2E = 1.4426950408889634
BF = jnp.bfloat16
F32 = jnp.float32
MESH = pl.DeviceIdType.MESH


def dotf(a, b):
    return jnp.dot(a, b, preferred_element_type=F32)


def dot_nt(a, b):
    return lax.dot_general(a, b, (((1,), (1,)), ((), ())), preferred_element_type=F32)


def iota(shape, axis):
    return lax.broadcasted_iota(jnp.int32, shape, axis)


def as_mask(cond):
    return jnp.where(cond, 1.0, 0.0).astype(BF)


def lane_copy(row):
    return jnp.broadcast_to(row.astype(F32), (LANES, BLK)).T


def select_rows(order_row, count):
    want = lane_copy(order_row).astype(jnp.int32)
    lane = iota((BLK, LANES), 1)
    return jnp.concatenate([as_mask(want == lane + c * LANES) for c in range(count // LANES)], axis=1)


def exchange_kernel(
    scan, voxels, send_order, arrive_order, shard, point,
    pts, dout,
    x, v, sendp, sendv, sendi, gotp, gotv, goti, place,
    in_sem, send_sem, recv_sem, ring_send, ring_recv,
):
    seq, mp = lax.axis_index("seq"), lax.axis_index("mp")
    n, m = lax.axis_size("seq"), lax.axis_size("mp")
    rows = x.shape[0]
    grp = rows // n
    cap = gotv.shape[0] // n
    blocks = rows // BLK
    right, left = lax.rem(mp + 1, m), lax.rem(mp + m - 1, m)
    mine = pl.ds(pl.multiple_of(mp * LANES, LANES), LANES)
    in_x = pltpu.make_async_copy(scan.at[:, mine], x, in_sem.at[0])
    in_v = pltpu.make_async_copy(voxels.at[:, mine], v, in_sem.at[1])
    in_x.start()
    in_v.start()
    barrier = pltpu.get_barrier_semaphore()
    for k in range(1, n):
        pl.semaphore_signal(barrier, inc=1, device_id={"seq": lax.rem(seq + k, n)}, device_id_type=MESH)
    pl.semaphore_signal(barrier, inc=1, device_id={"mp": right}, device_id_type=MESH)
    pl.semaphore_signal(barrier, inc=1, device_id={"mp": left}, device_id_type=MESH)

    tri = as_mask(iota((BLK, BLK), 0) < iota((BLK, BLK), 1))
    carry = jnp.zeros((n, 1), F32)
    codes = jnp.zeros((3 * n, cap), F32)
    for b in range(blocks):
        target = shard[b : b + 1, :]
        hot = jnp.where(iota((n, BLK), 0) == target, 1.0, 0.0)
        before = dotf(hot.astype(BF), tri) + carry
        rank = jnp.sum(before * hot, axis=0, keepdims=True)
        carry = carry + jnp.sum(hot, axis=1, keepdims=True)
        place[b : b + 1, :] = target * cap + rank.astype(jnp.int32)
        where_to = point[b : b + 1, :]
        high = (where_to // 64).astype(F32)
        low = (where_to % 64).astype(F32)
        slot = as_mask(iota((cap, BLK), 0) == rank.astype(jnp.int32))
        coded = jnp.concatenate([hot * high, hot * low, hot], axis=0).astype(BF)
        codes = codes + dot_nt(coded, slot)
    sub = iota((16, cap), 0)
    for t in range(n):
        sendi[t] = jnp.where(
            sub == 0, codes[t : t + 1], jnp.where(sub == 1, codes[n + t : n + t + 1], codes[2 * n + t : 2 * n + t + 1])
        ).astype(BF)

    pl.semaphore_wait(barrier, n + 1)

    def send(src, dst, kind, peer):
        return pltpu.make_async_remote_copy(
            src_ref=src, dst_ref=dst, send_sem=send_sem.at[kind], recv_sem=recv_sem.at[kind],
            device_id={"seq": peer}, device_id_type=MESH,
        )

    def rows_of(block, size):
        return pl.ds(pl.multiple_of(block * size, size), size)

    in_x.wait()
    per = BLK // grp

    def points_out(i, _):
        b = lax.rem(i + seq // per, blocks)
        hot = select_rows(send_order[pl.ds(b, 1), :], rows)
        sendp[rows_of(b, BLK), :] = dotf(hot, x[...]).astype(BF)
        for u in range(per):
            peer = b * per + u

            @pl.when(peer != seq)
            def _():
                send(sendp.at[rows_of(peer, grp)], gotp.at[rows_of(seq, grp)], 0, peer).start()

        return 0

    lax.fori_loop(0, blocks, points_out, 0)
    gotp[rows_of(seq, grp), :] = sendp[rows_of(seq, grp), :]
    in_v.wait()
    per_v = BLK // cap
    vblocks = n // per_v

    def voxels_out(i, _):
        b = lax.rem(i + seq // per_v, vblocks)
        slot = iota((BLK, BLK), 0) + b * BLK
        hot = jnp.concatenate([as_mask(slot == place[c : c + 1, :]) for c in range(blocks)], axis=1)
        sendv[rows_of(b, BLK), :] = dotf(hot, v[...]).astype(BF)
        for u in range(per_v):
            peer = b * per_v + u

            @pl.when(peer != seq)
            def _():
                send(sendv.at[rows_of(peer, cap)], gotv.at[rows_of(seq, cap)], 1, peer).start()
                send(sendi.at[peer], goti.at[seq], 2, peer).start()

        return 0

    lax.fori_loop(0, vblocks, voxels_out, 0)
    gotv[rows_of(seq, cap), :] = sendv[rows_of(seq, cap), :]
    goti[seq] = sendi[seq]

    def ring(full, kind, owner, b, to):
        at = full.at[owner, rows_of(b, BLK)]
        return pltpu.make_async_remote_copy(
            src_ref=at, dst_ref=at, send_sem=ring_send.at[kind], recv_sem=ring_recv.at[kind, owner, b],
            device_id={"mp": to}, device_id_type=MESH,
        )

    half = blocks // 2

    def relay(full, kind, b):
        @pl.when(b < half)
        def _():
            ring(full, kind, left, b, right).wait_recv()
            ring(full, kind, left, b, right).start()

        @pl.when(b >= half)
        def _():
            ring(full, kind, right, b, left).wait_recv()
            ring(full, kind, right, b, left).start()

    def wait_all(kind, ref, part):
        other = ref.at[pl.ds(0, part)]
        send(other, other, kind, seq).wait_recv()
        send(other, other, kind, seq).wait_send()

    wait_all(0, gotp, (n - 1) * grp)

    def points_in(b, _):
        hot = select_rows(arrive_order[pl.ds(b, 1), :], rows)
        pts[mp, rows_of(b, BLK), :] = dotf(hot, gotp[...]).astype(BF)
        ring(pts, 0, mp, b, right).start()
        ring(pts, 0, mp, b, left).start()
        return 0

    lax.fori_loop(0, blocks, points_in, 0)
    wait_all(1, gotv, (n - 1) * cap)
    wait_all(2, goti, n - 1)

    def voxels_in(b, _):
        pos = iota((BLK, cap), 0) + b * BLK
        tiles = []
        for s in range(n):
            code = goti[s].astype(F32)
            at = jnp.where(code[2:3, :] > 0.5, code[0:1, :] * 64.0 + code[1:2, :], -1.0).astype(jnp.int32)
            tiles.append(as_mask(pos == at))
        dout[mp, rows_of(b, BLK), :] = dotf(jnp.concatenate(tiles, axis=1), gotv[...]).astype(BF)
        ring(dout, 1, mp, b, right).start()
        ring(dout, 1, mp, b, left).start()
        relay(pts, 0, b)
        return 0

    lax.fori_loop(0, blocks, voxels_in, 0)

    def late(b, _):
        relay(dout, 1, b)
        return 0

    lax.fori_loop(0, blocks, late, 0)
    opposite = lax.rem(mp + 2, m)
    for kind, full in ((0, pts), (1, dout)):
        for b in range(blocks):
            ring(full, kind, left if b >= half else right, b, right).wait_recv()
            ring(full, kind, opposite, b, right).wait_recv()
        for _ in range(2):
            ring_all = full.at[0]
            pltpu.make_async_remote_copy(
                src_ref=ring_all, dst_ref=ring_all, send_sem=ring_send.at[kind], recv_sem=ring_recv.at[kind, 0, 0],
                device_id={"mp": right}, device_id_type=MESH,
            ).wait_send()
        ring_half = full.at[0]
        pltpu.make_async_remote_copy(
            src_ref=ring_half, dst_ref=ring_half, send_sem=ring_send.at[kind], recv_sem=ring_recv.at[kind, 0, 0],
            device_id={"mp": right}, device_id_type=MESH,
        ).wait_send()


def exchange(scan, voxels, send_order, arrive_order, shard, point, n, m):
    rows = scan.shape[0]
    grp, cap = rows // n, 2 * voxels.shape[0] // n
    blocks = rows // BLK
    vmem, hbm = pl.BlockSpec(memory_space=pltpu.VMEM), pl.BlockSpec(memory_space=pl.ANY)
    dma = pltpu.SemaphoreType.DMA
    return pl.pallas_call(
        exchange_kernel,
        out_shape=[jax.ShapeDtypeStruct((m, rows, LANES), BF)] * 2,
        in_specs=[hbm, hbm, vmem, vmem, vmem, vmem],
        out_specs=[vmem, vmem],
        scratch_shapes=[
            pltpu.VMEM((rows, LANES), BF),
            pltpu.VMEM((rows, LANES), BF),
            pltpu.VMEM((rows, LANES), BF),
            pltpu.VMEM((n * cap, LANES), BF),
            pltpu.VMEM((n, 16, cap), BF),
            pltpu.VMEM((rows, LANES), BF),
            pltpu.VMEM((n * cap, LANES), BF),
            pltpu.VMEM((n, 16, cap), BF),
            pltpu.VMEM((blocks, BLK), jnp.int32),
            dma((2,)),
            dma((3,)),
            dma((3,)),
            dma((2,)),
            dma((2, m, blocks)),
        ],
        compiler_params=pltpu.CompilerParams(
            collective_id=0, has_side_effects=True, vmem_limit_bytes=48 * 1024 * 1024
        ),
        name="exchange",
    )(
        scan, voxels, send_order.reshape(blocks, BLK), arrive_order.reshape(blocks, BLK),
        shard.reshape(blocks, BLK), point.reshape(blocks, BLK),
    )


def lanes_of(ref, r):
    return jnp.concatenate([ref[j, r, :] for j in range(ref.shape[0])], axis=1)


def core_kernel(
    points, dout, wq, wk, wv, wo, part, grads, stats, normq, invb,
    hid, kk, vv, qhl, qn, kt, vt, dat, dpt, qm, s_ref, e_ref, ds_ref, dan, dvk,
):
    m, rows, _ = points.shape
    npatch = rows // PATCH
    wcat = jnp.concatenate([wq[...], wk[...], wv[...]], axis=1)
    ones_lane = as_mask(iota((BLK, LANES), 1) < 3)
    for p in range(npatch):
        for b in range(PATCH // BLK):
            r = pl.ds(p * PATCH + b * BLK, BLK)
            c = pl.ds(b * BLK, BLK)
            x = lanes_of(points, r).astype(F32)
            x = x - jnp.mean(x, axis=1, keepdims=True)
            inv = lax.rsqrt(jnp.mean(x * x, axis=1, keepdims=True) + EPSILON)
            normed = x * inv
            hidden = normed.astype(BF)
            hid[r, :] = hidden
            invb[r, :] = jnp.broadcast_to(inv, (BLK, LANES))
            mp = lax.axis_index("mp")
            own = normed[:, 0:LANES]
            for j in range(1, m):
                own = jnp.where(mp == j, normed[:, j * LANES : (j + 1) * LANES], own)
            normq[r, :] = own
            proj = dotf(hidden, wcat)
            q, k, v = (proj[:, t * LANES : (t + 1) * LANES].astype(BF) for t in range(3))
            qn[r, :] = q
            kk[r, 0:LANES] = k
            kk[r, LANES : 2 * LANES] = k
            vv[r, 0:LANES] = v
            vv[r, LANES : 2 * LANES] = ones_lane
            qs = (q.astype(F32) * (0.25 * LOG2E)).T
            high = qs.astype(BF)
            qhl[p, 0:LANES, c] = high
            qhl[p, LANES : 2 * LANES, c] = (qs - high.astype(F32)).astype(BF)
            kt[p, :, c] = k.astype(F32).T.astype(BF)
            vt[p, :, c] = v.astype(F32).T.astype(BF)
            dat[p, :, c] = dotf(lanes_of(dout, r), wo[...]).astype(BF).astype(F32).T.astype(BF)

    def patch_body(p, _):
        prow = pl.ds(pl.multiple_of(p * PATCH, PATCH), PATCH)
        dvk[...] = jnp.zeros_like(dvk)

        def head_body(h, _):
            hrow = pl.ds(pl.multiple_of(h * HD, HD), HD)
            rmask = (iota((LANES, PATCH), 0) // HD) == h
            zero = jnp.zeros((LANES, PATCH), BF)
            qm[0:LANES, :] = jnp.where(rmask, qhl[p, 0:LANES, :], zero)
            qm[LANES : 2 * LANES, :] = jnp.where(rmask, qhl[p, LANES : 2 * LANES, :], zero)
            lmask = (iota((PATCH, LANES), 1) // HD) == h
            k2 = kk[prow, :]
            v2 = vv[prow, :]
            vt1 = jnp.concatenate([vt[p, hrow, :], jnp.ones((HD, PATCH), BF)], axis=0)
            kth = kt[p, hrow, :]
            for b in range(PATCH // QB):
                c = pl.ds(b * QB, QB)
                s_ref[b % 2] = dotf(k2, qm[:, c])
                top = jnp.max(s_ref[b % 2], axis=0, keepdims=True)
                e = jnp.exp2(s_ref[b % 2] - top).astype(BF)
                e_ref[:, c] = e
                av = dotf(vt1, e)
                inv = 1.0 / av[HD : HD + 1, :]
                att = (av[0:HD, :] * inv).astype(BF)
                dpt[p, pl.ds(pl.multiple_of(3 * LANES + h * HD, HD), HD), c] = att
                da = (dat[p, hrow, c].astype(F32) * inv).astype(BF).astype(F32)
                delta = jnp.sum(da * att.astype(F32), axis=0, keepdims=True)
                d1 = delta.astype(BF).astype(F32)
                d2 = (delta - d1).astype(BF).astype(F32)
                d3 = delta - d1 - d2
                sub = iota((LANES, QB), 0)
                tile = jnp.where(sub // HD == h, jnp.concatenate([da] * (LANES // HD), axis=0), 0.0)
                tail = jnp.where(sub == 0, -d1, jnp.where(sub == 1, -d2, jnp.where(sub == 2, -d3, 0.0)))
                dan[c, :] = tile.T.astype(BF)
                dp = dotf(v2, jnp.concatenate([tile, tail], axis=0).astype(BF))
                ds = (e_ref[:, c].astype(F32) * dp).astype(BF)
                ds_ref[:, c] = ds
                dpt[p, hrow, c] = (dotf(kth, ds) * 0.25).astype(BF)
            dvk[:, 0:LANES] += dotf(ds_ref[...], jnp.where(lmask, qn[prow, :], jnp.zeros((PATCH, LANES), BF)))
            dvk[:, LANES : 2 * LANES] += dotf(e_ref[...], dan[...])
            return 0

        lax.fori_loop(0, LANES // HD, head_body, 0)
        dk = (dvk[:, 0:LANES] * 0.25).astype(BF)
        dv = dvk[:, LANES : 2 * LANES].astype(BF)
        dpt[p, LANES : 2 * LANES, :] = dk.astype(F32).T.astype(BF)
        dpt[p, 2 * LANES : 3 * LANES, :] = dv.astype(F32).T.astype(BF)
        dq = dpt[p, 0:LANES, :].astype(F32).T.astype(BF)
        dproj = jnp.concatenate([dq, dk, dv], axis=1)
        for b in range(PATCH // BLK):
            r = pl.ds(pl.multiple_of(p * PATCH + b * BLK, BLK), BLK)
            pd = dot_nt(dproj[b * BLK : (b + 1) * BLK], wcat).astype(BF)
            for j in range(m):
                part[j, r, :] = pd[:, j * LANES : (j + 1) * LANES]
            x = lanes_of(points, r).astype(F32)
            normed = (x - jnp.mean(x, axis=1, keepdims=True)) * invb[r, 0:1]
            z = pd.astype(F32) * normed
            zh = z.astype(BF)
            zl = (z - zh.astype(F32)).astype(BF)
            on = jnp.ones((8, pd.shape[1]), BF)
            total = dot_nt(on, pd)
            cross = dot_nt(on, zh) + dot_nt(on, zl)
            stats[p, :, b * BLK : (b + 1) * BLK] = jnp.where(iota((8, BLK), 0) == 0, total, cross)
        return 0

    lax.fori_loop(0, npatch, patch_body, 0)
    upper, lower = 0.0, 0.0
    for p in range(npatch):
        r = pl.ds(p * PATCH, PATCH)
        upper = upper + dotf(dpt[p, 0 : 3 * LANES, :], hid[r, :])
        lower = lower + dotf(dpt[p, 3 * LANES : 4 * LANES, :], lanes_of(dout, r))
    grads[:, 0 : 3 * LANES] = upper.T.astype(BF)
    grads[:, 3 * LANES : 4 * LANES] = lower.T.astype(BF)


def core(points, dout, wq, wk, wv, wo):
    m, rows, _ = points.shape
    npatch = rows // PATCH
    feats = m * LANES
    vmem = pl.BlockSpec(memory_space=pltpu.VMEM)
    return pl.pallas_call(
        core_kernel,
        out_shape=[
            jax.ShapeDtypeStruct((m, rows, LANES), BF),
            jax.ShapeDtypeStruct((feats, 4 * LANES), BF),
            jax.ShapeDtypeStruct((npatch, 8, PATCH), F32),
            jax.ShapeDtypeStruct((rows, LANES), F32),
            jax.ShapeDtypeStruct((rows, LANES), F32),
        ],
        in_specs=[vmem] * 6,
        out_specs=[vmem] * 5,
        scratch_shapes=[
            pltpu.VMEM((rows, feats), BF),
            pltpu.VMEM((rows, 2 * LANES), BF),
            pltpu.VMEM((rows, 2 * LANES), BF),
            pltpu.VMEM((npatch, 2 * LANES, PATCH), BF),
            pltpu.VMEM((rows, LANES), BF),
            pltpu.VMEM((npatch, LANES, PATCH), BF),
            pltpu.VMEM((npatch, LANES, PATCH), BF),
            pltpu.VMEM((npatch, LANES, PATCH), BF),
            pltpu.VMEM((npatch, 4 * LANES, PATCH), BF),
            pltpu.VMEM((2 * LANES, PATCH), BF),
            pltpu.VMEM((2, PATCH, QB), F32),
            pltpu.VMEM((PATCH, PATCH), BF),
            pltpu.VMEM((PATCH, PATCH), BF),
            pltpu.VMEM((PATCH, LANES), BF),
            pltpu.VMEM((PATCH, 2 * LANES), F32),
        ],
        compiler_params=pltpu.CompilerParams(vmem_limit_bytes=60 * 1024 * 1024),
        name="core",
    )(points, dout, wq, wk, wv, wo)


def finish_kernel(
    part, grads, stats, normq, invb, dout,
    d_points, grad_qkv, grad_out,
    got_l, got_r, rel_l, rel_r, got_s, got_g,
    g_send, g_recv, s_send, s_recv, p_send, p_recv,
):
    seq, mp = lax.axis_index("seq"), lax.axis_index("mp")
    n, m = lax.axis_size("seq"), lax.axis_size("mp")
    rows = normq.shape[0]
    npatch = rows // PATCH
    right, left, opposite = lax.rem(mp + 1, m), lax.rem(mp + m - 1, m), lax.rem(mp + 2, m)
    barrier = pltpu.get_barrier_semaphore()
    for k in range(1, n):
        pl.semaphore_signal(barrier, inc=1, device_id={"seq": lax.rem(seq + k, n)}, device_id_type=MESH)
    for to in (right, left, opposite):
        pl.semaphore_signal(barrier, inc=1, device_id={"mp": to}, device_id_type=MESH)
    pl.semaphore_wait(barrier, n - 1 + m - 1)
    half = rows // 2
    low, high = pl.ds(0, half), pl.ds(half, half)

    def hop(src, dst, sem, to):
        return pltpu.make_async_remote_copy(
            src_ref=src, dst_ref=dst, send_sem=p_send.at[sem], recv_sem=p_recv.at[sem],
            device_id={"mp": to}, device_id_type=MESH,
        )

    first = [
        hop(part.at[opposite, low], rel_l, 0, right),
        hop(part.at[opposite, high], rel_r, 1, left),
        hop(part.at[right, high], got_l.at[high], 2, right),
        hop(part.at[left, low], got_r.at[low], 3, left),
    ]
    for c in first:
        c.start()

    def stat_copy(i, to):
        return pltpu.make_async_remote_copy(
            src_ref=stats, dst_ref=got_s.at[i], send_sem=s_send.at[i], recv_sem=s_recv.at[i],
            device_id={"mp": to}, device_id_type=MESH,
        )

    for i, to in enumerate((right, left, opposite)):
        stat_copy(i, to).start()
    band = grads.shape[0] // n

    def grad_copy(src, dst, peer):
        return pltpu.make_async_remote_copy(
            src_ref=src, dst_ref=dst, send_sem=g_send, recv_sem=g_recv,
            device_id={"seq": peer}, device_id_type=MESH,
        )

    def grads_out(k, _):
        peer = lax.rem(seq + k, n)
        at = pl.ds(pl.multiple_of(peer * band, band), band)
        grad_copy(grads.at[at], got_g.at[seq], peer).start()
        return 0

    lax.fori_loop(1, n, grads_out, 0)
    got_g[seq] = grads[pl.ds(pl.multiple_of(seq * band, band), band), :]
    first[0].wait_recv()
    first[0].wait_send()
    rel_l[...] = (rel_l[...].astype(F32) + part[right, low, :].astype(F32)).astype(BF)
    second_r = hop(rel_l, got_l.at[low], 4, right)
    second_r.start()
    first[1].wait_recv()
    first[1].wait_send()
    rel_r[...] = (rel_r[...].astype(F32) + part[left, high, :].astype(F32)).astype(BF)
    second_l = hop(rel_r, got_r.at[high], 5, left)
    second_l.start()
    others = got_g.at[pl.ds(0, n - 1)]
    grad_copy(others, others, seq).wait()
    total = jnp.zeros((band, grads.shape[1]), F32)
    for k in range(n):
        total = total + got_g[k].astype(F32)
    for t in range(3):
        grad_qkv[:, t, :] = total[:, t * LANES : (t + 1) * LANES]
    grad_out[...] = total[:, 3 * LANES : 4 * LANES]
    for i, to in enumerate((right, left, opposite)):
        stat_copy(i, to).wait()
    first[2].wait()
    first[3].wait()
    second_r.wait()
    second_l.wait()
    scale = 1.0 / (m * LANES)
    for p in range(npatch):
        st = (stats[p] + got_s[0, p] + got_s[1, p] + got_s[2, p]) * scale
        for b in range(PATCH // BLK):
            r = pl.ds(p * PATCH + b * BLK, BLK)
            mean_grad = lane_copy(st[0:1, b * BLK : (b + 1) * BLK])
            mean_cross = lane_copy(st[1:2, b * BLK : (b + 1) * BLK])
            d_hidden = part[mp, r, :].astype(F32) + got_l[r, :].astype(F32) + got_r[r, :].astype(F32)
            d_points[r, :] = dout[mp, r, :].astype(F32) + invb[r, :] * (
                d_hidden - mean_grad - normq[r, :] * mean_cross
            )


def finish(part, grads, stats, normq, invb, dout, n):
    m, rows, _ = part.shape
    npatch = rows // PATCH
    band = grads.shape[0] // n
    vmem = pl.BlockSpec(memory_space=pltpu.VMEM)
    dma = pltpu.SemaphoreType.DMA
    return pl.pallas_call(
        finish_kernel,
        out_shape=[
            jax.ShapeDtypeStruct((rows, LANES), F32),
            jax.ShapeDtypeStruct((band, 3, LANES), F32),
            jax.ShapeDtypeStruct((band, LANES), F32),
        ],
        in_specs=[vmem] * 6,
        out_specs=[vmem] * 3,
        scratch_shapes=[
            pltpu.VMEM((rows, LANES), BF),
            pltpu.VMEM((rows, LANES), BF),
            pltpu.VMEM((rows // 2, LANES), BF),
            pltpu.VMEM((rows // 2, LANES), BF),
            pltpu.VMEM((m - 1, npatch, 8, PATCH), F32),
            pltpu.VMEM((n, band, 4 * LANES), BF),
            dma(()),
            dma(()),
            dma((m - 1,)),
            dma((m - 1,)),
            dma((6,)),
            dma((6,)),
        ],
        compiler_params=pltpu.CompilerParams(
            collective_id=1, has_side_effects=True, vmem_limit_bytes=48 * 1024 * 1024
        ),
        name="finish",
    )(part, grads, stats, normq, invb, dout)


def local(
    scan_points, send_order, arrive_order, qkv_weight, out_weight, voxel_grads, voxel_shard, voxel_point
):
    n, m = lax.axis_size("seq"), lax.axis_size("mp")
    pts, dout = exchange(
        scan_points, voxel_grads, send_order, arrive_order, voxel_shard, voxel_point, n, m
    )
    part, grads, stats, normq, invb = core(
        pts, dout, qkv_weight[:, 0], qkv_weight[:, 1], qkv_weight[:, 2], out_weight
    )
    return tuple(finish(part, grads, stats, normq, invb, dout, n))


def solution(mesh):
    in_specs = (
        P("seq", None), P("seq"), P("seq"), P(None, None, "mp"), P(None, "mp"),
        P("seq", None), P("seq", None), P("seq"),
    )
    out_specs = (P("seq", "mp"), P("seq", None, "mp"), P("seq", "mp"))
    return jax.shard_map(local, mesh=mesh, in_specs=in_specs, out_specs=out_specs, check_vma=False)
```

```python
import jax
import jax.numpy as jnp
from jax import lax
from jax.experimental import pallas as pl
from jax.experimental.pallas import tpu as pltpu
from jax.sharding import PartitionSpec as P

HD = 16
PATCH = 1024
LANES = 128
BLK = 256
HEADS = LANES // HD
PBLK = PATCH // BLK
QH = 512
EPSILON = 1e-05
LOG2E = 1.4426950408889634
BF = jnp.bfloat16
F32 = jnp.float32
MESH = pl.DeviceIdType.MESH


def dotf(a, b):
    return jnp.dot(a, b, preferred_element_type=F32)


def dot_nt(a, b):
    return lax.dot_general(a, b, (((1,), (1,)), ((), ())), preferred_element_type=F32)


def iota(shape, axis):
    return lax.broadcasted_iota(jnp.int32, shape, axis)


def as_mask(cond):
    return jnp.where(cond, 1.0, 0.0).astype(BF)


def lane_copy(row):
    return jnp.broadcast_to(row.astype(F32), (LANES, BLK)).T


def select_rows(order_row, count):
    want = lane_copy(order_row).astype(jnp.int32)
    lane = iota((BLK, LANES), 1)
    return jnp.concatenate([as_mask(want == lane + c * LANES) for c in range(count // LANES)], axis=1)


def lanes_of(ref, r):
    return jnp.concatenate([ref[j, r, :] for j in range(ref.shape[0])], axis=1)


def rows_of(block, size):
    return pl.ds(pl.multiple_of(block * size, size), size)


def remote(src, dst, send_sem, recv_sem, axis, to):
    return pltpu.make_async_remote_copy(
        src_ref=src, dst_ref=dst, send_sem=send_sem, recv_sem=recv_sem,
        device_id={axis: to}, device_id_type=MESH,
    )


def layer_kernel(
    scan, voxels, orders, wq, wk, wv, wo,
    d_points, grad_qkv, grad_out,
    x, v, sendp, sendv, sendi, gotp, gotv, goti, place,
    pts, dout, hid, kn, vn, qhl, qt, kt, vt, dat, dpt, qm0, qm1, s0, s1, e_all, ds0, ds1, top, linv,
    grads, stats, invb, rel_l, rel_r, got_s, got_g,
    in_sem, send_sem, recv_sem, ring_send, ring_recv, p_send, p_recv, s_send, s_recv, g_send, g_recv,
):
    seq, mp = lax.axis_index("seq"), lax.axis_index("mp")
    n, m = lax.axis_size("seq"), lax.axis_size("mp")
    rows = x.shape[0]
    npatch = rows // PATCH
    grp = rows // n
    cap = gotv.shape[0] // n
    blocks = rows // BLK
    right, left, opposite = lax.rem(mp + 1, m), lax.rem(mp + m - 1, m), lax.rem(mp + 2, m)
    part, got_l, got_r = pts, x, v
    send_order, arrive_order, shard, point = (orders.at[i] for i in range(4))

    mine = pl.ds(pl.multiple_of(mp * LANES, LANES), LANES)
    in_x = pltpu.make_async_copy(scan.at[:, mine], x, in_sem.at[0])
    in_v = pltpu.make_async_copy(voxels.at[:, mine], v, in_sem.at[1])
    in_x.start()
    in_v.start()
    barrier = pltpu.get_barrier_semaphore()
    for k in range(1, n):
        pl.semaphore_signal(barrier, inc=1, device_id={"seq": lax.rem(seq + k, n)}, device_id_type=MESH)
    for to in (right, left, opposite):
        pl.semaphore_signal(barrier, inc=1, device_id={"mp": to}, device_id_type=MESH)

    def send(src, dst, kind, peer):
        return remote(src, dst, send_sem.at[kind], recv_sem.at[kind], "seq", peer)

    in_x.wait()
    pl.semaphore_wait(barrier, n + m - 2)
    per = BLK // grp

    def points_out(i, _):
        b = lax.rem(i + seq // per, blocks)
        hot = select_rows(send_order[pl.ds(b, 1), :], rows)
        sendp[rows_of(b, BLK), :] = dotf(hot, x[...]).astype(BF)
        for u in range(per):
            peer = b * per + u

            @pl.when(peer != seq)
            def _():
                send(sendp.at[rows_of(peer, grp)], gotp.at[rows_of(seq, grp)], 0, peer).start()

        return 0

    lax.fori_loop(0, blocks, points_out, 0)
    gotp[rows_of(seq, grp), :] = sendp[rows_of(seq, grp), :]

    tri = as_mask(iota((BLK, BLK), 0) < iota((BLK, BLK), 1))
    carry = jnp.zeros((n, 1), F32)
    codes = jnp.zeros((3 * n, cap), F32)
    for b in range(blocks):
        target = shard[b : b + 1, :]
        hot = jnp.where(iota((n, BLK), 0) == target, 1.0, 0.0)
        before = dotf(hot.astype(BF), tri) + carry
        rank = jnp.sum(before * hot, axis=0, keepdims=True)
        carry = carry + jnp.sum(hot, axis=1, keepdims=True)
        place[b : b + 1, :] = target * cap + rank.astype(jnp.int32)
        where_to = point[b : b + 1, :]
        high = (where_to // 64).astype(F32)
        low = (where_to % 64).astype(F32)
        slot = as_mask(iota((cap, BLK), 0) == rank.astype(jnp.int32))
        coded = jnp.concatenate([hot * high, hot * low, hot], axis=0).astype(BF)
        codes = codes + dot_nt(coded, slot)
    sub16 = iota((16, cap), 0)
    for t in range(n):
        a, b, c = codes[t : t + 1], codes[n + t : n + t + 1], codes[2 * n + t : 2 * n + t + 1]
        sendi[t] = jnp.where(sub16 == 0, a, jnp.where(sub16 == 1, b, c)).astype(BF)
    in_v.wait()
    per_v = BLK // cap
    vblocks = n // per_v

    def voxels_out(i, _):
        b = lax.rem(i + seq // per_v, vblocks)
        slot = iota((BLK, BLK), 0) + b * BLK
        hot = jnp.concatenate([as_mask(slot == place[c : c + 1, :]) for c in range(blocks)], axis=1)
        sendv[rows_of(b, BLK), :] = dotf(hot, v[...]).astype(BF)
        for u in range(per_v):
            peer = b * per_v + u

            @pl.when(peer != seq)
            def _():
                send(sendv.at[rows_of(peer, cap)], gotv.at[rows_of(seq, cap)], 1, peer).start()
                send(sendi.at[peer], goti.at[seq], 2, peer).start()

        return 0

    def wait_all(kind, ref, size):
        other = ref.at[pl.ds(0, size)]
        send(other, other, kind, seq).wait_recv()
        send(other, other, kind, seq).wait_send()

    def ring(full, kind, owner, b, to):
        at = full.at[owner, rows_of(b, BLK)]
        return remote(at, at, ring_send.at[kind], ring_recv.at[kind, owner, b], "mp", to)

    def goes_right(b):
        return lax.rem(b, PBLK) < PBLK // 2

    def relay(full, kind, b):
        @pl.when(goes_right(b))
        def _():
            ring(full, kind, left, b, right).wait_recv()
            ring(full, kind, left, b, right).start()

        @pl.when(jnp.logical_not(goes_right(b)))
        def _():
            ring(full, kind, right, b, left).wait_recv()
            ring(full, kind, right, b, left).start()

    def arrived(full, kind, b):
        @pl.when(goes_right(b))
        def _():
            ring(full, kind, right, b, left).wait_recv()

        @pl.when(jnp.logical_not(goes_right(b)))
        def _():
            ring(full, kind, left, b, right).wait_recv()

        ring(full, kind, opposite, b, right).wait_recv()

    def ring_sent(full, kind):
        for _ in range(3):
            remote(full.at[0], full.at[0], ring_send.at[kind], ring_recv.at[kind, 0, 0], "mp", right).wait_send()

    wait_all(0, gotp, (n - 1) * grp)

    def points_in(b, _):
        hot = select_rows(arrive_order[pl.ds(b, 1), :], rows)
        pts[mp, rows_of(b, BLK), :] = dotf(hot, gotp[...]).astype(BF)
        ring(pts, 0, mp, b, right).start()
        ring(pts, 0, mp, b, left).start()
        return 0

    lax.fori_loop(0, blocks, points_in, 0)
    lax.fori_loop(0, vblocks, voxels_out, 0)
    gotv[rows_of(seq, cap), :] = sendv[rows_of(seq, cap), :]
    goti[seq] = sendi[seq]

    def points_on(b, _):
        relay(pts, 0, b)
        return 0

    lax.fori_loop(0, blocks, points_on, 0)
    wait_all(1, gotv, (n - 1) * cap)
    wait_all(2, goti, n - 1)

    def voxels_in(b, _):
        pos = iota((BLK, cap), 0) + b * BLK
        tiles = []
        for t in range(n):
            code = goti[t].astype(F32)
            at = jnp.where(code[2:3, :] > 0.5, code[0:1, :] * 64.0 + code[1:2, :], -1.0).astype(jnp.int32)
            tiles.append(as_mask(pos == at))
        dout[mp, rows_of(b, BLK), :] = dotf(jnp.concatenate(tiles, axis=1), gotv[...]).astype(BF)
        ring(dout, 1, mp, b, right).start()
        ring(dout, 1, mp, b, left).start()
        return 0

    lax.fori_loop(0, blocks, voxels_in, 0)

    wcat = jnp.concatenate([wq[...], wk[...], wv[...]], axis=1)
    ones_lane = as_mask(iota((PATCH, LANES), 1) < 3)
    halves = ((qm0, s0, ds0), (qm1, s1, ds1))

    def normalise(p):
        for b in range(PBLK):
            r = rows_of(p * PBLK + b, BLK)
            c = pl.ds(b * BLK, BLK)
            xb = lanes_of(pts, r).astype(F32)
            xb = xb - jnp.mean(xb, axis=1, keepdims=True)
            inv = lax.rsqrt(jnp.mean(xb * xb, axis=1, keepdims=True) + EPSILON)
            normed = xb * inv
            hidden = normed.astype(BF)
            hid[r, :] = hidden
            invb[r, :] = jnp.broadcast_to(inv, (BLK, LANES))
            own = normed[:, 0:LANES]
            for j in range(1, m):
                own = jnp.where(mp == j, normed[:, j * LANES : (j + 1) * LANES], own)
            d_points[r, :] = own
            proj = dotf(hidden, wcat)
            q, k, val = (proj[:, t * LANES : (t + 1) * LANES].astype(BF) for t in range(3))
            kn[r, :] = k
            vn[r, :] = val
            qf = q.astype(F32).T
            qt[p, :, c] = qf.astype(BF)
            qs = qf * (0.25 * LOG2E)
            high = qs.astype(BF)
            qhl[p, 0:LANES, c] = high
            qhl[p, LANES : 2 * LANES, c] = (qs - high.astype(F32)).astype(BF)
            kt[p, :, c] = k.astype(F32).T.astype(BF)
            vt[p, :, c] = val.astype(F32).T.astype(BF)

    def head_rows(h, base=0):
        return pl.ds(pl.multiple_of(base * LANES + h * HD, HD), HD)

    def scores(p, h, half):
        qm, s = halves[half][:2]
        c = pl.ds(half * QH, QH)
        rmask = (iota((LANES, QH), 0) // HD) == h
        zero = jnp.zeros((LANES, QH), BF)
        qm[0:LANES, :] = jnp.where(rmask, qhl[p, 0:LANES, c], zero)
        qm[LANES : 2 * LANES, :] = jnp.where(rmask, qhl[p, LANES : 2 * LANES, c], zero)
        k = kn[rows_of(p, PATCH), :]
        val = dotf(jnp.concatenate([k, k], axis=1), qm[...])
        s[...] = val
        top[half] = jnp.max(val, axis=0, keepdims=True)

    def forward(p, h, half):
        s = halves[half][1]
        c = pl.ds(half * QH, QH)
        e = jnp.exp2(s[...] - top[half]).astype(BF)
        e_all[p * HEADS + h, :, c] = e
        vt1 = jnp.concatenate([vt[p, head_rows(h), :], jnp.ones((HD, PATCH), BF)], axis=0)
        av = dotf(vt1, e)
        inv = 1.0 / av[HD : HD + 1, :]
        linv[p * HEADS + h, :, c] = inv
        dpt[p, head_rows(h, 3), c] = (av[0:HD, :] * inv).astype(BF)

    def forward_patch(p, _):
        def ready(b, _):
            arrived(pts, 0, p * PBLK + b)
            return 0

        lax.fori_loop(0, PBLK, ready, 0)
        normalise(p)
        scores(p, 0, 0)

        def step(h, _):
            @pl.when(lax.rem(h, 2) == 0)
            def _():
                relay(dout, 1, p * PBLK + h // 2)

            scores(p, h, 1)
            forward(p, h, 0)
            scores(p, jnp.minimum(h + 1, HEADS - 1), 0)
            forward(p, h, 1)
            return 0

        lax.fori_loop(0, HEADS, step, 0)
        return 0

    lax.fori_loop(0, npatch, forward_patch, 0)

    def hop(p, sem, src, dst, to):
        return remote(src, dst, p_send.at[p, sem], p_recv.at[p, sem], "mp", to)

    def hops(p, *which):
        low, high = rows_of(2 * p, PATCH // 2), rows_of(2 * p + 1, PATCH // 2)
        ends = (
            (part.at[opposite, low], rel_l.at[p], right),
            (part.at[opposite, high], rel_r.at[p], left),
            (part.at[right, high], got_l.at[high], right),
            (part.at[left, low], got_r.at[low], left),
            (rel_l.at[p], got_l.at[low], right),
            (rel_r.at[p], got_r.at[high], left),
        )
        return [hop(p, w, *ends[w]) for w in which]

    def hand_on(p):
        low, high = rows_of(2 * p, PATCH // 2), rows_of(2 * p + 1, PATCH // 2)
        in_l, in_r, out_l, out_r = hops(p, 0, 1, 4, 5)
        in_l.wait()
        rel_l[p] = (rel_l[p].astype(F32) + part[right, low, :].astype(F32)).astype(BF)
        out_l.start()
        in_r.wait()
        rel_r[p] = (rel_r[p].astype(F32) + part[left, high, :].astype(F32)).astype(BF)
        out_r.start()

    def backward(p, h, half):
        ds_ref = halves[half][2]
        i = p * HEADS + h
        c = pl.ds(half * QH, QH)
        scaled = (dat[head_rows(h), c].astype(F32) * linv[i, :, c]).astype(BF)
        da = scaled.astype(F32)
        delta = jnp.sum(da * dpt[p, head_rows(h, 3), c].astype(F32), axis=0, keepdims=True)
        d1 = delta.astype(BF).astype(F32)
        d2 = (delta - d1).astype(BF).astype(F32)
        d3 = delta - d1 - d2
        sub = iota((LANES, QH), 0)
        tile = jnp.where(sub // HD == h, jnp.concatenate([da] * HEADS, axis=0), 0.0)
        tail = jnp.where(sub == 0, -d1, jnp.where(sub == 1, -d2, jnp.where(sub == 2, -d3, 0.0)))
        vv = jnp.concatenate([vn[rows_of(p, PATCH), :], ones_lane], axis=1)
        dp = dotf(vv, jnp.concatenate([tile, tail], axis=0).astype(BF))
        ds = e_all[i, :, c] * dp.astype(BF)
        ds_ref[...] = ds
        dpt[p, head_rows(h), c] = (dotf(kt[p, head_rows(h), :], ds) * 0.25).astype(BF)
        return dot_nt(qt[p, head_rows(h), c], ds_ref[...]), dot_nt(scaled, e_all[i, :, c])

    def dout_in(b, _):
        arrived(dout, 1, b)
        return 0

    lax.fori_loop(0, blocks, dout_in, 0)
    ring_sent(pts, 0)
    ring_sent(dout, 1)

    def backward_patch(p, _):
        for b in range(PBLK):
            da = dotf(lanes_of(dout, rows_of(p * PBLK + b, BLK)), wo[...]).astype(BF)
            dat[:, b * BLK : (b + 1) * BLK] = da.astype(F32).T.astype(BF)

        def step(h, _):
            @pl.when(jnp.logical_and(p == 1, h == HEADS // 2))
            def _():
                hand_on(0)

            dk0, dv0 = backward(p, h, 0)
            dk1, dv1 = backward(p, h, 1)
            dpt[p, head_rows(h, 1), :] = ((dk0 + dk1) * 0.25).astype(BF)
            dpt[p, head_rows(h, 2), :] = (dv0 + dv1).astype(BF)
            return 0

        lax.fori_loop(0, HEADS, step, 0)
        for b in range(PBLK):
            r = rows_of(p * PBLK + b, BLK)
            dproj = dpt[p, 0 : 3 * LANES, pl.ds(b * BLK, BLK)].astype(F32).T.astype(BF)
            pd = dot_nt(dproj, wcat).astype(BF)
            xb = lanes_of(pts, r).astype(F32)
            normed = (xb - jnp.mean(xb, axis=1, keepdims=True)) * invb[r, 0:1]
            for j in range(m):
                part[j, r, :] = pd[:, j * LANES : (j + 1) * LANES]
            z = pd.astype(F32) * normed
            zh = z.astype(BF)
            zl = (z - zh.astype(F32)).astype(BF)
            on = jnp.ones((8, pd.shape[1]), BF)
            total = dot_nt(on, pd)
            cross = dot_nt(on, zh) + dot_nt(on, zl)
            stats[p, :, b * BLK : (b + 1) * BLK] = jnp.where(iota((8, BLK), 0) == 0, total, cross)
        for c in hops(p, 0, 1, 2, 3):
            c.start()
        return 0

    lax.fori_loop(0, npatch, backward_patch, 0)

    def stat_copy(i, to):
        return remote(stats, got_s.at[i], s_send.at[i], s_recv.at[i], "mp", to)

    for i, to in enumerate((right, left, opposite)):
        stat_copy(i, to).start()
    upper, lower = 0.0, 0.0
    for p in range(npatch):
        r = pl.ds(p * PATCH, PATCH)
        upper = upper + dotf(dpt[p, 0 : 3 * LANES, :], hid[r, :])
        lower = lower + dotf(dpt[p, 3 * LANES : 4 * LANES, :], lanes_of(dout, r))
    grads[:, 0 : 3 * LANES] = upper.T.astype(BF)
    grads[:, 3 * LANES : 4 * LANES] = lower.T.astype(BF)
    band = grads.shape[0] // n

    def grad_copy(src, dst, peer):
        return remote(src, dst, g_send, g_recv, "seq", peer)

    def grads_out(k, _):
        peer = lax.rem(seq + k, n)
        grad_copy(grads.at[rows_of(peer, band)], got_g.at[seq], peer).start()
        return 0

    lax.fori_loop(1, n, grads_out, 0)
    got_g[seq] = grads[rows_of(seq, band), :]
    hand_on(1)
    others = got_g.at[pl.ds(0, n - 1)]
    grad_copy(others, others, seq).wait()
    total = jnp.zeros((band, grads.shape[1]), F32)
    for k in range(n):
        total = total + got_g[k].astype(F32)
    for t in range(3):
        grad_qkv[:, t, :] = total[:, t * LANES : (t + 1) * LANES]
    grad_out[...] = total[:, 3 * LANES : 4 * LANES]
    for i, to in enumerate((right, left, opposite)):
        stat_copy(i, to).wait()
    scale = 1.0 / (m * LANES)
    for p in range(npatch):
        for c in hops(p, 2, 3, 4, 5):
            c.wait()
        st = (stats[p] + got_s[0, p] + got_s[1, p] + got_s[2, p]) * scale
        for b in range(PBLK):
            r = pl.ds(p * PATCH + b * BLK, BLK)
            mean_grad = lane_copy(st[0:1, b * BLK : (b + 1) * BLK])
            mean_cross = lane_copy(st[1:2, b * BLK : (b + 1) * BLK])
            d_hidden = part[mp, r, :].astype(F32) + got_l[r, :].astype(F32) + got_r[r, :].astype(F32)
            d_points[r, :] = dout[mp, r, :].astype(F32) + invb[r, :] * (
                d_hidden - mean_grad - d_points[r, :] * mean_cross
            )


def local(
    scan_points, send_order, arrive_order, qkv_weight, out_weight, voxel_grads, voxel_shard, voxel_point
):
    n, m = lax.axis_size("seq"), lax.axis_size("mp")
    rows = scan_points.shape[0]
    feats = m * LANES
    grp, cap = rows // n, 2 * voxel_grads.shape[0] // n
    blocks, npatch, band = rows // BLK, rows // PATCH, feats // n
    orders = jnp.stack([send_order, arrive_order, voxel_shard[:, 0], voxel_point]).reshape(4, blocks, BLK)
    vmem, hbm = pl.BlockSpec(memory_space=pltpu.VMEM), pl.BlockSpec(memory_space=pl.ANY)
    dma = pltpu.SemaphoreType.DMA
    col = pltpu.VMEM((rows, LANES), BF)
    per_patch = pltpu.VMEM((npatch, LANES, PATCH), BF)
    half_f = pltpu.VMEM((PATCH, QH), F32)
    half_b = pltpu.VMEM((PATCH, QH), BF)
    masked = pltpu.VMEM((2 * LANES, QH), BF)
    coded = pltpu.VMEM((n, 16, cap), BF)
    full = pltpu.VMEM((m, rows, LANES), BF)
    hop_buf = pltpu.VMEM((npatch, PATCH // 2, LANES), BF)
    return tuple(
        pl.pallas_call(
            layer_kernel,
            out_shape=[
                jax.ShapeDtypeStruct((rows, LANES), F32),
                jax.ShapeDtypeStruct((band, 3, LANES), F32),
                jax.ShapeDtypeStruct((band, LANES), F32),
            ],
            in_specs=[hbm, hbm] + [vmem] * 5,
            out_specs=[vmem] * 3,
            scratch_shapes=[
                col, col, col, pltpu.VMEM((n * cap, LANES), BF), coded,
                col, pltpu.VMEM((n * cap, LANES), BF), coded, pltpu.VMEM((blocks, BLK), jnp.int32),
                full, full, pltpu.VMEM((rows, feats), BF), col, col,
                pltpu.VMEM((npatch, 2 * LANES, PATCH), BF),
                per_patch, per_patch, per_patch, pltpu.VMEM((LANES, PATCH), BF),
                pltpu.VMEM((npatch, 4 * LANES, PATCH), BF),
                masked, masked, half_f, half_f,
                pltpu.VMEM((npatch * HEADS, PATCH, PATCH), BF),
                half_b, half_b,
                pltpu.VMEM((2, 1, QH), F32),
                pltpu.VMEM((npatch * HEADS, 1, PATCH), F32),
                pltpu.VMEM((feats, 4 * LANES), BF),
                pltpu.VMEM((npatch, 8, PATCH), F32),
                pltpu.VMEM((rows, LANES), F32),
                hop_buf, hop_buf,
                pltpu.VMEM((m - 1, npatch, 8, PATCH), F32),
                pltpu.VMEM((n, band, 4 * LANES), BF),
                dma((2,)), dma((3,)), dma((3,)), dma((2,)), dma((2, m, blocks)),
                dma((npatch, 6)), dma((npatch, 6)), dma((m - 1,)), dma((m - 1,)), dma(()), dma(()),
            ],
            compiler_params=pltpu.CompilerParams(
                collective_id=0, has_side_effects=True, vmem_limit_bytes=67043328
            ),
            name="layer",
        )(
            scan_points, voxel_grads, orders,
            qkv_weight[:, 0], qkv_weight[:, 1], qkv_weight[:, 2], out_weight,
        )
    )


def solution(mesh):
    in_specs = (
        P("seq", None), P("seq"), P("seq"), P(None, None, "mp"), P(None, "mp"),
        P("seq", None), P("seq", None), P("seq"),
    )
    out_specs = (P("seq", "mp"), P("seq", None, "mp"), P("seq", "mp"))
    return jax.shard_map(local, mesh=mesh, in_specs=in_specs, out_specs=out_specs, check_vma=False)
```

```python
import jax
import jax.numpy as jnp
from jax import lax
from jax.experimental import pallas as pl
from jax.experimental.pallas import tpu as pltpu
from jax.sharding import PartitionSpec as P

HD = 16
PATCH = 1024
LANES = 128
BLK = 256
HEADS = LANES // HD
PBLK = PATCH // BLK
QH = 512
EPSILON = 1e-05
LOG2E = 1.4426950408889634
BF = jnp.bfloat16
F32 = jnp.float32
MESH = pl.DeviceIdType.MESH


def dotf(a, b):
    return jnp.dot(a, b, preferred_element_type=F32)


def dot_nt(a, b):
    return lax.dot_general(a, b, (((1,), (1,)), ((), ())), preferred_element_type=F32)


def iota(shape, axis):
    return lax.broadcasted_iota(jnp.int32, shape, axis)


def as_mask(cond):
    return jnp.where(cond, 1.0, 0.0).astype(BF)


def small_iota(shape, axis):
    return iota(shape, axis).astype(F32).astype(BF)


def lane_copy(row):
    return jnp.broadcast_to(row.astype(F32), (LANES, BLK)).T


def block_row(ref, b):
    per = BLK // LANES
    return jnp.concatenate([ref[pl.ds(b * per + u, 1), :] for u in range(per)], axis=1)


def select_rows(order_row, count):
    want = lane_copy(order_row)
    high = jnp.floor(want * (1.0 / LANES))
    low = (want - high * LANES).astype(BF)
    high = high.astype(BF)
    zero = jnp.zeros((BLK, LANES), BF)
    here = jnp.where(low == small_iota((BLK, LANES), 1), jnp.ones((BLK, LANES), BF), zero)
    return jnp.concatenate([jnp.where(high == c, here, zero) for c in range(count // LANES)], axis=1)


def hits(position, b):
    shape = (BLK, position.shape[1])
    near = jnp.clip(position.astype(F32) - (b * BLK).astype(F32), -1.0, float(BLK)).astype(BF)
    return jnp.where(small_iota(shape, 0) == near, jnp.ones(shape, BF), jnp.zeros(shape, BF))


def lanes_of(ref, r):
    return jnp.concatenate([ref[j, r, :] for j in range(ref.shape[0])], axis=1)


def rows_of(block, size):
    return pl.ds(pl.multiple_of(block * size, size), size)


def remote(src, dst, send_sem, recv_sem, axis, to):
    return pltpu.make_async_remote_copy(
        src_ref=src, dst_ref=dst, send_sem=send_sem, recv_sem=recv_sem,
        device_id={axis: to}, device_id_type=MESH,
    )


def layer_kernel(
    scan, voxels, send_order, arrive_order, point, shard, w, wo,
    d_points, grad_qkv, grad_out,
    x, v, sendp, sendv, sendi, gotp, gotv, goti, place, at_all,
    pts, dout, hid, kn, vn, qhl, qt, kt, vt, dat, dpt, qm0, qm1, s0, s1, e_all, ds0, ds1, top, linv,
    grads, stats, invb, rel_l, rel_r, got_s, got_g,
    in_sem, send_sem, recv_sem, ring_send, ring_recv, p_send, p_recv, s_send, s_recv, g_send, g_recv,
):
    seq, mp = lax.axis_index("seq"), lax.axis_index("mp")
    n, m = lax.axis_size("seq"), lax.axis_size("mp")
    rows = x.shape[0]
    npatch = rows // PATCH
    grp = rows // n
    cap = gotv.shape[0] // n
    blocks = rows // BLK
    right, left, opposite = lax.rem(mp + 1, m), lax.rem(mp + m - 1, m), lax.rem(mp + 2, m)
    part, got_l, got_r = pts, x, v

    mine = pl.ds(pl.multiple_of(mp * LANES, LANES), LANES)
    in_x = pltpu.make_async_copy(scan.at[:, mine], x, in_sem.at[0])
    in_v = pltpu.make_async_copy(voxels.at[:, mine], v, in_sem.at[1])
    in_x.start()
    in_v.start()
    barrier = pltpu.get_barrier_semaphore()
    for k in range(1, n):
        pl.semaphore_signal(barrier, inc=1, device_id={"seq": lax.rem(seq + k, n)}, device_id_type=MESH)
    for to in (right, left, opposite):
        pl.semaphore_signal(barrier, inc=1, device_id={"mp": to}, device_id_type=MESH)

    def send(src, dst, kind, peer):
        return remote(src, dst, send_sem.at[kind], recv_sem.at[kind], "seq", peer)

    tri = as_mask(iota((BLK, BLK), 0) < iota((BLK, BLK), 1))
    carry = jnp.zeros((n, 1), F32)
    codes = jnp.zeros((3 * n, cap), F32)
    for b in range(blocks):
        target = shard[:, b * BLK : (b + 1) * BLK]
        hot = jnp.where(iota((n, BLK), 0) == target, 1.0, 0.0)
        before = dotf(hot.astype(BF), tri) + carry
        rank = jnp.sum(before * hot, axis=0, keepdims=True)
        carry = carry + jnp.sum(hot, axis=1, keepdims=True)
        place[b : b + 1, :] = target * cap + rank.astype(jnp.int32)
        where_to = block_row(point, b)
        high = (where_to // 64).astype(F32)
        low = (where_to % 64).astype(F32)
        slot = as_mask(iota((cap, BLK), 0) == rank.astype(jnp.int32))
        coded = jnp.concatenate([hot * high, hot * low, hot], axis=0).astype(BF)
        codes = codes + dot_nt(coded, slot)
    sub16 = iota((16, cap), 0)
    for t in range(n):
        a, b, c = codes[t : t + 1], codes[n + t : n + t + 1], codes[2 * n + t : 2 * n + t + 1]
        sendi[t] = jnp.where(sub16 == 0, a, jnp.where(sub16 == 1, b, c)).astype(BF)
    in_x.wait()
    pl.semaphore_wait(barrier, n + m - 2)
    per = BLK // grp

    def points_out(i, _):
        b = lax.rem(i + seq // per, blocks)
        hot = select_rows(block_row(send_order, b), rows)
        sendp[rows_of(b, BLK), :] = dotf(hot, x[...]).astype(BF)
        for u in range(per):
            peer = b * per + u

            @pl.when(peer != seq)
            def _():
                send(sendp.at[rows_of(peer, grp)], gotp.at[rows_of(seq, grp)], 0, peer).start()

        return 0

    lax.fori_loop(0, blocks, points_out, 0)
    gotp[rows_of(seq, grp), :] = sendp[rows_of(seq, grp), :]

    in_v.wait()
    per_v = BLK // cap
    vblocks = n // per_v

    def voxels_out(i, _):
        b = lax.rem(i + seq // per_v, vblocks)
        hot = jnp.concatenate([hits(place[c : c + 1, :], b) for c in range(blocks)], axis=1)
        sendv[rows_of(b, BLK), :] = dotf(hot, v[...]).astype(BF)
        for u in range(per_v):
            peer = b * per_v + u

            @pl.when(peer != seq)
            def _():
                send(sendv.at[rows_of(peer, cap)], gotv.at[rows_of(seq, cap)], 1, peer).start()
                send(sendi.at[peer], goti.at[seq], 2, peer).start()

        return 0

    lax.fori_loop(0, vblocks, voxels_out, 0)
    gotv[rows_of(seq, cap), :] = sendv[rows_of(seq, cap), :]
    goti[seq] = sendi[seq]

    def wait_all(kind, ref, size):
        other = ref.at[pl.ds(0, size)]
        send(other, other, kind, seq).wait_recv()
        send(other, other, kind, seq).wait_send()

    def ring(full, kind, owner, b, to):
        at = full.at[owner, rows_of(b, BLK)]
        return remote(at, at, ring_send.at[kind], ring_recv.at[kind, owner, b], "mp", to)

    def goes_right(b):
        return lax.rem(b, PBLK) < PBLK // 2

    def relay(full, kind, b):
        @pl.when(goes_right(b))
        def _():
            ring(full, kind, left, b, right).wait_recv()
            ring(full, kind, left, b, right).start()

        @pl.when(jnp.logical_not(goes_right(b)))
        def _():
            ring(full, kind, right, b, left).wait_recv()
            ring(full, kind, right, b, left).start()

    def arrived(full, kind, b):
        @pl.when(goes_right(b))
        def _():
            ring(full, kind, right, b, left).wait_recv()

        @pl.when(jnp.logical_not(goes_right(b)))
        def _():
            ring(full, kind, left, b, right).wait_recv()

        ring(full, kind, opposite, b, right).wait_recv()

    def ring_sent(full, kind):
        for _ in range(3):
            remote(full.at[0], full.at[0], ring_send.at[kind], ring_recv.at[kind, 0, 0], "mp", right).wait_send()

    wait_all(0, gotp, (n - 1) * grp)

    def points_in(b, _):
        hot = select_rows(block_row(arrive_order, b), rows)
        pts[mp, rows_of(b, BLK), :] = dotf(hot, gotp[...]).astype(BF)
        ring(pts, 0, mp, b, right).start()
        ring(pts, 0, mp, b, left).start()
        return 0

    lax.fori_loop(0, blocks, points_in, 0)
    wait_all(1, gotv, (n - 1) * cap)
    wait_all(2, goti, n - 1)
    for t in range(n):
        code = goti[t].astype(F32)
        at_all[t : t + 1, :] = jnp.where(code[2:3, :] > 0.5, code[0:1, :] * 64.0 + code[1:2, :], -1.0)

    def voxels_in(b, _):
        hot = jnp.concatenate([hits(at_all[t : t + 1, :], b) for t in range(n)], axis=1)
        dout[mp, rows_of(b, BLK), :] = dotf(hot, gotv[...]).astype(BF)
        ring(dout, 1, mp, b, right).start()
        ring(dout, 1, mp, b, left).start()
        relay(pts, 0, b)
        return 0

    lax.fori_loop(0, blocks, voxels_in, 0)

    wcat = jnp.concatenate([w[t] for t in range(3)], axis=1)
    ones_lane = as_mask(iota((PATCH, LANES), 1) < 3)
    halves = ((qm0, s0, ds0), (qm1, s1, ds1))

    def normalise(p):
        for b in range(PBLK):
            r = rows_of(p * PBLK + b, BLK)
            c = pl.ds(b * BLK, BLK)
            xb = lanes_of(pts, r).astype(F32)
            xb = xb - jnp.mean(xb, axis=1, keepdims=True)
            inv = lax.rsqrt(jnp.mean(xb * xb, axis=1, keepdims=True) + EPSILON)
            normed = xb * inv
            hidden = normed.astype(BF)
            hid[r, :] = hidden
            invb[r, :] = jnp.broadcast_to(inv, (BLK, LANES))
            own = normed[:, 0:LANES]
            for j in range(1, m):
                own = jnp.where(mp == j, normed[:, j * LANES : (j + 1) * LANES], own)
            d_points[r, :] = own
            proj = dotf(hidden, wcat)
            q, k, val = (proj[:, t * LANES : (t + 1) * LANES].astype(BF) for t in range(3))
            kn[r, :] = k
            vn[r, :] = val
            qf = q.astype(F32).T
            qt[p, :, c] = qf.astype(BF)
            qs = qf * (0.25 * LOG2E)
            high = qs.astype(BF)
            qhl[p, 0:LANES, c] = high
            qhl[p, LANES : 2 * LANES, c] = (qs - high.astype(F32)).astype(BF)
            kt[p, :, c] = k.astype(F32).T.astype(BF)
            vt[p, :, c] = val.astype(F32).T.astype(BF)

    def head_rows(h, base=0):
        return pl.ds(pl.multiple_of(base * LANES + h * HD, HD), HD)

    def scores(p, h, half):
        qm, s = halves[half][:2]
        c = pl.ds(half * QH, QH)
        rmask = (iota((LANES, QH), 0) // HD) == h
        zero = jnp.zeros((LANES, QH), BF)
        qm[0:LANES, :] = jnp.where(rmask, qhl[p, 0:LANES, c], zero)
        qm[LANES : 2 * LANES, :] = jnp.where(rmask, qhl[p, LANES : 2 * LANES, c], zero)
        k = kn[rows_of(p, PATCH), :]
        val = dotf(jnp.concatenate([k, k], axis=1), qm[...])
        s[...] = val
        top[half] = jnp.max(val, axis=0, keepdims=True)

    def forward(p, h, half):
        s = halves[half][1]
        c = pl.ds(half * QH, QH)
        e = jnp.exp2(s[...] - top[half]).astype(BF)
        e_all[p * HEADS + h, :, c] = e
        vt1 = jnp.concatenate([vt[p, head_rows(h), :], jnp.ones((HD, PATCH), BF)], axis=0)
        av = dotf(vt1, e)
        inv = 1.0 / av[HD : HD + 1, :]
        linv[p * HEADS + h, :, c] = inv
        dpt[p, head_rows(h, 3), c] = (av[0:HD, :] * inv).astype(BF)

    def forward_patch(p, _):
        def ready(b, _):
            arrived(pts, 0, p * PBLK + b)
            return 0

        lax.fori_loop(0, PBLK, ready, 0)
        normalise(p)
        scores(p, 0, 0)

        def step(h, _):
            @pl.when(lax.rem(h, 2) == 0)
            def _():
                relay(dout, 1, p * PBLK + h // 2)

            scores(p, h, 1)
            forward(p, h, 0)
            scores(p, jnp.minimum(h + 1, HEADS - 1), 0)
            forward(p, h, 1)
            return 0

        lax.fori_loop(0, HEADS, step, 0)
        return 0

    lax.fori_loop(0, npatch, forward_patch, 0)

    def hop(p, sem, src, dst, to):
        return remote(src, dst, p_send.at[p, sem], p_recv.at[p, sem], "mp", to)

    def hops(p, *which):
        low, high = rows_of(2 * p, PATCH // 2), rows_of(2 * p + 1, PATCH // 2)
        ends = (
            (part.at[opposite, low], rel_l.at[p], right),
            (part.at[opposite, high], rel_r.at[p], left),
            (part.at[right, high], got_l.at[high], right),
            (part.at[left, low], got_r.at[low], left),
            (rel_l.at[p], got_l.at[low], right),
            (rel_r.at[p], got_r.at[high], left),
        )
        return [hop(p, w, *ends[w]) for w in which]

    def hand_on(p):
        low, high = rows_of(2 * p, PATCH // 2), rows_of(2 * p + 1, PATCH // 2)
        in_l, in_r, out_l, out_r = hops(p, 0, 1, 4, 5)
        in_l.wait()
        rel_l[p] = (rel_l[p].astype(F32) + part[right, low, :].astype(F32)).astype(BF)
        out_l.start()
        in_r.wait()
        rel_r[p] = (rel_r[p].astype(F32) + part[left, high, :].astype(F32)).astype(BF)
        out_r.start()

    def backward(p, h, half):
        ds_ref = halves[half][2]
        i = p * HEADS + h
        c = pl.ds(half * QH, QH)
        scaled = (dat[head_rows(h), c].astype(F32) * linv[i, :, c]).astype(BF)
        da = scaled.astype(F32)
        delta = jnp.sum(da * dpt[p, head_rows(h, 3), c].astype(F32), axis=0, keepdims=True)
        d1 = delta.astype(BF).astype(F32)
        d2 = (delta - d1).astype(BF).astype(F32)
        d3 = delta - d1 - d2
        sub = iota((LANES, QH), 0)
        tile = jnp.where(sub // HD == h, jnp.concatenate([da] * HEADS, axis=0), 0.0)
        tail = jnp.where(sub == 0, -d1, jnp.where(sub == 1, -d2, jnp.where(sub == 2, -d3, 0.0)))
        vv = jnp.concatenate([vn[rows_of(p, PATCH), :], ones_lane], axis=1)
        dp = dotf(vv, jnp.concatenate([tile, tail], axis=0).astype(BF))
        ds = e_all[i, :, c] * dp.astype(BF)
        ds_ref[...] = ds
        dpt[p, head_rows(h), c] = (dotf(kt[p, head_rows(h), :], ds) * 0.25).astype(BF)
        return dot_nt(qt[p, head_rows(h), c], ds_ref[...]), dot_nt(scaled, e_all[i, :, c])

    def dout_in(b, _):
        arrived(dout, 1, b)
        return 0

    lax.fori_loop(0, blocks, dout_in, 0)
    ring_sent(pts, 0)
    ring_sent(dout, 1)

    def backward_patch(p, _):
        for b in range(PBLK):
            da = dotf(lanes_of(dout, rows_of(p * PBLK + b, BLK)), wo[...]).astype(BF)
            dat[:, b * BLK : (b + 1) * BLK] = da.astype(F32).T.astype(BF)

        def step(h, _):
            @pl.when(jnp.logical_and(p == 1, h == HEADS // 2))
            def _():
                hand_on(0)

            dk0, dv0 = backward(p, h, 0)
            dk1, dv1 = backward(p, h, 1)
            dpt[p, head_rows(h, 1), :] = ((dk0 + dk1) * 0.25).astype(BF)
            dpt[p, head_rows(h, 2), :] = (dv0 + dv1).astype(BF)
            return 0

        lax.fori_loop(0, HEADS, step, 0)
        for b in range(PBLK):
            r = rows_of(p * PBLK + b, BLK)
            dproj = dpt[p, 0 : 3 * LANES, pl.ds(b * BLK, BLK)].astype(F32).T.astype(BF)
            pd = dot_nt(dproj, wcat).astype(BF)
            xb = lanes_of(pts, r).astype(F32)
            normed = (xb - jnp.mean(xb, axis=1, keepdims=True)) * invb[r, 0:1]
            for j in range(m):
                part[j, r, :] = pd[:, j * LANES : (j + 1) * LANES]
            z = pd.astype(F32) * normed
            zh = z.astype(BF)
            zl = (z - zh.astype(F32)).astype(BF)
            on = jnp.ones((8, pd.shape[1]), BF)
            total = dot_nt(on, pd)
            cross = dot_nt(on, zh) + dot_nt(on, zl)
            stats[p, :, b * BLK : (b + 1) * BLK] = jnp.where(iota((8, BLK), 0) == 0, total, cross)
        for c in hops(p, 0, 1, 2, 3):
            c.start()
        return 0

    lax.fori_loop(0, npatch, backward_patch, 0)

    def stat_copy(i, to):
        return remote(stats, got_s.at[i], s_send.at[i], s_recv.at[i], "mp", to)

    for i, to in enumerate((right, left, opposite)):
        stat_copy(i, to).start()
    upper, lower = 0.0, 0.0
    for p in range(npatch):
        r = pl.ds(p * PATCH, PATCH)
        upper = upper + dotf(dpt[p, 0 : 3 * LANES, :], hid[r, :])
        lower = lower + dotf(dpt[p, 3 * LANES : 4 * LANES, :], lanes_of(dout, r))
    grads[:, 0 : 3 * LANES] = upper.T.astype(BF)
    grads[:, 3 * LANES : 4 * LANES] = lower.T.astype(BF)
    band = grads.shape[0] // n

    def grad_copy(src, dst, peer):
        return remote(src, dst, g_send, g_recv, "seq", peer)

    def grads_out(k, _):
        peer = lax.rem(seq + k, n)
        grad_copy(grads.at[rows_of(peer, band)], got_g.at[seq], peer).start()
        return 0

    lax.fori_loop(1, n, grads_out, 0)
    got_g[seq] = grads[rows_of(seq, band), :]
    hand_on(1)
    for i, to in enumerate((right, left, opposite)):
        stat_copy(i, to).wait()
    scale = 1.0 / (m * LANES)

    def finish(p):
        for c in hops(p, 2, 3, 4, 5):
            c.wait()
        st = (stats[p] + got_s[0, p] + got_s[1, p] + got_s[2, p]) * scale
        for b in range(PBLK):
            r = pl.ds(p * PATCH + b * BLK, BLK)
            mean_grad = lane_copy(st[0:1, b * BLK : (b + 1) * BLK])
            mean_cross = lane_copy(st[1:2, b * BLK : (b + 1) * BLK])
            d_hidden = part[mp, r, :].astype(F32) + got_l[r, :].astype(F32) + got_r[r, :].astype(F32)
            d_points[r, :] = dout[mp, r, :].astype(F32) + invb[r, :] * (
                d_hidden - mean_grad - d_points[r, :] * mean_cross
            )

    finish(0)
    others = got_g.at[pl.ds(0, n - 1)]
    grad_copy(others, others, seq).wait()
    total = jnp.zeros((band, grads.shape[1]), F32)
    for k in range(n):
        total = total + got_g[k].astype(F32)
    for t in range(3):
        grad_qkv[t] = total[:, t * LANES : (t + 1) * LANES]
    grad_out[...] = total[:, 3 * LANES : 4 * LANES]
    finish(1)


def local(
    scan_points, send_order, arrive_order, qkv_weight, out_weight, voxel_grads, voxel_shard, voxel_point
):
    n, m = lax.axis_size("seq"), lax.axis_size("mp")
    rows = scan_points.shape[0]
    feats = m * LANES
    grp, cap = rows // n, 2 * voxel_grads.shape[0] // n
    blocks, npatch, band = rows // BLK, rows // PATCH, feats // n
    vmem, hbm = pl.BlockSpec(memory_space=pltpu.VMEM), pl.BlockSpec(memory_space=pl.ANY)
    dma = pltpu.SemaphoreType.DMA
    col = pltpu.VMEM((rows, LANES), BF)
    per_patch = pltpu.VMEM((npatch, LANES, PATCH), BF)
    half_f = pltpu.VMEM((PATCH, QH), F32)
    half_b = pltpu.VMEM((PATCH, QH), BF)
    masked = pltpu.VMEM((2 * LANES, QH), BF)
    coded = pltpu.VMEM((n, 16, cap), BF)
    full = pltpu.VMEM((m, rows, LANES), BF)
    hop_buf = pltpu.VMEM((npatch, PATCH // 2, LANES), BF)
    d_points, grad_qkv, grad_out = (
        pl.pallas_call(
            layer_kernel,
            out_shape=[
                jax.ShapeDtypeStruct((rows, LANES), F32),
                jax.ShapeDtypeStruct((3, band, LANES), F32),
                jax.ShapeDtypeStruct((band, LANES), F32),
            ],
            in_specs=[hbm, hbm] + [vmem] * 6,
            out_specs=[vmem] * 3,
            scratch_shapes=[
                col, col, col, pltpu.VMEM((n * cap, LANES), BF), coded,
                col, pltpu.VMEM((n * cap, LANES), BF), coded, pltpu.VMEM((blocks, BLK), jnp.int32), pltpu.VMEM((n, cap), F32),
                full, full, pltpu.VMEM((rows, feats), BF), col, col,
                pltpu.VMEM((npatch, 2 * LANES, PATCH), BF),
                per_patch, per_patch, per_patch, pltpu.VMEM((LANES, PATCH), BF),
                pltpu.VMEM((npatch, 4 * LANES, PATCH), BF),
                masked, masked, half_f, half_f,
                pltpu.VMEM((npatch * HEADS, PATCH, PATCH), BF),
                half_b, half_b,
                pltpu.VMEM((2, 1, QH), F32),
                pltpu.VMEM((npatch * HEADS, 1, PATCH), F32),
                pltpu.VMEM((feats, 4 * LANES), BF),
                pltpu.VMEM((npatch, 8, PATCH), F32),
                pltpu.VMEM((rows, LANES), F32),
                hop_buf, hop_buf,
                pltpu.VMEM((m - 1, npatch, 8, PATCH), F32),
                pltpu.VMEM((n, band, 4 * LANES), BF),
                dma((2,)), dma((3,)), dma((3,)), dma((2,)), dma((2, m, blocks)),
                dma((npatch, 6)), dma((npatch, 6)), dma((m - 1,)), dma((m - 1,)), dma(()), dma(()),
            ],
            compiler_params=pltpu.CompilerParams(
                collective_id=0, has_side_effects=True, vmem_limit_bytes=67043328
            ),
            name="layer",
        )(
            scan_points, voxel_grads,
            send_order.reshape(-1, LANES), arrive_order.reshape(-1, LANES), voxel_point.reshape(-1, LANES),
            voxel_shard.reshape(1, -1), jnp.transpose(qkv_weight, (1, 0, 2)), out_weight,
        )
    )
    return d_points, jnp.transpose(grad_qkv, (1, 0, 2)), grad_out


def solution(mesh):
    in_specs = (
        P("seq", None), P("seq"), P("seq"), P(None, None, "mp"), P(None, "mp"),
        P("seq", None), P("seq", None), P("seq"),
    )
    out_specs = (P("seq", "mp"), P("seq", None, "mp"), P("seq", "mp"))
    return jax.shard_map(local, mesh=mesh, in_specs=in_specs, out_specs=out_specs, check_vma=False)
```

```python
import jax
import jax.numpy as jnp
from jax import lax
from jax.experimental import pallas as pl
from jax.experimental.pallas import tpu as pltpu
from jax.sharding import PartitionSpec as P

HD = 16
PATCH = 1024
LANES = 128
BLK = 256
HEADS = LANES // HD
PBLK = PATCH // BLK
QH = 512
CH = 256
EPSILON = 1e-05
LOG2E = 1.4426950408889634
BF = jnp.bfloat16
F32 = jnp.float32
MESH = pl.DeviceIdType.MESH


def dotf(a, b):
    return jnp.dot(a, b, preferred_element_type=F32)


def dot_nt(a, b):
    return lax.dot_general(a, b, (((1,), (1,)), ((), ())), preferred_element_type=F32)


def iota(shape, axis):
    return lax.broadcasted_iota(jnp.int32, shape, axis)


def as_mask(cond):
    return jnp.where(cond, 1.0, 0.0).astype(BF)


def small_iota(shape, axis):
    return iota(shape, axis).astype(F32).astype(BF)


def lane_copy(row):
    return jnp.broadcast_to(row.astype(F32), (LANES, BLK)).T


def block_row(ref, b):
    per = BLK // LANES
    return jnp.concatenate([ref[pl.ds(b * per + u, 1), :] for u in range(per)], axis=1)


def select_rows(order_row, count):
    want = lane_copy(order_row)
    high = jnp.floor(want * (1.0 / LANES))
    low = (want - high * LANES).astype(BF)
    high = high.astype(BF)
    zero = jnp.zeros((BLK, LANES), BF)
    here = jnp.where(low == small_iota((BLK, LANES), 1), jnp.ones((BLK, LANES), BF), zero)
    return jnp.concatenate([jnp.where(high == c, here, zero) for c in range(count // LANES)], axis=1)


def hits(position, b):
    shape = (BLK, position.shape[1])
    near = jnp.clip(position.astype(F32) - (b * BLK).astype(F32), -1.0, float(BLK)).astype(BF)
    return jnp.where(small_iota(shape, 0) == near, jnp.ones(shape, BF), jnp.zeros(shape, BF))


def lanes_of(ref, r):
    return jnp.concatenate([ref[j, r, :] for j in range(ref.shape[0])], axis=1)


def rows_of(block, size):
    return pl.ds(pl.multiple_of(block * size, size), size)


def remote(src, dst, send_sem, recv_sem, axis, to):
    return pltpu.make_async_remote_copy(
        src_ref=src, dst_ref=dst, send_sem=send_sem, recv_sem=recv_sem,
        device_id={axis: to}, device_id_type=MESH,
    )


def layer_kernel(
    scan, voxels, send_order, arrive_order, point, shard, w, wo,
    d_points, grad_qkv, grad_out,
    x, v, sendp, sendv, sendi, gotp, gotv, goti, place, at_all,
    pts, dout, hid, kn, vn, qhl, qt, kt, vt, dat, dpt, qm0, qm1, s0, s1, e_all, ds0, ds1, top, linv, dst, est,
    grads, stats, invb, rel_l, rel_r, got_s, got_g,
    in_sem, send_sem, recv_sem, ring_send, ring_recv, p_send, p_recv, s_send, s_recv, g_send, g_recv,
):
    seq, mp = lax.axis_index("seq"), lax.axis_index("mp")
    n, m = lax.axis_size("seq"), lax.axis_size("mp")
    rows = x.shape[0]
    npatch = rows // PATCH
    grp = rows // n
    cap = gotv.shape[0] // n
    blocks = rows // BLK
    right, left, opposite = lax.rem(mp + 1, m), lax.rem(mp + m - 1, m), lax.rem(mp + 2, m)
    part, got_l, got_r = pts, x, v

    mine = pl.ds(pl.multiple_of(mp * LANES, LANES), LANES)
    in_x = pltpu.make_async_copy(scan.at[:, mine], x, in_sem.at[0])
    in_v = pltpu.make_async_copy(voxels.at[:, mine], v, in_sem.at[1])
    in_x.start()
    in_v.start()
    barrier = pltpu.get_barrier_semaphore()
    for k in range(1, n):
        pl.semaphore_signal(barrier, inc=1, device_id={"seq": lax.rem(seq + k, n)}, device_id_type=MESH)
    for to in (right, left, opposite):
        pl.semaphore_signal(barrier, inc=1, device_id={"mp": to}, device_id_type=MESH)

    def send(src, dst, kind, peer):
        return remote(src, dst, send_sem.at[kind], recv_sem.at[kind], "seq", peer)

    tri = as_mask(iota((BLK, BLK), 0) < iota((BLK, BLK), 1))
    carry = jnp.zeros((n, 1), F32)
    codes = jnp.zeros((3 * n, cap), F32)
    for b in range(blocks):
        target = shard[:, b * BLK : (b + 1) * BLK]
        hot = jnp.where(iota((n, BLK), 0) == target, 1.0, 0.0)
        before = dotf(hot.astype(BF), tri) + carry
        rank = jnp.sum(before * hot, axis=0, keepdims=True)
        carry = carry + jnp.sum(hot, axis=1, keepdims=True)
        place[b : b + 1, :] = target * cap + rank.astype(jnp.int32)
        where_to = block_row(point, b)
        high = (where_to // 64).astype(F32)
        low = (where_to % 64).astype(F32)
        slot = as_mask(iota((cap, BLK), 0) == rank.astype(jnp.int32))
        coded = jnp.concatenate([hot * high, hot * low, hot], axis=0).astype(BF)
        codes = codes + dot_nt(coded, slot)
    sub16 = iota((16, cap), 0)
    for t in range(n):
        a, b, c = codes[t : t + 1], codes[n + t : n + t + 1], codes[2 * n + t : 2 * n + t + 1]
        sendi[t] = jnp.where(sub16 == 0, a, jnp.where(sub16 == 1, b, c)).astype(BF)
    in_x.wait()
    per = BLK // grp

    def ordered(i):
        return lax.rem(i + seq // per, blocks)

    def points_pick(i, _):
        b = ordered(i)
        hot = select_rows(block_row(send_order, b), rows)
        sendp[rows_of(b, BLK), :] = dotf(hot, x[...]).astype(BF)
        return 0

    def points_send(i, _):
        for u in range(per):
            peer = ordered(i) * per + u

            @pl.when(peer != seq)
            def _():
                send(sendp.at[rows_of(peer, grp)], gotp.at[rows_of(seq, grp)], 0, peer).start()

        return 0

    def points_out(i, _):
        points_pick(i, 0)
        points_send(i, 0)
        return 0

    lax.fori_loop(0, blocks // 2, points_pick, 0)
    pl.semaphore_wait(barrier, n + m - 2)
    lax.fori_loop(0, blocks // 2, points_send, 0)
    lax.fori_loop(blocks // 2, blocks, points_out, 0)
    gotp[rows_of(seq, grp), :] = sendp[rows_of(seq, grp), :]

    in_v.wait()
    per_v = BLK // cap
    vblocks = n // per_v

    def voxels_out(i, _):
        b = lax.rem(i + seq // per_v, vblocks)
        hot = jnp.concatenate([hits(place[c : c + 1, :], b) for c in range(blocks)], axis=1)
        sendv[rows_of(b, BLK), :] = dotf(hot, v[...]).astype(BF)
        for u in range(per_v):
            peer = b * per_v + u

            @pl.when(peer != seq)
            def _():
                send(sendv.at[rows_of(peer, cap)], gotv.at[rows_of(seq, cap)], 1, peer).start()
                send(sendi.at[peer], goti.at[seq], 2, peer).start()

        return 0

    lax.fori_loop(0, vblocks, voxels_out, 0)
    gotv[rows_of(seq, cap), :] = sendv[rows_of(seq, cap), :]
    goti[seq] = sendi[seq]

    def wait_all(kind, ref, size):
        other = ref.at[pl.ds(0, size)]
        send(other, other, kind, seq).wait_recv()
        send(other, other, kind, seq).wait_send()

    def ring(full, kind, owner, b, to):
        at = full.at[owner, rows_of(b, BLK)]
        return remote(at, at, ring_send.at[kind], ring_recv.at[kind, owner, b], "mp", to)

    def goes_right(b):
        return lax.rem(b, PBLK) < PBLK // 2

    def relay(full, kind, b):
        @pl.when(goes_right(b))
        def _():
            ring(full, kind, left, b, right).wait_recv()
            ring(full, kind, left, b, right).start()

        @pl.when(jnp.logical_not(goes_right(b)))
        def _():
            ring(full, kind, right, b, left).wait_recv()
            ring(full, kind, right, b, left).start()

    def arrived(full, kind, b):
        @pl.when(goes_right(b))
        def _():
            ring(full, kind, right, b, left).wait_recv()

        @pl.when(jnp.logical_not(goes_right(b)))
        def _():
            ring(full, kind, left, b, right).wait_recv()

        ring(full, kind, opposite, b, right).wait_recv()

    def ring_sent(full, kind):
        for _ in range(3):
            remote(full.at[0], full.at[0], ring_send.at[kind], ring_recv.at[kind, 0, 0], "mp", right).wait_send()

    wait_all(0, gotp, (n - 1) * grp)

    def points_in(b, _):
        hot = select_rows(block_row(arrive_order, b), rows)
        pts[mp, rows_of(b, BLK), :] = dotf(hot, gotp[...]).astype(BF)
        ring(pts, 0, mp, b, right).start()
        ring(pts, 0, mp, b, left).start()
        return 0

    lax.fori_loop(0, blocks, points_in, 0)
    wait_all(1, gotv, (n - 1) * cap)
    wait_all(2, goti, n - 1)
    for t in range(n):
        code = goti[t].astype(F32)
        at_all[t : t + 1, :] = jnp.where(code[2:3, :] > 0.5, code[0:1, :] * 64.0 + code[1:2, :], -1.0)

    def voxels_in(b, _):
        relay(pts, 0, b)
        hot = jnp.concatenate([hits(at_all[t : t + 1, :], b) for t in range(n)], axis=1)
        dout[mp, rows_of(b, BLK), :] = dotf(hot, gotv[...]).astype(BF)
        ring(dout, 1, mp, b, right).start()
        ring(dout, 1, mp, b, left).start()
        return 0

    lax.fori_loop(0, blocks, voxels_in, 0)

    wcat = jnp.concatenate([w[t] for t in range(3)], axis=1)
    ones_lane = as_mask(iota((PATCH, LANES), 1) < 3)
    halves = ((qm0, s0, ds0), (qm1, s1, ds1))

    def normalise(p):
        for b in range(PBLK):
            r = rows_of(p * PBLK + b, BLK)
            c = pl.ds(b * BLK, BLK)
            xb = lanes_of(pts, r).astype(F32)
            xb = xb - jnp.mean(xb, axis=1, keepdims=True)
            inv = lax.rsqrt(jnp.mean(xb * xb, axis=1, keepdims=True) + EPSILON)
            normed = xb * inv
            hidden = normed.astype(BF)
            hid[r, :] = hidden
            invb[r, :] = jnp.broadcast_to(inv, (BLK, LANES))
            own = normed[:, 0:LANES]
            for j in range(1, m):
                own = jnp.where(mp == j, normed[:, j * LANES : (j + 1) * LANES], own)
            d_points[r, :] = own
            proj = dotf(hidden, wcat)
            q, k, val = (proj[:, t * LANES : (t + 1) * LANES].astype(BF) for t in range(3))
            kn[r, :] = k
            vn[r, :] = val
            qf = q.astype(F32).T
            qt[p, :, c] = qf.astype(BF)
            qs = qf * (0.25 * LOG2E)
            high = qs.astype(BF)
            qhl[p, 0:LANES, c] = high
            qhl[p, LANES : 2 * LANES, c] = (qs - high.astype(F32)).astype(BF)
            kt[p, :, c] = k.astype(F32).T.astype(BF)
            vt[p, :, c] = val.astype(F32).T.astype(BF)

    def head_rows(h, base=0):
        return pl.ds(pl.multiple_of(base * LANES + h * HD, HD), HD)

    def scores(p, h, half):
        qm, s = halves[half][:2]
        c = pl.ds(half * QH, QH)
        rmask = (iota((LANES, QH), 0) // HD) == h
        zero = jnp.zeros((LANES, QH), BF)
        qm[0:LANES, :] = jnp.where(rmask, qhl[p, 0:LANES, c], zero)
        qm[LANES : 2 * LANES, :] = jnp.where(rmask, qhl[p, LANES : 2 * LANES, c], zero)
        k = kn[rows_of(p, PATCH), :]
        val = dotf(jnp.concatenate([k, k], axis=1), qm[...])
        s[...] = val
        top[half] = jnp.max(val, axis=0, keepdims=True)

    def forward(p, h, half):
        s = halves[half][1]
        c = pl.ds(half * QH, QH)
        e = jnp.exp2(s[...] - top[half]).astype(BF)
        e_all[p * HEADS + h, :, c] = e
        vt1 = jnp.concatenate([vt[p, head_rows(h), :], jnp.ones((HD, PATCH), BF)], axis=0)
        av = dotf(vt1, e)
        inv = 1.0 / av[HD : HD + 1, :]
        linv[p * HEADS + h, :, c] = inv
        dpt[p, head_rows(h, 3), c] = (av[0:HD, :] * inv).astype(BF)

    def forward_patch(p, _):
        def ready(b, _):
            arrived(pts, 0, p * PBLK + b)
            return 0

        lax.fori_loop(0, PBLK, ready, 0)
        normalise(p)
        scores(p, 0, 0)

        def step(h, _):
            @pl.when(lax.rem(h, 2) == 0)
            def _():
                relay(dout, 1, p * PBLK + h // 2)

            scores(p, h, 1)
            forward(p, h, 0)
            scores(p, jnp.minimum(h + 1, HEADS - 1), 0)
            forward(p, h, 1)
            return 0

        lax.fori_loop(0, HEADS, step, 0)
        return 0

    lax.fori_loop(0, npatch, forward_patch, 0)

    def hop(p, sem, src, dst, to):
        return remote(src, dst, p_send.at[p, sem], p_recv.at[p, sem], "mp", to)

    def hops(p, *which):
        low, high = rows_of(2 * p, PATCH // 2), rows_of(2 * p + 1, PATCH // 2)
        ends = (
            (part.at[opposite, low], rel_l.at[p], right),
            (part.at[opposite, high], rel_r.at[p], left),
            (part.at[right, high], got_l.at[high], right),
            (part.at[left, low], got_r.at[low], left),
            (rel_l.at[p], got_l.at[low], right),
            (rel_r.at[p], got_r.at[high], left),
        )
        return [hop(p, w, *ends[w]) for w in which]

    def hand_on(p):
        low, high = rows_of(2 * p, PATCH // 2), rows_of(2 * p + 1, PATCH // 2)
        in_l, in_r, out_l, out_r = hops(p, 0, 1, 4, 5)
        in_l.wait()
        rel_l[p] = (rel_l[p].astype(F32) + part[right, low, :].astype(F32)).astype(BF)
        out_l.start()
        in_r.wait()
        rel_r[p] = (rel_r[p].astype(F32) + part[left, high, :].astype(F32)).astype(BF)
        out_r.start()

    def backward(p, h, half):
        ds_ref = halves[half][2]
        i = p * HEADS + h
        c = pl.ds(half * QH, QH)
        scaled = (dat[head_rows(h), c].astype(F32) * linv[i, :, c]).astype(BF)
        da = scaled.astype(F32)
        delta = jnp.sum(da * dpt[p, head_rows(h, 3), c].astype(F32), axis=0, keepdims=True)
        d1 = delta.astype(BF).astype(F32)
        d2 = (delta - d1).astype(BF).astype(F32)
        d3 = delta - d1 - d2
        sub = iota((LANES, QH), 0)
        tile = jnp.where(sub // HD == h, jnp.concatenate([da] * HEADS, axis=0), 0.0)
        tail = jnp.where(sub == 0, -d1, jnp.where(sub == 1, -d2, jnp.where(sub == 2, -d3, 0.0)))
        vv = jnp.concatenate([vn[rows_of(p, PATCH), :], ones_lane], axis=1)
        dp = dotf(vv, jnp.concatenate([tile, tail], axis=0).astype(BF))
        ds = e_all[i, :, c] * dp.astype(BF)
        ds_ref[...] = ds
        dpt[p, head_rows(h), c] = (dotf(kt[p, head_rows(h), :], ds) * 0.25).astype(BF)
        for u in range(PATCH // CH):
            r = pl.ds(u * CH, CH)
            dst[half, :, r] = ds_ref[r, :].T
        for u in range(PATCH // CH):
            r = pl.ds(u * CH, CH)
            est[half, :, r] = e_all[i, r, c].T
        return dotf(qt[p, head_rows(h), c], dst[half]), dotf(scaled, est[half])

    def dout_in(b, _):
        arrived(dout, 1, b)
        return 0

    lax.fori_loop(0, blocks, dout_in, 0)
    ring_sent(pts, 0)
    ring_sent(dout, 1)

    def stat_copy(p, i, to):
        return remote(stats.at[p], got_s.at[p, i], s_send.at[p, i], s_recv.at[p, i], "mp", to)

    def backward_patch(p, _):
        for b in range(PBLK):
            da = dotf(lanes_of(dout, rows_of(p * PBLK + b, BLK)), wo[...]).astype(BF)
            dat[:, b * BLK : (b + 1) * BLK] = da.astype(F32).T.astype(BF)

        def step(h, _):
            @pl.when(jnp.logical_and(p == 1, h == HEADS // 2))
            def _():
                hand_on(0)

            dk0, dv0 = backward(p, h, 0)
            dk1, dv1 = backward(p, h, 1)
            dpt[p, head_rows(h, 1), :] = ((dk0 + dk1) * 0.25).astype(BF)
            dpt[p, head_rows(h, 2), :] = (dv0 + dv1).astype(BF)
            return 0

        lax.fori_loop(0, HEADS, step, 0)
        for b in range(PBLK):
            r = rows_of(p * PBLK + b, BLK)
            dproj = dpt[p, 0 : 3 * LANES, pl.ds(b * BLK, BLK)].astype(F32).T.astype(BF)
            pd = dot_nt(dproj, wcat).astype(BF)
            for j in range(m):
                part[j, r, :] = pd[:, j * LANES : (j + 1) * LANES]
            if b % 2 == 1:
                for c in hops(p, *((0, 3), (1, 2))[b // 2]):
                    c.start()
            gram = dot_nt(pd, hid[r, :])
            cross = jnp.sum(jnp.where(iota((BLK, BLK), 0) == iota((BLK, BLK), 1), gram, 0.0), axis=0, keepdims=True)
            total = dot_nt(jnp.ones((8, pd.shape[1]), BF), pd)
            stats[p, 2 * b : 2 * b + 1, :] = total[0:1]
            stats[p, 2 * b + 1 : 2 * b + 2, :] = cross
        for i, to in enumerate((right, left, opposite)):
            stat_copy(p, i, to).start()
        return 0

    lax.fori_loop(0, npatch, backward_patch, 0)

    upper, lower = 0.0, 0.0
    for p in range(npatch):
        r = pl.ds(p * PATCH, PATCH)
        upper = upper + dotf(dpt[p, 0 : 3 * LANES, :], hid[r, :])
        lower = lower + dotf(dpt[p, 3 * LANES : 4 * LANES, :], lanes_of(dout, r))
    grads[:, 0 : 3 * LANES] = upper.T.astype(BF)
    grads[:, 3 * LANES : 4 * LANES] = lower.T.astype(BF)
    band = grads.shape[0] // n

    def grad_copy(src, dst, peer):
        return remote(src, dst, g_send, g_recv, "seq", peer)

    def grads_out(k, _):
        peer = lax.rem(seq + k, n)
        grad_copy(grads.at[rows_of(peer, band)], got_g.at[seq], peer).start()
        return 0

    lax.fori_loop(1, n, grads_out, 0)
    got_g[seq] = grads[rows_of(seq, band), :]
    hand_on(1)
    scale = 1.0 / (m * LANES)

    def finish(p):
        for c in hops(p, 2, 3, 4, 5):
            c.wait()
        for i, to in enumerate((right, left, opposite)):
            stat_copy(p, i, to).wait()
        st = (stats[p] + got_s[p, 0] + got_s[p, 1] + got_s[p, 2]) * scale
        for b in range(PBLK):
            r = pl.ds(p * PATCH + b * BLK, BLK)
            mean_grad = lane_copy(st[2 * b : 2 * b + 1])
            mean_cross = lane_copy(st[2 * b + 1 : 2 * b + 2])
            d_hidden = part[mp, r, :].astype(F32) + got_l[r, :].astype(F32) + got_r[r, :].astype(F32)
            d_points[r, :] = dout[mp, r, :].astype(F32) + invb[r, :] * (
                d_hidden - mean_grad - d_points[r, :] * mean_cross
            )

    finish(0)
    others = got_g.at[pl.ds(0, n - 1)]
    grad_copy(others, others, seq).wait()
    total = jnp.zeros((band, grads.shape[1]), F32)
    for k in range(n):
        total = total + got_g[k].astype(F32)
    for t in range(3):
        grad_qkv[t] = total[:, t * LANES : (t + 1) * LANES]
    grad_out[...] = total[:, 3 * LANES : 4 * LANES]
    finish(1)


def local(
    scan_points, send_order, arrive_order, qkv_weight, out_weight, voxel_grads, voxel_shard, voxel_point
):
    n, m = lax.axis_size("seq"), lax.axis_size("mp")
    rows = scan_points.shape[0]
    feats = m * LANES
    grp, cap = rows // n, 2 * voxel_grads.shape[0] // n
    blocks, npatch, band = rows // BLK, rows // PATCH, feats // n
    vmem, hbm = pl.BlockSpec(memory_space=pltpu.VMEM), pl.BlockSpec(memory_space=pl.ANY)
    dma = pltpu.SemaphoreType.DMA
    col = pltpu.VMEM((rows, LANES), BF)
    per_patch = pltpu.VMEM((npatch, LANES, PATCH), BF)
    half_f = pltpu.VMEM((PATCH, QH), F32)
    half_b = pltpu.VMEM((PATCH, QH), BF)
    masked = pltpu.VMEM((2 * LANES, QH), BF)
    coded = pltpu.VMEM((n, 16, cap), BF)
    full = pltpu.VMEM((m, rows, LANES), BF)
    hop_buf = pltpu.VMEM((npatch, PATCH // 2, LANES), BF)
    d_points, grad_qkv, grad_out = (
        pl.pallas_call(
            layer_kernel,
            out_shape=[
                jax.ShapeDtypeStruct((rows, LANES), F32),
                jax.ShapeDtypeStruct((3, band, LANES), F32),
                jax.ShapeDtypeStruct((band, LANES), F32),
            ],
            in_specs=[hbm, hbm] + [vmem] * 6,
            out_specs=[vmem] * 3,
            scratch_shapes=[
                col, col, col, pltpu.VMEM((n * cap, LANES), BF), coded,
                col, pltpu.VMEM((n * cap, LANES), BF), coded, pltpu.VMEM((blocks, BLK), jnp.int32), pltpu.VMEM((n, cap), F32),
                full, full, pltpu.VMEM((rows, feats), BF), col, col,
                pltpu.VMEM((npatch, 2 * LANES, PATCH), BF),
                per_patch, per_patch, per_patch, pltpu.VMEM((LANES, PATCH), BF),
                pltpu.VMEM((npatch, 4 * LANES, PATCH), BF),
                masked, masked, half_f, half_f,
                pltpu.VMEM((npatch * HEADS, PATCH, PATCH), BF),
                half_b, half_b,
                pltpu.VMEM((2, 1, QH), F32),
                pltpu.VMEM((npatch * HEADS, 1, PATCH), F32), pltpu.VMEM((2, QH, PATCH), BF), pltpu.VMEM((2, QH, PATCH), BF),
                pltpu.VMEM((feats, 4 * LANES), BF),
                pltpu.VMEM((npatch, 2 * PBLK, BLK), F32),
                pltpu.VMEM((rows, LANES), F32),
                hop_buf, hop_buf,
                pltpu.VMEM((npatch, m - 1, 2 * PBLK, BLK), F32),
                pltpu.VMEM((n, band, 4 * LANES), BF),
                dma((2,)), dma((3,)), dma((3,)), dma((2,)), dma((2, m, blocks)),
                dma((npatch, 6)), dma((npatch, 6)), dma((npatch, m - 1)), dma((npatch, m - 1)), dma(()), dma(()),
            ],
            compiler_params=pltpu.CompilerParams(
                collective_id=0, has_side_effects=True, vmem_limit_bytes=67043328
            ),
            name="layer",
        )(
            scan_points, voxel_grads,
            send_order.reshape(-1, LANES), arrive_order.reshape(-1, LANES), voxel_point.reshape(-1, LANES),
            voxel_shard.reshape(1, -1), jnp.transpose(qkv_weight, (1, 0, 2)), out_weight,
        )
    )
    return d_points, jnp.transpose(grad_qkv, (1, 0, 2)), grad_out


def solution(mesh):
    in_specs = (
        P("seq", None), P("seq"), P("seq"), P(None, None, "mp"), P(None, "mp"),
        P("seq", None), P("seq", None), P("seq"),
    )
    out_specs = (P("seq", "mp"), P("seq", None, "mp"), P("seq", "mp"))
    return jax.shard_map(local, mesh=mesh, in_specs=in_specs, out_specs=out_specs, check_vma=False)
```

```python
import jax
import jax.numpy as jnp
from jax import lax
from jax.experimental import pallas as pl
from jax.experimental.pallas import tpu as pltpu
from jax.sharding import PartitionSpec as P

HD = 16
PATCH = 1024
LANES = 128
BLK = 256
HEADS = LANES // HD
PBLK = PATCH // BLK
QH = 512
CH = 256
EPSILON = 1e-05
LOG2E = 1.4426950408889634
BF = jnp.bfloat16
F32 = jnp.float32
MESH = pl.DeviceIdType.MESH


def dotf(a, b):
    return jnp.dot(a, b, preferred_element_type=F32)


def dot_nt(a, b):
    return lax.dot_general(a, b, (((1,), (1,)), ((), ())), preferred_element_type=F32)


def iota(shape, axis):
    return lax.broadcasted_iota(jnp.int32, shape, axis)


def as_mask(cond):
    return jnp.where(cond, 1.0, 0.0).astype(BF)


def small_iota(shape, axis):
    return iota(shape, axis).astype(F32).astype(BF)


def lane_copy(row):
    return jnp.broadcast_to(row.astype(F32), (LANES, BLK)).T


def block_row(ref, b):
    per = BLK // LANES
    return jnp.concatenate([ref[pl.ds(b * per + u, 1), :] for u in range(per)], axis=1)


def select_rows(order_row, count):
    want = lane_copy(order_row)
    high = jnp.floor(want * (1.0 / LANES))
    low = (want - high * LANES).astype(BF)
    high = high.astype(BF)
    zero = jnp.zeros((BLK, LANES), BF)
    here = jnp.where(low == small_iota((BLK, LANES), 1), jnp.ones((BLK, LANES), BF), zero)
    return jnp.concatenate([jnp.where(high == c, here, zero) for c in range(count // LANES)], axis=1)


def hits(position, b):
    shape = (BLK, position.shape[1])
    near = jnp.clip(position.astype(F32) - (b * BLK).astype(F32), -1.0, float(BLK)).astype(BF)
    return jnp.where(small_iota(shape, 0) == near, jnp.ones(shape, BF), jnp.zeros(shape, BF))


def lanes_of(ref, r):
    return jnp.concatenate([ref[j, r, :] for j in range(ref.shape[0])], axis=1)


def rows_of(block, size):
    return pl.ds(pl.multiple_of(block * size, size), size)


def remote(src, dst, send_sem, recv_sem, axis, to):
    return pltpu.make_async_remote_copy(
        src_ref=src, dst_ref=dst, send_sem=send_sem, recv_sem=recv_sem,
        device_id={axis: to}, device_id_type=MESH,
    )


def layer_kernel(
    scan, voxels, send_order, arrive_order, point, shard, w, wo,
    d_high, d_low, grad_qkv, grad_out,
    normq, x, v, sendp, sendv, sendi, gotp, gotv, goti, place, at_all,
    pts, dout, hid, kn, vn, qhl, qt, kt, vt, dat, dpt, qm0, qm1, s0, s1, e_all, ds0, ds1, top, linv, dst, est,
    grads, stats, invb, rel_l, rel_r, got_s, got_g,
    in_sem, send_sem, recv_sem, ring_send, ring_recv, p_send, p_recv, s_send, s_recv, g_send, g_recv,
):
    seq, mp = lax.axis_index("seq"), lax.axis_index("mp")
    n, m = lax.axis_size("seq"), lax.axis_size("mp")
    rows = x.shape[0]
    npatch = rows // PATCH
    grp = rows // n
    cap = gotv.shape[0] // n
    blocks = rows // BLK
    right, left, opposite = lax.rem(mp + 1, m), lax.rem(mp + m - 1, m), lax.rem(mp + 2, m)
    part, got_l, got_r = pts, x, v

    mine = pl.ds(pl.multiple_of(mp * LANES, LANES), LANES)
    in_x = pltpu.make_async_copy(scan.at[:, mine], x, in_sem.at[0])
    in_v = pltpu.make_async_copy(voxels.at[:, mine], v, in_sem.at[1])
    in_x.start()
    in_v.start()
    barrier = pltpu.get_barrier_semaphore()
    for k in range(1, n):
        pl.semaphore_signal(barrier, inc=1, device_id={"seq": lax.rem(seq + k, n)}, device_id_type=MESH)
    for to in (right, left, opposite):
        pl.semaphore_signal(barrier, inc=1, device_id={"mp": to}, device_id_type=MESH)

    def send(src, dst, kind, peer):
        return remote(src, dst, send_sem.at[kind], recv_sem.at[kind], "seq", peer)

    tri = as_mask(iota((BLK, BLK), 0) < iota((BLK, BLK), 1))
    carry = jnp.zeros((n, 1), F32)
    codes = jnp.zeros((3 * n, cap), F32)
    for b in range(blocks):
        target = shard[:, b * BLK : (b + 1) * BLK]
        hot = jnp.where(iota((n, BLK), 0) == target, 1.0, 0.0)
        before = dotf(hot.astype(BF), tri) + carry
        rank = jnp.sum(before * hot, axis=0, keepdims=True)
        carry = carry + jnp.sum(hot, axis=1, keepdims=True)
        place[b : b + 1, :] = target * cap + rank.astype(jnp.int32)
        where_to = block_row(point, b)
        high = (where_to // 64).astype(F32)
        low = (where_to % 64).astype(F32)
        slot = as_mask(iota((cap, BLK), 0) == rank.astype(jnp.int32))
        coded = jnp.concatenate([hot * high, hot * low, hot], axis=0).astype(BF)
        codes = codes + dot_nt(coded, slot)
    sub16 = iota((16, cap), 0)
    for t in range(n):
        a, b, c = codes[t : t + 1], codes[n + t : n + t + 1], codes[2 * n + t : 2 * n + t + 1]
        sendi[t] = jnp.where(sub16 == 0, a, jnp.where(sub16 == 1, b, c)).astype(BF)
    in_x.wait()
    per = BLK // grp

    def ordered(i):
        return lax.rem(i + seq // per, blocks)

    def points_pick(i, _):
        b = ordered(i)
        hot = select_rows(block_row(send_order, b), rows)
        sendp[rows_of(b, BLK), :] = dotf(hot, x[...]).astype(BF)
        return 0

    def points_send(i, _):
        for u in range(per):
            peer = ordered(i) * per + u

            @pl.when(peer != seq)
            def _():
                send(sendp.at[rows_of(peer, grp)], gotp.at[rows_of(seq, grp)], 0, peer).start()

        return 0

    def points_out(i, _):
        points_pick(i, 0)
        points_send(i, 0)
        return 0

    lax.fori_loop(0, blocks // 2, points_pick, 0)
    pl.semaphore_wait(barrier, n + m - 2)
    lax.fori_loop(0, blocks // 2, points_send, 0)
    lax.fori_loop(blocks // 2, blocks, points_out, 0)
    gotp[rows_of(seq, grp), :] = sendp[rows_of(seq, grp), :]

    in_v.wait()
    per_v = BLK // cap
    vblocks = n // per_v

    def voxels_out(i, _):
        b = lax.rem(i + seq // per_v, vblocks)
        hot = jnp.concatenate([hits(place[c : c + 1, :], b) for c in range(blocks)], axis=1)
        sendv[rows_of(b, BLK), :] = dotf(hot, v[...]).astype(BF)
        for u in range(per_v):
            peer = b * per_v + u

            @pl.when(peer != seq)
            def _():
                send(sendv.at[rows_of(peer, cap)], gotv.at[rows_of(seq, cap)], 1, peer).start()
                send(sendi.at[peer], goti.at[seq], 2, peer).start()

        return 0

    lax.fori_loop(0, vblocks, voxels_out, 0)
    gotv[rows_of(seq, cap), :] = sendv[rows_of(seq, cap), :]
    goti[seq] = sendi[seq]

    def wait_all(kind, ref, size):
        other = ref.at[pl.ds(0, size)]
        send(other, other, kind, seq).wait_recv()
        send(other, other, kind, seq).wait_send()

    def ring(full, kind, owner, b, to):
        at = full.at[owner, rows_of(b, BLK)]
        return remote(at, at, ring_send.at[kind], ring_recv.at[kind, owner, b], "mp", to)

    def goes_right(b):
        return lax.rem(b, PBLK) < PBLK // 2

    def relay(full, kind, b):
        @pl.when(goes_right(b))
        def _():
            ring(full, kind, left, b, right).wait_recv()
            ring(full, kind, left, b, right).start()

        @pl.when(jnp.logical_not(goes_right(b)))
        def _():
            ring(full, kind, right, b, left).wait_recv()
            ring(full, kind, right, b, left).start()

    def arrived(full, kind, b):
        @pl.when(goes_right(b))
        def _():
            ring(full, kind, right, b, left).wait_recv()

        @pl.when(jnp.logical_not(goes_right(b)))
        def _():
            ring(full, kind, left, b, right).wait_recv()

        ring(full, kind, opposite, b, right).wait_recv()

    def ring_sent(full, kind):
        for _ in range(3):
            remote(full.at[0], full.at[0], ring_send.at[kind], ring_recv.at[kind, 0, 0], "mp", right).wait_send()

    wait_all(0, gotp, (n - 1) * grp)

    def points_in(b, _):
        hot = select_rows(block_row(arrive_order, b), rows)
        pts[mp, rows_of(b, BLK), :] = dotf(hot, gotp[...]).astype(BF)
        ring(pts, 0, mp, b, right).start()
        ring(pts, 0, mp, b, left).start()
        return 0

    lax.fori_loop(0, blocks, points_in, 0)
    wait_all(1, gotv, (n - 1) * cap)
    wait_all(2, goti, n - 1)
    for t in range(n):
        code = goti[t].astype(F32)
        at_all[t : t + 1, :] = jnp.where(code[2:3, :] > 0.5, code[0:1, :] * 64.0 + code[1:2, :], -1.0)

    def voxels_in(b, _):
        relay(pts, 0, b)
        hot = jnp.concatenate([hits(at_all[t : t + 1, :], b) for t in range(n)], axis=1)
        dout[mp, rows_of(b, BLK), :] = dotf(hot, gotv[...]).astype(BF)
        ring(dout, 1, mp, b, right).start()
        ring(dout, 1, mp, b, left).start()
        return 0

    lax.fori_loop(0, blocks, voxels_in, 0)

    wcat = jnp.concatenate([w[t] for t in range(3)], axis=1)
    ones_lane = as_mask(iota((PATCH, LANES), 1) < 3)
    halves = ((qm0, s0, ds0), (qm1, s1, ds1))

    def normalise(p):
        for b in range(PBLK):
            r = rows_of(p * PBLK + b, BLK)
            c = pl.ds(b * BLK, BLK)
            xb = lanes_of(pts, r).astype(F32)
            xb = xb - jnp.mean(xb, axis=1, keepdims=True)
            inv = lax.rsqrt(jnp.mean(xb * xb, axis=1, keepdims=True) + EPSILON)
            normed = xb * inv
            hidden = normed.astype(BF)
            hid[r, :] = hidden
            invb[r, :] = jnp.broadcast_to(inv, (BLK, LANES))
            own = normed[:, 0:LANES]
            for j in range(1, m):
                own = jnp.where(mp == j, normed[:, j * LANES : (j + 1) * LANES], own)
            normq[r, :] = own
            proj = dotf(hidden, wcat)
            q, k, val = (proj[:, t * LANES : (t + 1) * LANES].astype(BF) for t in range(3))
            kn[r, :] = k
            vn[r, :] = val
            qf = q.astype(F32).T
            qt[p, :, c] = qf.astype(BF)
            qs = qf * (0.25 * LOG2E)
            high = qs.astype(BF)
            qhl[p, 0:LANES, c] = high
            qhl[p, LANES : 2 * LANES, c] = (qs - high.astype(F32)).astype(BF)
            kt[p, :, c] = k.astype(F32).T.astype(BF)
            vt[p, :, c] = val.astype(F32).T.astype(BF)

    def head_rows(h, base=0):
        return pl.ds(pl.multiple_of(base * LANES + h * HD, HD), HD)

    def scores(p, h, half):
        qm, s = halves[half][:2]
        c = pl.ds(half * QH, QH)
        rmask = (iota((LANES, QH), 0) // HD) == h
        zero = jnp.zeros((LANES, QH), BF)
        qm[0:LANES, :] = jnp.where(rmask, qhl[p, 0:LANES, c], zero)
        qm[LANES : 2 * LANES, :] = jnp.where(rmask, qhl[p, LANES : 2 * LANES, c], zero)
        k = kn[rows_of(p, PATCH), :]
        val = dotf(jnp.concatenate([k, k], axis=1), qm[...])
        s[...] = val
        top[half] = jnp.max(val, axis=0, keepdims=True)

    def forward(p, h, half):
        s = halves[half][1]
        c = pl.ds(half * QH, QH)
        e = jnp.exp2(s[...] - top[half]).astype(BF)
        e_all[p * HEADS + h, :, c] = e
        vt1 = jnp.concatenate([vt[p, head_rows(h), :], jnp.ones((HD, PATCH), BF)], axis=0)
        av = dotf(vt1, e)
        inv = 1.0 / av[HD : HD + 1, :]
        linv[p * HEADS + h, :, c] = inv
        dpt[p, head_rows(h, 3), c] = (av[0:HD, :] * inv).astype(BF)

    def forward_patch(p, _):
        def ready(b, _):
            arrived(pts, 0, p * PBLK + b)
            return 0

        lax.fori_loop(0, PBLK, ready, 0)
        normalise(p)
        scores(p, 0, 0)

        def step(i, _):
            h = i // 2

            b = (p * 2 * HEADS + i - HEADS) // 2

            @pl.when(jnp.logical_and(lax.rem(i, 2) == 0, jnp.logical_and(b >= 0, b < blocks)))
            def _():
                relay(dout, 1, b)

            @pl.when(lax.rem(i, 2) == 0)
            def _():
                scores(p, h, 1)
                forward(p, h, 0)

            @pl.when(jnp.logical_and(lax.rem(i, 2) == 1, h < HEADS - 1))
            def _():
                scores(p, h + 1, 0)
                forward(p, h, 1)

            @pl.when(i == 2 * HEADS - 1)
            def _():
                forward(p, HEADS - 1, 1)

            return 0

        lax.fori_loop(0, 2 * HEADS, step, 0)
        return 0

    lax.fori_loop(0, npatch, forward_patch, 0)

    def hop(p, sem, src, dst, to):
        return remote(src, dst, p_send.at[p, sem], p_recv.at[p, sem], "mp", to)

    def hops(p, *which):
        low, high = rows_of(2 * p, PATCH // 2), rows_of(2 * p + 1, PATCH // 2)
        ends = (
            (part.at[opposite, low], rel_l.at[p], right),
            (part.at[opposite, high], rel_r.at[p], left),
            (part.at[right, high], got_l.at[high], right),
            (part.at[left, low], got_r.at[low], left),
            (rel_l.at[p], got_l.at[low], right),
            (rel_r.at[p], got_r.at[high], left),
        )
        return [hop(p, w, *ends[w]) for w in which]

    def hand_on(p):
        low, high = rows_of(2 * p, PATCH // 2), rows_of(2 * p + 1, PATCH // 2)
        in_l, in_r, out_l, out_r = hops(p, 0, 1, 4, 5)
        in_l.wait()
        rel_l[p] = (rel_l[p].astype(F32) + part[right, low, :].astype(F32)).astype(BF)
        out_l.start()
        in_r.wait()
        rel_r[p] = (rel_r[p].astype(F32) + part[left, high, :].astype(F32)).astype(BF)
        out_r.start()

    def backward(p, h, half):
        ds_ref = halves[half][2]
        i = p * HEADS + h
        c = pl.ds(half * QH, QH)
        scaled = (dat[head_rows(h), c].astype(F32) * linv[i, :, c]).astype(BF)
        da = scaled.astype(F32)
        delta = jnp.sum(da * dpt[p, head_rows(h, 3), c].astype(F32), axis=0, keepdims=True)
        d1 = delta.astype(BF).astype(F32)
        d2 = (delta - d1).astype(BF).astype(F32)
        d3 = delta - d1 - d2
        sub = iota((LANES, QH), 0)
        tile = jnp.where(sub // HD == h, jnp.concatenate([da] * HEADS, axis=0), 0.0)
        tail = jnp.where(sub == 0, -d1, jnp.where(sub == 1, -d2, jnp.where(sub == 2, -d3, 0.0)))
        vv = jnp.concatenate([vn[rows_of(p, PATCH), :], ones_lane], axis=1)
        dp = dotf(vv, jnp.concatenate([tile, tail], axis=0).astype(BF))
        ds = e_all[i, :, c] * dp.astype(BF)
        ds_ref[...] = ds
        dpt[p, head_rows(h), c] = (dotf(kt[p, head_rows(h), :], ds) * 0.25).astype(BF)
        for u in range(PATCH // CH):
            r = pl.ds(u * CH, CH)
            dst[half, :, r] = ds_ref[r, :].T
        for u in range(PATCH // CH):
            r = pl.ds(u * CH, CH)
            est[half, :, r] = e_all[i, r, c].T
        return dotf(qt[p, head_rows(h), c], dst[half]), dotf(scaled, est[half])

    def dout_in(b, _):
        arrived(dout, 1, b)
        return 0

    lax.fori_loop(0, blocks, dout_in, 0)
    ring_sent(pts, 0)
    ring_sent(dout, 1)

    def stat_copy(p, i, to):
        return remote(stats.at[p], got_s.at[p, i], s_send.at[p, i], s_recv.at[p, i], "mp", to)

    def backward_patch(p, _):
        for b in range(PBLK):
            da = dotf(lanes_of(dout, rows_of(p * PBLK + b, BLK)), wo[...]).astype(BF)
            dat[:, b * BLK : (b + 1) * BLK] = da.astype(F32).T.astype(BF)

        def step(h, _):
            @pl.when(jnp.logical_and(p == 1, h == HEADS // 2))
            def _():
                hand_on(0)

            dk0, dv0 = backward(p, h, 0)
            dk1, dv1 = backward(p, h, 1)
            dpt[p, head_rows(h, 1), :] = ((dk0 + dk1) * 0.25).astype(BF)
            dpt[p, head_rows(h, 2), :] = (dv0 + dv1).astype(BF)
            return 0

        lax.fori_loop(0, HEADS, step, 0)
        for b in range(PBLK):
            r = rows_of(p * PBLK + b, BLK)
            dproj = dpt[p, 0 : 3 * LANES, pl.ds(b * BLK, BLK)].astype(F32).T.astype(BF)
            pd = dot_nt(dproj, wcat).astype(BF)
            for j in range(m):
                part[j, r, :] = pd[:, j * LANES : (j + 1) * LANES]
            if b % 2 == 1:
                for c in hops(p, *((0,), (1, 3, 2))[b // 2]):
                    c.start()
            gram = dot_nt(pd, hid[r, :])
            cross = jnp.sum(jnp.where(iota((BLK, BLK), 0) == iota((BLK, BLK), 1), gram, 0.0), axis=0, keepdims=True)
            total = dot_nt(jnp.ones((8, pd.shape[1]), BF), pd)
            stats[p, 2 * b : 2 * b + 1, :] = total[0:1]
            stats[p, 2 * b + 1 : 2 * b + 2, :] = cross
        for i, to in enumerate((right, left, opposite)):
            stat_copy(p, i, to).start()
        return 0

    lax.fori_loop(0, npatch, backward_patch, 0)

    upper, lower = 0.0, 0.0
    for p in range(npatch):
        r = pl.ds(p * PATCH, PATCH)
        upper = upper + dotf(dpt[p, 0 : 3 * LANES, :], hid[r, :])
        lower = lower + dotf(dpt[p, 3 * LANES : 4 * LANES, :], lanes_of(dout, r))
    grads[:, 0 : 3 * LANES] = upper.T.astype(BF)
    grads[:, 3 * LANES : 4 * LANES] = lower.T.astype(BF)
    band = grads.shape[0] // n

    def grad_copy(src, dst, peer):
        return remote(src, dst, g_send, g_recv, "seq", peer)

    def grads_out(k, _):
        peer = lax.rem(seq + k, n)
        grad_copy(grads.at[rows_of(peer, band)], got_g.at[seq], peer).start()
        return 0

    lax.fori_loop(1, n, grads_out, 0)
    got_g[seq] = grads[rows_of(seq, band), :]
    hand_on(1)
    scale = 1.0 / (m * LANES)

    def finish(p):
        for c in hops(p, 2, 3, 4, 5):
            c.wait()
        for i, to in enumerate((right, left, opposite)):
            stat_copy(p, i, to).wait()
        st = (stats[p] + got_s[p, 0] + got_s[p, 1] + got_s[p, 2]) * scale
        for b in range(PBLK):
            r = pl.ds(p * PATCH + b * BLK, BLK)
            mean_grad = lane_copy(st[2 * b : 2 * b + 1])
            mean_cross = lane_copy(st[2 * b + 1 : 2 * b + 2])
            d_hidden = part[mp, r, :].astype(F32) + got_l[r, :].astype(F32) + got_r[r, :].astype(F32)
            grad = dout[mp, r, :].astype(F32) + invb[r, :] * (
                d_hidden - mean_grad - normq[r, :] * mean_cross
            )
            high = grad.astype(BF)
            d_high[r, :] = high
            d_low[r, :] = (grad - high.astype(F32)).astype(BF)

    finish(0)
    others = got_g.at[pl.ds(0, n - 1)]
    grad_copy(others, others, seq).wait()
    total = jnp.zeros((band, grads.shape[1]), F32)
    for k in range(n):
        total = total + got_g[k].astype(F32)
    for t in range(3):
        grad_qkv[t] = total[:, t * LANES : (t + 1) * LANES]
    grad_out[...] = total[:, 3 * LANES : 4 * LANES]
    finish(1)


def local(
    scan_points, send_order, arrive_order, qkv_weight, out_weight, voxel_grads, voxel_shard, voxel_point
):
    n, m = lax.axis_size("seq"), lax.axis_size("mp")
    rows = scan_points.shape[0]
    feats = m * LANES
    grp, cap = rows // n, 2 * voxel_grads.shape[0] // n
    blocks, npatch, band = rows // BLK, rows // PATCH, feats // n
    vmem, hbm = pl.BlockSpec(memory_space=pltpu.VMEM), pl.BlockSpec(memory_space=pl.ANY)
    dma = pltpu.SemaphoreType.DMA
    col = pltpu.VMEM((rows, LANES), BF)
    per_patch = pltpu.VMEM((npatch, LANES, PATCH), BF)
    half_f = pltpu.VMEM((PATCH, QH), F32)
    half_b = pltpu.VMEM((PATCH, QH), BF)
    masked = pltpu.VMEM((2 * LANES, QH), BF)
    coded = pltpu.VMEM((n, 16, cap), BF)
    full = pltpu.VMEM((m, rows, LANES), BF)
    hop_buf = pltpu.VMEM((npatch, PATCH // 2, LANES), BF)
    d_high, d_low, grad_qkv, grad_out = (
        pl.pallas_call(
            layer_kernel,
            out_shape=[
                jax.ShapeDtypeStruct((rows, LANES), BF),
                jax.ShapeDtypeStruct((rows, LANES), BF),
                jax.ShapeDtypeStruct((3, band, LANES), F32),
                jax.ShapeDtypeStruct((band, LANES), F32),
            ],
            in_specs=[hbm, hbm] + [vmem] * 6,
            out_specs=[vmem] * 4,
            scratch_shapes=[
                pltpu.VMEM((rows, LANES), F32), col, col, col, pltpu.VMEM((n * cap, LANES), BF), coded,
                col, pltpu.VMEM((n * cap, LANES), BF), coded, pltpu.VMEM((blocks, BLK), jnp.int32), pltpu.VMEM((n, cap), F32),
                full, full, pltpu.VMEM((rows, feats), BF), col, col,
                pltpu.VMEM((npatch, 2 * LANES, PATCH), BF),
                per_patch, per_patch, per_patch, pltpu.VMEM((LANES, PATCH), BF),
                pltpu.VMEM((npatch, 4 * LANES, PATCH), BF),
                masked, masked, half_f, half_f,
                pltpu.VMEM((npatch * HEADS, PATCH, PATCH), BF),
                half_b, half_b,
                pltpu.VMEM((2, 1, QH), F32),
                pltpu.VMEM((npatch * HEADS, 1, PATCH), F32), pltpu.VMEM((2, QH, PATCH), BF), pltpu.VMEM((2, QH, PATCH), BF),
                pltpu.VMEM((feats, 4 * LANES), BF),
                pltpu.VMEM((npatch, 2 * PBLK, BLK), F32),
                pltpu.VMEM((rows, LANES), F32),
                hop_buf, hop_buf,
                pltpu.VMEM((npatch, m - 1, 2 * PBLK, BLK), F32),
                pltpu.VMEM((n, band, 4 * LANES), BF),
                dma((2,)), dma((3,)), dma((3,)), dma((2,)), dma((2, m, blocks)),
                dma((npatch, 6)), dma((npatch, 6)), dma((npatch, m - 1)), dma((npatch, m - 1)), dma(()), dma(()),
            ],
            compiler_params=pltpu.CompilerParams(
                collective_id=0, has_side_effects=True, vmem_limit_bytes=67043328
            ),
            name="layer",
        )(
            scan_points, voxel_grads,
            send_order.reshape(-1, LANES), arrive_order.reshape(-1, LANES), voxel_point.reshape(-1, LANES),
            voxel_shard.reshape(1, -1), jnp.transpose(qkv_weight, (1, 0, 2)), out_weight,
        )
    )
    return d_high.astype(F32) + d_low.astype(F32), jnp.transpose(grad_qkv, (1, 0, 2)), grad_out


def solution(mesh):
    in_specs = (
        P("seq", None), P("seq"), P("seq"), P(None, None, "mp"), P(None, "mp"),
        P("seq", None), P("seq", None), P("seq"),
    )
    out_specs = (P("seq", "mp"), P("seq", None, "mp"), P("seq", "mp"))
    return jax.shard_map(local, mesh=mesh, in_specs=in_specs, out_specs=out_specs, check_vma=False)
```

```python
import jax
import jax.numpy as jnp
from jax import lax
from jax.experimental import pallas as pl
from jax.experimental.pallas import tpu as pltpu
from jax.sharding import PartitionSpec as P

HD = 16
PATCH = 1024
LANES = 128
BLK = 256
HEADS = LANES // HD
PBLK = PATCH // BLK
QH = 512
CH = 256
EPSILON = 1e-05
LOG2E = 1.4426950408889634
BF = jnp.bfloat16
F32 = jnp.float32
MESH = pl.DeviceIdType.MESH


def dotf(a, b):
    return jnp.dot(a, b, preferred_element_type=F32)


def dot_nt(a, b):
    return lax.dot_general(a, b, (((1,), (1,)), ((), ())), preferred_element_type=F32)


def iota(shape, axis):
    return lax.broadcasted_iota(jnp.int32, shape, axis)


def as_mask(cond):
    return jnp.where(cond, 1.0, 0.0).astype(BF)


def small_iota(shape, axis):
    return iota(shape, axis).astype(F32).astype(BF)


def lane_copy(row):
    return jnp.broadcast_to(row.astype(F32), (LANES, BLK)).T


def block_row(ref, b):
    per = BLK // LANES
    return jnp.concatenate([ref[pl.ds(b * per + u, 1), :] for u in range(per)], axis=1)


def select_rows(order_row, count):
    want = lane_copy(order_row)
    high = jnp.floor(want * (1.0 / LANES))
    low = (want - high * LANES).astype(BF)
    high = high.astype(BF)
    zero = jnp.zeros((BLK, LANES), BF)
    here = jnp.where(low == small_iota((BLK, LANES), 1), jnp.ones((BLK, LANES), BF), zero)
    return jnp.concatenate([jnp.where(high == c, here, zero) for c in range(count // LANES)], axis=1)


def hits(position, b):
    shape = (BLK, position.shape[1])
    near = jnp.clip(position.astype(F32) - (b * BLK).astype(F32), -1.0, float(BLK)).astype(BF)
    return jnp.where(small_iota(shape, 0) == near, jnp.ones(shape, BF), jnp.zeros(shape, BF))


def lanes_of(ref, r):
    return jnp.concatenate([ref[j, r, :] for j in range(ref.shape[0])], axis=1)


def rows_of(block, size):
    return pl.ds(pl.multiple_of(block * size, size), size)


def remote(src, dst, send_sem, recv_sem, axis, to):
    return pltpu.make_async_remote_copy(
        src_ref=src, dst_ref=dst, send_sem=send_sem, recv_sem=recv_sem,
        device_id={axis: to}, device_id_type=MESH,
    )


def layer_kernel(
    scan, voxels, send_order, arrive_order, point, shard, w, wo,
    d_high, d_low, grad_qkv, grad_out,
    normq, x, v, sendp, sendv, sendi, gotp, gotv, goti, place, at_all,
    pts, dout, hid, kn, vn, qhl, qt, kt, vt, dat, dpt, qm0, qm1, s0, s1, e_all, ds0, ds1, top, linv, dst, est,
    grads, stats, invb, rel_l, rel_r, got_s, got_g,
    in_sem, send_sem, recv_sem, ring_send, ring_recv, p_send, p_recv, s_send, s_recv, g_send, g_recv,
):
    seq, mp = lax.axis_index("seq"), lax.axis_index("mp")
    n, m = lax.axis_size("seq"), lax.axis_size("mp")
    rows = x.shape[0]
    npatch = rows // PATCH
    grp = rows // n
    cap = gotv.shape[0] // n
    blocks = rows // BLK
    right, left, opposite = lax.rem(mp + 1, m), lax.rem(mp + m - 1, m), lax.rem(mp + 2, m)
    part, got_l, got_r = pts, x, v

    mine = pl.ds(pl.multiple_of(mp * LANES, LANES), LANES)
    in_x = pltpu.make_async_copy(scan.at[:, mine], x, in_sem.at[0])
    in_v = pltpu.make_async_copy(voxels.at[:, mine], v, in_sem.at[1])
    in_x.start()
    in_v.start()
    barrier = pltpu.get_barrier_semaphore()
    for k in range(1, n):
        pl.semaphore_signal(barrier, inc=1, device_id={"seq": lax.rem(seq + k, n)}, device_id_type=MESH)
    for to in (right, left, opposite):
        pl.semaphore_signal(barrier, inc=1, device_id={"mp": to}, device_id_type=MESH)

    def send(src, dst, kind, peer):
        return remote(src, dst, send_sem.at[kind], recv_sem.at[kind], "seq", peer)

    tri = as_mask(iota((BLK, BLK), 0) < iota((BLK, BLK), 1))
    carry = jnp.zeros((n, 1), F32)
    codes = jnp.zeros((3 * n, cap), F32)
    for b in range(blocks):
        target = shard[:, b * BLK : (b + 1) * BLK]
        hot = jnp.where(iota((n, BLK), 0) == target, 1.0, 0.0)
        before = dotf(hot.astype(BF), tri) + carry
        rank = jnp.sum(before * hot, axis=0, keepdims=True)
        carry = carry + jnp.sum(hot, axis=1, keepdims=True)
        place[b : b + 1, :] = target * cap + rank.astype(jnp.int32)
        where_to = block_row(point, b)
        high = (where_to // 64).astype(F32)
        low = (where_to % 64).astype(F32)
        slot = as_mask(iota((cap, BLK), 0) == rank.astype(jnp.int32))
        coded = jnp.concatenate([hot * high, hot * low, hot], axis=0).astype(BF)
        codes = codes + dot_nt(coded, slot)
    sub16 = iota((16, cap), 0)
    for t in range(n):
        a, b, c = codes[t : t + 1], codes[n + t : n + t + 1], codes[2 * n + t : 2 * n + t + 1]
        sendi[t] = jnp.where(sub16 == 0, a, jnp.where(sub16 == 1, b, c)).astype(BF)
    in_x.wait()
    per = BLK // grp

    def ordered(i):
        return lax.rem(i + seq // per, blocks)

    def points_pick(i, _):
        b = ordered(i)
        hot = select_rows(block_row(send_order, b), rows)
        sendp[rows_of(b, BLK), :] = dotf(hot, x[...]).astype(BF)
        return 0

    def points_send(i, _):
        for u in range(per):
            peer = ordered(i) * per + u

            @pl.when(peer != seq)
            def _():
                send(sendp.at[rows_of(peer, grp)], gotp.at[rows_of(seq, grp)], 0, peer).start()

        return 0

    def points_out(i, _):
        points_pick(i, 0)
        points_send(i, 0)
        return 0

    lax.fori_loop(0, blocks // 2, points_pick, 0)
    pl.semaphore_wait(barrier, n + m - 2)
    lax.fori_loop(0, blocks // 2, points_send, 0)
    lax.fori_loop(blocks // 2, blocks, points_out, 0)
    gotp[rows_of(seq, grp), :] = sendp[rows_of(seq, grp), :]

    in_v.wait()
    per_v = BLK // cap
    vblocks = n // per_v

    def voxels_out(i, _):
        b = lax.rem(i + seq // per_v, vblocks)
        hot = jnp.concatenate([hits(place[c : c + 1, :], b) for c in range(blocks)], axis=1)
        sendv[rows_of(b, BLK), :] = dotf(hot, v[...]).astype(BF)
        for u in range(per_v):
            peer = b * per_v + u

            @pl.when(peer != seq)
            def _():
                send(sendv.at[rows_of(peer, cap)], gotv.at[rows_of(seq, cap)], 1, peer).start()
                send(sendi.at[peer], goti.at[seq], 2, peer).start()

        return 0

    lax.fori_loop(0, vblocks // 2, voxels_out, 0)

    def wait_all(kind, ref, size):
        other = ref.at[pl.ds(0, size)]
        send(other, other, kind, seq).wait_recv()
        send(other, other, kind, seq).wait_send()

    def ring(full, kind, owner, b, to):
        at = full.at[owner, rows_of(b, BLK)]
        return remote(at, at, ring_send.at[kind], ring_recv.at[kind, owner, b], "mp", to)

    def goes_right(b):
        return lax.rem(b, PBLK) < PBLK // 2

    def relay(full, kind, b):
        @pl.when(goes_right(b))
        def _():
            ring(full, kind, left, b, right).wait_recv()
            ring(full, kind, left, b, right).start()

        @pl.when(jnp.logical_not(goes_right(b)))
        def _():
            ring(full, kind, right, b, left).wait_recv()
            ring(full, kind, right, b, left).start()

    def arrived(full, kind, b):
        @pl.when(goes_right(b))
        def _():
            ring(full, kind, right, b, left).wait_recv()

        @pl.when(jnp.logical_not(goes_right(b)))
        def _():
            ring(full, kind, left, b, right).wait_recv()

        ring(full, kind, opposite, b, right).wait_recv()

    def ring_sent(full, kind):
        for _ in range(3):
            remote(full.at[0], full.at[0], ring_send.at[kind], ring_recv.at[kind, 0, 0], "mp", right).wait_send()

    wait_all(0, gotp, (n - 1) * grp)

    def points_in(b, _):
        hot = select_rows(block_row(arrive_order, b), rows)
        pts[mp, rows_of(b, BLK), :] = dotf(hot, gotp[...]).astype(BF)
        ring(pts, 0, mp, b, right).start()
        ring(pts, 0, mp, b, left).start()
        return 0

    lax.fori_loop(0, blocks, points_in, 0)
    lax.fori_loop(vblocks // 2, vblocks, voxels_out, 0)
    gotv[rows_of(seq, cap), :] = sendv[rows_of(seq, cap), :]
    goti[seq] = sendi[seq]
    wait_all(1, gotv, (n - 1) * cap)
    wait_all(2, goti, n - 1)
    for t in range(n):
        code = goti[t].astype(F32)
        at_all[t : t + 1, :] = jnp.where(code[2:3, :] > 0.5, code[0:1, :] * 64.0 + code[1:2, :], -1.0)

    def voxels_in(b, _):
        relay(pts, 0, b)
        hot = jnp.concatenate([hits(at_all[t : t + 1, :], b) for t in range(n)], axis=1)
        dout[mp, rows_of(b, BLK), :] = dotf(hot, gotv[...]).astype(BF)
        ring(dout, 1, mp, b, right).start()
        ring(dout, 1, mp, b, left).start()
        return 0

    lax.fori_loop(0, blocks, voxels_in, 0)

    wcat = jnp.concatenate([w[t] for t in range(3)], axis=1)
    ones_lane = as_mask(iota((PATCH, LANES), 1) < 3)
    halves = ((qm0, s0, ds0), (qm1, s1, ds1))

    def normalise(p):
        for b in range(PBLK):
            r = rows_of(p * PBLK + b, BLK)
            c = pl.ds(b * BLK, BLK)
            xb = lanes_of(pts, r).astype(F32)
            xb = xb - jnp.mean(xb, axis=1, keepdims=True)
            inv = lax.rsqrt(jnp.mean(xb * xb, axis=1, keepdims=True) + EPSILON)
            normed = xb * inv
            hidden = normed.astype(BF)
            hid[r, :] = hidden
            invb[r, :] = jnp.broadcast_to(inv, (BLK, LANES))
            own = normed[:, 0:LANES]
            for j in range(1, m):
                own = jnp.where(mp == j, normed[:, j * LANES : (j + 1) * LANES], own)
            normq[r, :] = own
            proj = dotf(hidden, wcat)
            q, k, val = (proj[:, t * LANES : (t + 1) * LANES].astype(BF) for t in range(3))
            kn[r, :] = k
            vn[r, :] = val
            qf = q.astype(F32).T
            qt[p, :, c] = qf.astype(BF)
            qs = qf * (0.25 * LOG2E)
            high = qs.astype(BF)
            qhl[p, 0:LANES, c] = high
            qhl[p, LANES : 2 * LANES, c] = (qs - high.astype(F32)).astype(BF)
            kt[p, :, c] = k.astype(F32).T.astype(BF)
            vt[p, :, c] = val.astype(F32).T.astype(BF)

    def head_rows(h, base=0):
        return pl.ds(pl.multiple_of(base * LANES + h * HD, HD), HD)

    def scores(p, h, half):
        qm, s = halves[half][:2]
        c = pl.ds(half * QH, QH)
        rmask = (iota((LANES, QH), 0) // HD) == h
        zero = jnp.zeros((LANES, QH), BF)
        qm[0:LANES, :] = jnp.where(rmask, qhl[p, 0:LANES, c], zero)
        qm[LANES : 2 * LANES, :] = jnp.where(rmask, qhl[p, LANES : 2 * LANES, c], zero)
        k = kn[rows_of(p, PATCH), :]
        val = dotf(jnp.concatenate([k, k], axis=1), qm[...])
        s[...] = val
        top[half] = jnp.max(val, axis=0, keepdims=True)

    def forward(p, h, half):
        s = halves[half][1]
        c = pl.ds(half * QH, QH)
        e = jnp.exp2(s[...] - top[half]).astype(BF)
        e_all[p * HEADS + h, :, c] = e
        vt1 = jnp.concatenate([vt[p, head_rows(h), :], jnp.ones((HD, PATCH), BF)], axis=0)
        av = dotf(vt1, e)
        inv = 1.0 / av[HD : HD + 1, :]
        linv[p * HEADS + h, :, c] = inv
        dpt[p, head_rows(h, 3), c] = (av[0:HD, :] * inv).astype(BF)

    def forward_patch(p, _):
        def ready(b, _):
            arrived(pts, 0, p * PBLK + b)
            return 0

        lax.fori_loop(0, PBLK, ready, 0)
        normalise(p)
        scores(p, 0, 0)

        def step(i, _):
            h = i // 2

            b = (p * 2 * HEADS + i - 6) // 2

            @pl.when(jnp.logical_and(lax.rem(i, 2) == 0, jnp.logical_and(b >= 0, b < blocks)))
            def _():
                relay(dout, 1, b)

            @pl.when(lax.rem(i, 2) == 0)
            def _():
                scores(p, h, 1)
                forward(p, h, 0)

            @pl.when(jnp.logical_and(lax.rem(i, 2) == 1, h < HEADS - 1))
            def _():
                scores(p, h + 1, 0)
                forward(p, h, 1)

            @pl.when(i == 2 * HEADS - 1)
            def _():
                forward(p, HEADS - 1, 1)

            return 0

        lax.fori_loop(0, 2 * HEADS, step, 0)
        return 0

    lax.fori_loop(0, npatch, forward_patch, 0)

    def hop(p, sem, src, dst, to):
        return remote(src, dst, p_send.at[p, sem], p_recv.at[p, sem], "mp", to)

    def hops(p, *which):
        low, high = rows_of(2 * p, PATCH // 2), rows_of(2 * p + 1, PATCH // 2)
        ends = (
            (part.at[opposite, low], rel_l.at[p], right),
            (part.at[opposite, high], rel_r.at[p], left),
            (part.at[right, high], got_l.at[high], right),
            (part.at[left, low], got_r.at[low], left),
            (rel_l.at[p], got_l.at[low], right),
            (rel_r.at[p], got_r.at[high], left),
        )
        return [hop(p, w, *ends[w]) for w in which]

    def hand_on(p):
        low, high = rows_of(2 * p, PATCH // 2), rows_of(2 * p + 1, PATCH // 2)
        in_l, in_r, out_l, out_r = hops(p, 0, 1, 4, 5)
        in_l.wait()
        rel_l[p] = (rel_l[p].astype(F32) + part[right, low, :].astype(F32)).astype(BF)
        out_l.start()
        in_r.wait()
        rel_r[p] = (rel_r[p].astype(F32) + part[left, high, :].astype(F32)).astype(BF)
        out_r.start()

    def backward(p, h, half):
        ds_ref = halves[half][2]
        i = p * HEADS + h
        c = pl.ds(half * QH, QH)
        scaled = (dat[head_rows(h), c].astype(F32) * linv[i, :, c]).astype(BF)
        da = scaled.astype(F32)
        delta = jnp.sum(da * dpt[p, head_rows(h, 3), c].astype(F32), axis=0, keepdims=True)
        d1 = delta.astype(BF).astype(F32)
        d2 = (delta - d1).astype(BF).astype(F32)
        d3 = delta - d1 - d2
        sub = iota((LANES, QH), 0)
        tile = jnp.where(sub // HD == h, jnp.concatenate([da] * HEADS, axis=0), 0.0)
        tail = jnp.where(sub == 0, -d1, jnp.where(sub == 1, -d2, jnp.where(sub == 2, -d3, 0.0)))
        vv = jnp.concatenate([vn[rows_of(p, PATCH), :], ones_lane], axis=1)
        dp = dotf(vv, jnp.concatenate([tile, tail], axis=0).astype(BF))
        ds = e_all[i, :, c] * dp.astype(BF)
        ds_ref[...] = ds
        dpt[p, head_rows(h), c] = (dotf(kt[p, head_rows(h), :], ds) * 0.25).astype(BF)
        for u in range(PATCH // CH):
            r = pl.ds(u * CH, CH)
            dst[half, :, r] = ds_ref[r, :].T
        for u in range(PATCH // CH):
            r = pl.ds(u * CH, CH)
            est[half, :, r] = e_all[i, r, c].T
        return dotf(qt[p, head_rows(h), c], dst[half]), dotf(scaled, est[half])

    def dout_in(b, _):
        arrived(dout, 1, b)
        return 0

    lax.fori_loop(0, blocks, dout_in, 0)
    ring_sent(pts, 0)
    ring_sent(dout, 1)

    def stat_copy(p, i, to):
        return remote(stats.at[p], got_s.at[p, i], s_send.at[p, i], s_recv.at[p, i], "mp", to)

    def backward_patch(p, _):
        for b in range(PBLK):
            da = dotf(lanes_of(dout, rows_of(p * PBLK + b, BLK)), wo[...]).astype(BF)
            dat[:, b * BLK : (b + 1) * BLK] = da.astype(F32).T.astype(BF)

        def step(h, _):
            @pl.when(jnp.logical_and(p == 1, h == HEADS // 2))
            def _():
                hand_on(0)

            dk0, dv0 = backward(p, h, 0)
            dk1, dv1 = backward(p, h, 1)
            dpt[p, head_rows(h, 1), :] = ((dk0 + dk1) * 0.25).astype(BF)
            dpt[p, head_rows(h, 2), :] = (dv0 + dv1).astype(BF)
            return 0

        lax.fori_loop(0, HEADS, step, 0)
        for b in range(PBLK):
            r = rows_of(p * PBLK + b, BLK)
            dproj = dpt[p, 0 : 3 * LANES, pl.ds(b * BLK, BLK)].astype(F32).T.astype(BF)
            pd = dot_nt(dproj, wcat).astype(BF)
            for j in range(m):
                part[j, r, :] = pd[:, j * LANES : (j + 1) * LANES]
            if b % 2 == 1:
                for c in hops(p, *((0,), (1, 3, 2))[b // 2]):
                    c.start()
            gram = dot_nt(pd, hid[r, :])
            cross = jnp.sum(jnp.where(iota((BLK, BLK), 0) == iota((BLK, BLK), 1), gram, 0.0), axis=0, keepdims=True)
            total = dot_nt(jnp.ones((8, pd.shape[1]), BF), pd)
            stats[p, 2 * b : 2 * b + 1, :] = total[0:1]
            stats[p, 2 * b + 1 : 2 * b + 2, :] = cross
        for i, to in enumerate((right, left, opposite)):
            stat_copy(p, i, to).start()
        return 0

    lax.fori_loop(0, npatch, backward_patch, 0)

    upper, lower = 0.0, 0.0
    for p in range(npatch):
        r = pl.ds(p * PATCH, PATCH)
        upper = upper + dotf(dpt[p, 0 : 3 * LANES, :], hid[r, :])
        lower = lower + dotf(dpt[p, 3 * LANES : 4 * LANES, :], lanes_of(dout, r))
    grads[:, 0 : 3 * LANES] = upper.T.astype(BF)
    grads[:, 3 * LANES : 4 * LANES] = lower.T.astype(BF)
    band = grads.shape[0] // n

    def grad_copy(src, dst, peer):
        return remote(src, dst, g_send, g_recv, "seq", peer)

    def grads_out(k, _):
        peer = lax.rem(seq + k, n)
        grad_copy(grads.at[rows_of(peer, band)], got_g.at[seq], peer).start()
        return 0

    lax.fori_loop(1, n, grads_out, 0)
    got_g[seq] = grads[rows_of(seq, band), :]
    hand_on(1)
    scale = 1.0 / (m * LANES)

    def finish(p):
        for c in hops(p, 2, 3, 4, 5):
            c.wait()
        for i, to in enumerate((right, left, opposite)):
            stat_copy(p, i, to).wait()
        st = (stats[p] + got_s[p, 0] + got_s[p, 1] + got_s[p, 2]) * scale
        for b in range(PBLK):
            r = pl.ds(p * PATCH + b * BLK, BLK)
            mean_grad = lane_copy(st[2 * b : 2 * b + 1])
            mean_cross = lane_copy(st[2 * b + 1 : 2 * b + 2])
            d_hidden = part[mp, r, :].astype(F32) + got_l[r, :].astype(F32) + got_r[r, :].astype(F32)
            grad = dout[mp, r, :].astype(F32) + invb[r, :] * (
                d_hidden - mean_grad - normq[r, :] * mean_cross
            )
            high = grad.astype(BF)
            d_high[r, :] = high
            d_low[r, :] = (grad - high.astype(F32)).astype(BF)

    finish(0)
    others = got_g.at[pl.ds(0, n - 1)]
    grad_copy(others, others, seq).wait()
    total = jnp.zeros((band, grads.shape[1]), F32)
    for k in range(n):
        total = total + got_g[k].astype(F32)
    for t in range(3):
        grad_qkv[t] = total[:, t * LANES : (t + 1) * LANES]
    grad_out[...] = total[:, 3 * LANES : 4 * LANES]
    finish(1)


def local(
    scan_points, send_order, arrive_order, qkv_weight, out_weight, voxel_grads, voxel_shard, voxel_point
):
    n, m = lax.axis_size("seq"), lax.axis_size("mp")
    rows = scan_points.shape[0]
    feats = m * LANES
    grp, cap = rows // n, 2 * voxel_grads.shape[0] // n
    blocks, npatch, band = rows // BLK, rows // PATCH, feats // n
    vmem, hbm = pl.BlockSpec(memory_space=pltpu.VMEM), pl.BlockSpec(memory_space=pl.ANY)
    dma = pltpu.SemaphoreType.DMA
    col = pltpu.VMEM((rows, LANES), BF)
    per_patch = pltpu.VMEM((npatch, LANES, PATCH), BF)
    half_f = pltpu.VMEM((PATCH, QH), F32)
    half_b = pltpu.VMEM((PATCH, QH), BF)
    masked = pltpu.VMEM((2 * LANES, QH), BF)
    coded = pltpu.VMEM((n, 16, cap), BF)
    full = pltpu.VMEM((m, rows, LANES), BF)
    hop_buf = pltpu.VMEM((npatch, PATCH // 2, LANES), BF)
    d_high, d_low, grad_qkv, grad_out = (
        pl.pallas_call(
            layer_kernel,
            out_shape=[
                jax.ShapeDtypeStruct((rows, LANES), BF),
                jax.ShapeDtypeStruct((rows, LANES), BF),
                jax.ShapeDtypeStruct((3, band, LANES), F32),
                jax.ShapeDtypeStruct((band, LANES), F32),
            ],
            in_specs=[hbm, hbm] + [vmem] * 6,
            out_specs=[vmem] * 4,
            scratch_shapes=[
                pltpu.VMEM((rows, LANES), F32), col, col, col, pltpu.VMEM((n * cap, LANES), BF), coded,
                col, pltpu.VMEM((n * cap, LANES), BF), coded, pltpu.VMEM((blocks, BLK), jnp.int32), pltpu.VMEM((n, cap), F32),
                full, full, pltpu.VMEM((rows, feats), BF), col, col,
                pltpu.VMEM((npatch, 2 * LANES, PATCH), BF),
                per_patch, per_patch, per_patch, pltpu.VMEM((LANES, PATCH), BF),
                pltpu.VMEM((npatch, 4 * LANES, PATCH), BF),
                masked, masked, half_f, half_f,
                pltpu.VMEM((npatch * HEADS, PATCH, PATCH), BF),
                half_b, half_b,
                pltpu.VMEM((2, 1, QH), F32),
                pltpu.VMEM((npatch * HEADS, 1, PATCH), F32), pltpu.VMEM((2, QH, PATCH), BF), pltpu.VMEM((2, QH, PATCH), BF),
                pltpu.VMEM((feats, 4 * LANES), BF),
                pltpu.VMEM((npatch, 2 * PBLK, BLK), F32),
                pltpu.VMEM((rows, LANES), F32),
                hop_buf, hop_buf,
                pltpu.VMEM((npatch, m - 1, 2 * PBLK, BLK), F32),
                pltpu.VMEM((n, band, 4 * LANES), BF),
                dma((2,)), dma((3,)), dma((3,)), dma((2,)), dma((2, m, blocks)),
                dma((npatch, 6)), dma((npatch, 6)), dma((npatch, m - 1)), dma((npatch, m - 1)), dma(()), dma(()),
            ],
            compiler_params=pltpu.CompilerParams(
                collective_id=0, has_side_effects=True, vmem_limit_bytes=67043328
            ),
            name="layer",
        )(
            scan_points, voxel_grads,
            send_order.reshape(-1, LANES), arrive_order.reshape(-1, LANES), voxel_point.reshape(-1, LANES),
            voxel_shard.reshape(1, -1), jnp.transpose(qkv_weight, (1, 0, 2)), out_weight,
        )
    )
    return d_high.astype(F32) + d_low.astype(F32), jnp.transpose(grad_qkv, (1, 0, 2)), grad_out


def solution(mesh):
    in_specs = (
        P("seq", None), P("seq"), P("seq"), P(None, None, "mp"), P(None, "mp"),
        P("seq", None), P("seq", None), P("seq"),
    )
    out_specs = (P("seq", "mp"), P("seq", None, "mp"), P("seq", "mp"))
    return jax.shard_map(local, mesh=mesh, in_specs=in_specs, out_specs=out_specs, check_vma=False)
```

```python
import jax
import jax.numpy as jnp
from jax import lax
from jax.experimental import pallas as pl
from jax.experimental.pallas import tpu as pltpu
from jax.sharding import PartitionSpec as P

HD = 16
PATCH = 1024
LANES = 128
BLK = 256
HEADS = LANES // HD
PBLK = PATCH // BLK
QH = 512
CH = 256
EPSILON = 1e-05
LOG2E = 1.4426950408889634
BF = jnp.bfloat16
F32 = jnp.float32
MESH = pl.DeviceIdType.MESH


def dotf(a, b):
    return jnp.dot(a, b, preferred_element_type=F32)


def dot_nt(a, b):
    return lax.dot_general(a, b, (((1,), (1,)), ((), ())), preferred_element_type=F32)


def iota(shape, axis):
    return lax.broadcasted_iota(jnp.int32, shape, axis)


def as_mask(cond):
    return jnp.where(cond, 1.0, 0.0).astype(BF)


def small_iota(shape, axis):
    return iota(shape, axis).astype(F32).astype(BF)


def lane_copy(row):
    return jnp.broadcast_to(row.astype(F32), (LANES, BLK)).T


def block_row(ref, b):
    per = BLK // LANES
    return jnp.concatenate([ref[pl.ds(b * per + u, 1), :] for u in range(per)], axis=1)


def select_rows(order_row, count):
    want = lane_copy(order_row)
    high = jnp.floor(want * (1.0 / LANES))
    low = (want - high * LANES).astype(BF)
    high = high.astype(BF)
    zero = jnp.zeros((BLK, LANES), BF)
    here = jnp.where(low == small_iota((BLK, LANES), 1), jnp.ones((BLK, LANES), BF), zero)
    return jnp.concatenate([jnp.where(high == c, here, zero) for c in range(count // LANES)], axis=1)


def hits(position, b):
    shape = (BLK, position.shape[1])
    near = jnp.clip(position.astype(F32) - (b * BLK).astype(F32), -1.0, float(BLK)).astype(BF)
    return jnp.where(small_iota(shape, 0) == near, jnp.ones(shape, BF), jnp.zeros(shape, BF))


def lanes_of(ref, r):
    return jnp.concatenate([ref[j, r, :] for j in range(ref.shape[0])], axis=1)


def rows_of(block, size):
    return pl.ds(pl.multiple_of(block * size, size), size)


def remote(src, dst, send_sem, recv_sem, axis, to):
    return pltpu.make_async_remote_copy(
        src_ref=src, dst_ref=dst, send_sem=send_sem, recv_sem=recv_sem,
        device_id={axis: to}, device_id_type=MESH,
    )


def layer_kernel(
    scan, voxels, send_order, arrive_order, point, shard, w, wo,
    d_high, d_low, grad_all,
    normq, x, v, sendp, sendv, sendi, gotp, gotv, goti, place, at_all,
    pts, dout, hid, kn, vn, qhl, qt, kt, vt, dat, dpt, qm0, qm1, s0, s1, e_all, ds0, ds1, top, linv, dst, est,
    grads, stats, invb, rel_l, rel_r, got_s, got_g,
    in_sem, send_sem, recv_sem, ring_send, ring_recv, p_send, p_recv, s_send, s_recv, g_send, g_recv,
):
    seq, mp = lax.axis_index("seq"), lax.axis_index("mp")
    n, m = lax.axis_size("seq"), lax.axis_size("mp")
    rows = x.shape[0]
    npatch = rows // PATCH
    grp = rows // n
    cap = gotv.shape[0] // n
    blocks = rows // BLK
    right, left, opposite = lax.rem(mp + 1, m), lax.rem(mp + m - 1, m), lax.rem(mp + 2, m)
    part, got_l, got_r = pts, x, v

    mine = pl.ds(pl.multiple_of(mp * LANES, LANES), LANES)
    in_x = pltpu.make_async_copy(scan.at[:, mine], x, in_sem.at[0])
    in_v = pltpu.make_async_copy(voxels.at[:, mine], v, in_sem.at[1])
    in_x.start()
    in_v.start()
    barrier = pltpu.get_barrier_semaphore()
    for k in range(1, n):
        pl.semaphore_signal(barrier, inc=1, device_id={"seq": lax.rem(seq + k, n)}, device_id_type=MESH)
    for to in (right, left, opposite):
        pl.semaphore_signal(barrier, inc=1, device_id={"mp": to}, device_id_type=MESH)

    def send(src, dst, kind, peer):
        return remote(src, dst, send_sem.at[kind], recv_sem.at[kind], "seq", peer)

    tri = as_mask(iota((BLK, BLK), 0) < iota((BLK, BLK), 1))
    carry = jnp.zeros((n, 1), F32)
    codes = jnp.zeros((3 * n, cap), F32)
    for b in range(blocks):
        target = shard[:, b * BLK : (b + 1) * BLK]
        hot = jnp.where(iota((n, BLK), 0) == target, 1.0, 0.0)
        before = dotf(hot.astype(BF), tri) + carry
        rank = jnp.sum(before * hot, axis=0, keepdims=True)
        carry = carry + jnp.sum(hot, axis=1, keepdims=True)
        place[b : b + 1, :] = target * cap + rank.astype(jnp.int32)
        where_to = block_row(point, b)
        high = (where_to // 64).astype(F32)
        low = (where_to % 64).astype(F32)
        slot = as_mask(iota((cap, BLK), 0) == rank.astype(jnp.int32))
        coded = jnp.concatenate([hot * high, hot * low, hot], axis=0).astype(BF)
        codes = codes + dot_nt(coded, slot)
    sub16 = iota((16, cap), 0)
    for t in range(n):
        a, b, c = codes[t : t + 1], codes[n + t : n + t + 1], codes[2 * n + t : 2 * n + t + 1]
        sendi[t] = jnp.where(sub16 == 0, a, jnp.where(sub16 == 1, b, c)).astype(BF)
    in_x.wait()
    per = BLK // grp

    def ordered(i):
        return lax.rem(i + seq // per, blocks)

    def points_pick(i, _):
        b = ordered(i)
        hot = select_rows(block_row(send_order, b), rows)
        sendp[rows_of(b, BLK), :] = dotf(hot, x[...]).astype(BF)
        return 0

    def points_send(i, _):
        for u in range(per):
            peer = ordered(i) * per + u

            @pl.when(peer != seq)
            def _():
                send(sendp.at[rows_of(peer, grp)], gotp.at[rows_of(seq, grp)], 0, peer).start()

        return 0

    def points_out(i, _):
        points_pick(i, 0)
        points_send(i, 0)
        return 0

    lax.fori_loop(0, blocks // 2, points_pick, 0)
    pl.semaphore_wait(barrier, n + m - 2)
    lax.fori_loop(0, blocks // 2, points_send, 0)
    lax.fori_loop(blocks // 2, blocks, points_out, 0)
    gotp[rows_of(seq, grp), :] = sendp[rows_of(seq, grp), :]

    in_v.wait()
    per_v = BLK // cap
    vblocks = n // per_v

    def voxels_out(i, _):
        b = lax.rem(i + seq // per_v, vblocks)
        hot = jnp.concatenate([hits(place[c : c + 1, :], b) for c in range(blocks)], axis=1)
        sendv[rows_of(b, BLK), :] = dotf(hot, v[...]).astype(BF)
        for u in range(per_v):
            peer = b * per_v + u

            @pl.when(peer != seq)
            def _():
                send(sendv.at[rows_of(peer, cap)], gotv.at[rows_of(seq, cap)], 1, peer).start()
                send(sendi.at[peer], goti.at[seq], 2, peer).start()

        return 0

    lax.fori_loop(0, vblocks, voxels_out, 0)
    gotv[rows_of(seq, cap), :] = sendv[rows_of(seq, cap), :]
    goti[seq] = sendi[seq]

    def wait_all(kind, ref, size):
        other = ref.at[pl.ds(0, size)]
        send(other, other, kind, seq).wait_recv()
        send(other, other, kind, seq).wait_send()

    def ring(full, kind, owner, b, to):
        at = full.at[owner, rows_of(b, BLK)]
        return remote(at, at, ring_send.at[kind], ring_recv.at[kind, owner, b], "mp", to)

    def goes_right(b):
        return lax.rem(b, PBLK) < PBLK // 2

    def relay(full, kind, b):
        @pl.when(goes_right(b))
        def _():
            ring(full, kind, left, b, right).wait_recv()
            ring(full, kind, left, b, right).start()

        @pl.when(jnp.logical_not(goes_right(b)))
        def _():
            ring(full, kind, right, b, left).wait_recv()
            ring(full, kind, right, b, left).start()

    def arrived(full, kind, b):
        @pl.when(goes_right(b))
        def _():
            ring(full, kind, right, b, left).wait_recv()

        @pl.when(jnp.logical_not(goes_right(b)))
        def _():
            ring(full, kind, left, b, right).wait_recv()

        ring(full, kind, opposite, b, right).wait_recv()

    def ring_sent(full, kind):
        for _ in range(3):
            remote(full.at[0], full.at[0], ring_send.at[kind], ring_recv.at[kind, 0, 0], "mp", right).wait_send()

    wait_all(0, gotp, (n - 1) * grp)

    def points_in(b, _):
        hot = select_rows(block_row(arrive_order, b), rows)
        pts[mp, rows_of(b, BLK), :] = dotf(hot, gotp[...]).astype(BF)
        ring(pts, 0, mp, b, right).start()
        ring(pts, 0, mp, b, left).start()
        return 0

    lax.fori_loop(0, blocks, points_in, 0)
    wait_all(1, gotv, (n - 1) * cap)
    wait_all(2, goti, n - 1)
    for t in range(n):
        code = goti[t].astype(F32)
        at_all[t : t + 1, :] = jnp.where(code[2:3, :] > 0.5, code[0:1, :] * 64.0 + code[1:2, :], -1.0)

    def voxels_in(b, _):
        relay(pts, 0, b)
        hot = jnp.concatenate([hits(at_all[t : t + 1, :], b) for t in range(n)], axis=1)
        dout[mp, rows_of(b, BLK), :] = dotf(hot, gotv[...]).astype(BF)
        ring(dout, 1, mp, b, right).start()
        ring(dout, 1, mp, b, left).start()
        return 0

    lax.fori_loop(0, blocks, voxels_in, 0)

    wcat = jnp.concatenate([w[t] for t in range(3)], axis=1)
    ones_lane = as_mask(iota((PATCH, LANES), 1) < 3)
    halves = ((qm0, s0, ds0), (qm1, s1, ds1))

    def normalise(p):
        for b in range(PBLK):
            r = rows_of(p * PBLK + b, BLK)
            c = pl.ds(b * BLK, BLK)
            xb = lanes_of(pts, r).astype(F32)
            xb = xb - jnp.mean(xb, axis=1, keepdims=True)
            inv = lax.rsqrt(jnp.mean(xb * xb, axis=1, keepdims=True) + EPSILON)
            normed = xb * inv
            hidden = normed.astype(BF)
            hid[r, :] = hidden
            invb[r, :] = jnp.broadcast_to(inv, (BLK, LANES))
            own = normed[:, 0:LANES]
            for j in range(1, m):
                own = jnp.where(mp == j, normed[:, j * LANES : (j + 1) * LANES], own)
            normq[r, :] = own
            proj = dotf(hidden, wcat)
            q, k, val = (proj[:, t * LANES : (t + 1) * LANES].astype(BF) for t in range(3))
            kn[r, :] = k
            vn[r, :] = val
            qf = q.astype(F32).T
            qt[p, :, c] = qf.astype(BF)
            qs = qf * (0.25 * LOG2E)
            high = qs.astype(BF)
            qhl[p, 0:LANES, c] = high
            qhl[p, LANES : 2 * LANES, c] = (qs - high.astype(F32)).astype(BF)
            kt[p, :, c] = k.astype(F32).T.astype(BF)
            vt[p, :, c] = val.astype(F32).T.astype(BF)

    def head_rows(h, base=0):
        return pl.ds(pl.multiple_of(base * LANES + h * HD, HD), HD)

    def scores(p, h, half):
        qm, s = halves[half][:2]
        c = pl.ds(half * QH, QH)
        rmask = (iota((LANES, QH), 0) // HD) == h
        zero = jnp.zeros((LANES, QH), BF)
        qm[0:LANES, :] = jnp.where(rmask, qhl[p, 0:LANES, c], zero)
        qm[LANES : 2 * LANES, :] = jnp.where(rmask, qhl[p, LANES : 2 * LANES, c], zero)
        k = kn[rows_of(p, PATCH), :]
        val = dotf(jnp.concatenate([k, k], axis=1), qm[...])
        s[...] = val
        top[half] = jnp.max(val, axis=0, keepdims=True)

    def forward(p, h, half):
        s = halves[half][1]
        c = pl.ds(half * QH, QH)
        e = jnp.exp2(s[...] - top[half]).astype(BF)
        e_all[p * HEADS + h, :, c] = e
        vt1 = jnp.concatenate([vt[p, head_rows(h), :], jnp.ones((HD, PATCH), BF)], axis=0)
        av = dotf(vt1, e)
        inv = 1.0 / av[HD : HD + 1, :]
        linv[p * HEADS + h, :, c] = inv
        dpt[p, head_rows(h, 3), c] = (av[0:HD, :] * inv).astype(BF)

    def forward_patch(p, _):
        def ready(b, _):
            arrived(pts, 0, p * PBLK + b)
            return 0

        lax.fori_loop(0, PBLK, ready, 0)
        normalise(p)
        scores(p, 0, 0)

        def step(i, _):
            h = i // 2

            b = (p * 2 * HEADS + i - HEADS) // 2

            @pl.when(jnp.logical_and(lax.rem(i, 2) == 0, jnp.logical_and(b >= 0, b < blocks)))
            def _():
                relay(dout, 1, b)

            @pl.when(lax.rem(i, 2) == 0)
            def _():
                scores(p, h, 1)
                forward(p, h, 0)

            @pl.when(jnp.logical_and(lax.rem(i, 2) == 1, h < HEADS - 1))
            def _():
                scores(p, h + 1, 0)
                forward(p, h, 1)

            @pl.when(i == 2 * HEADS - 1)
            def _():
                forward(p, HEADS - 1, 1)

            return 0

        lax.fori_loop(0, 2 * HEADS, step, 0)
        return 0

    lax.fori_loop(0, npatch, forward_patch, 0)

    def hop(p, sem, src, dst, to):
        return remote(src, dst, p_send.at[p, sem], p_recv.at[p, sem], "mp", to)

    def hops(p, *which):
        low, high = rows_of(2 * p, PATCH // 2), rows_of(2 * p + 1, PATCH // 2)
        ends = (
            (part.at[opposite, low], rel_l.at[p], right),
            (part.at[opposite, high], rel_r.at[p], left),
            (part.at[right, high], got_l.at[high], right),
            (part.at[left, low], got_r.at[low], left),
            (rel_l.at[p], got_l.at[low], right),
            (rel_r.at[p], got_r.at[high], left),
        )
        return [hop(p, w, *ends[w]) for w in which]

    def hand_on(p):
        low, high = rows_of(2 * p, PATCH // 2), rows_of(2 * p + 1, PATCH // 2)
        in_l, in_r, out_l, out_r = hops(p, 0, 1, 4, 5)
        in_l.wait()
        rel_l[p] = (rel_l[p].astype(F32) + part[right, low, :].astype(F32)).astype(BF)
        out_l.start()
        in_r.wait()
        rel_r[p] = (rel_r[p].astype(F32) + part[left, high, :].astype(F32)).astype(BF)
        out_r.start()

    def backward(p, h, half):
        ds_ref = halves[half][2]
        i = p * HEADS + h
        c = pl.ds(half * QH, QH)
        scaled = (dat[head_rows(h), c].astype(F32) * linv[i, :, c]).astype(BF)
        da = scaled.astype(F32)
        delta = jnp.sum(da * dpt[p, head_rows(h, 3), c].astype(F32), axis=0, keepdims=True)
        d1 = delta.astype(BF).astype(F32)
        d2 = (delta - d1).astype(BF).astype(F32)
        d3 = delta - d1 - d2
        sub = iota((LANES, QH), 0)
        tile = jnp.where(sub // HD == h, jnp.concatenate([da] * HEADS, axis=0), 0.0)
        tail = jnp.where(sub == 0, -d1, jnp.where(sub == 1, -d2, jnp.where(sub == 2, -d3, 0.0)))
        vv = jnp.concatenate([vn[rows_of(p, PATCH), :], ones_lane], axis=1)
        dp = dotf(vv, jnp.concatenate([tile, tail], axis=0).astype(BF))
        ds = e_all[i, :, c] * dp.astype(BF)
        ds_ref[...] = ds
        dpt[p, head_rows(h), c] = (dotf(kt[p, head_rows(h), :], ds) * 0.25).astype(BF)
        for u in range(PATCH // CH):
            r = pl.ds(u * CH, CH)
            dst[half, :, r] = ds_ref[r, :].T
        for u in range(PATCH // CH):
            r = pl.ds(u * CH, CH)
            est[half, :, r] = e_all[i, r, c].T
        return dotf(qt[p, head_rows(h), c], dst[half]), dotf(scaled, est[half])

    def dout_in(b, _):
        arrived(dout, 1, b)
        return 0

    lax.fori_loop(0, blocks, dout_in, 0)
    ring_sent(pts, 0)
    ring_sent(dout, 1)

    def stat_copy(p, i, to):
        return remote(stats.at[p], got_s.at[p, i], s_send.at[p, i], s_recv.at[p, i], "mp", to)

    def backward_patch(p, _):
        for b in range(PBLK):
            da = dotf(lanes_of(dout, rows_of(p * PBLK + b, BLK)), wo[...]).astype(BF)
            dat[:, b * BLK : (b + 1) * BLK] = da.astype(F32).T.astype(BF)

        def step(h, _):
            @pl.when(jnp.logical_and(p == 1, h == HEADS // 2))
            def _():
                hand_on(0)

            dk0, dv0 = backward(p, h, 0)
            dk1, dv1 = backward(p, h, 1)
            dpt[p, head_rows(h, 1), :] = ((dk0 + dk1) * 0.25).astype(BF)
            dpt[p, head_rows(h, 2), :] = (dv0 + dv1).astype(BF)
            return 0

        lax.fori_loop(0, HEADS, step, 0)
        for b in range(PBLK):
            r = rows_of(p * PBLK + b, BLK)
            dproj = dpt[p, 0 : 3 * LANES, pl.ds(b * BLK, BLK)].astype(F32).T.astype(BF)
            pd = dot_nt(dproj, wcat).astype(BF)
            for j in range(m):
                part[j, r, :] = pd[:, j * LANES : (j + 1) * LANES]
            if b % 2 == 1:
                for c in hops(p, *((0,), (1, 3, 2))[b // 2]):
                    c.start()
        for b in range(PBLK):
            r = rows_of(p * PBLK + b, BLK)
            pd = lanes_of(part, r)
            gram = dot_nt(pd, hid[r, :])
            cross = jnp.sum(jnp.where(iota((BLK, BLK), 0) == iota((BLK, BLK), 1), gram, 0.0), axis=0, keepdims=True)
            total = dot_nt(jnp.ones((8, pd.shape[1]), BF), pd)
            stats[p, 2 * b : 2 * b + 1, :] = total[0:1]
            stats[p, 2 * b + 1 : 2 * b + 2, :] = cross
        for i, to in enumerate((right, left, opposite)):
            stat_copy(p, i, to).start()
        return 0

    lax.fori_loop(0, npatch, backward_patch, 0)

    upper, lower = 0.0, 0.0
    for p in range(npatch):
        r = pl.ds(p * PATCH, PATCH)
        upper = upper + dotf(dpt[p, 0 : 3 * LANES, :], hid[r, :])
        lower = lower + dotf(dpt[p, 3 * LANES : 4 * LANES, :], lanes_of(dout, r))
    grads[:, 0 : 3 * LANES] = upper.T.astype(BF)
    grads[:, 3 * LANES : 4 * LANES] = lower.T.astype(BF)
    band = grads.shape[0] // n

    def grad_copy(src, dst, peer):
        return remote(src, dst, g_send, g_recv, "seq", peer)

    def grads_out(k, _):
        peer = lax.rem(seq + k, n)
        grad_copy(grads.at[rows_of(peer, band)], got_g.at[seq], peer).start()
        return 0

    lax.fori_loop(1, n, grads_out, 0)
    got_g[seq] = grads[rows_of(seq, band), :]
    hand_on(1)
    scale = 1.0 / (m * LANES)

    def finish(p):
        for c in hops(p, 2, 3, 4, 5):
            c.wait()
        for i, to in enumerate((right, left, opposite)):
            stat_copy(p, i, to).wait()
        st = (stats[p] + got_s[p, 0] + got_s[p, 1] + got_s[p, 2]) * scale
        for b in range(PBLK):
            r = pl.ds(p * PATCH + b * BLK, BLK)
            mean_grad = lane_copy(st[2 * b : 2 * b + 1])
            mean_cross = lane_copy(st[2 * b + 1 : 2 * b + 2])
            d_hidden = part[mp, r, :].astype(F32) + got_l[r, :].astype(F32) + got_r[r, :].astype(F32)
            grad = dout[mp, r, :].astype(F32) + invb[r, :] * (
                d_hidden - mean_grad - normq[r, :] * mean_cross
            )
            high = grad.astype(BF)
            d_high[r, :] = high
            d_low[r, :] = (grad - high.astype(F32)).astype(BF)

    finish(0)
    others = got_g.at[pl.ds(0, n - 1)]
    grad_copy(others, others, seq).wait()
    total = jnp.zeros((band, grads.shape[1]), F32)
    for k in range(n):
        total = total + got_g[k].astype(F32)
    for t in range(4):
        grad_all[t] = total[:, t * LANES : (t + 1) * LANES]
    finish(1)


def local(
    scan_points, send_order, arrive_order, qkv_weight, out_weight, voxel_grads, voxel_shard, voxel_point
):
    n, m = lax.axis_size("seq"), lax.axis_size("mp")
    rows = scan_points.shape[0]
    feats = m * LANES
    grp, cap = rows // n, 2 * voxel_grads.shape[0] // n
    blocks, npatch, band = rows // BLK, rows // PATCH, feats // n
    vmem, hbm = pl.BlockSpec(memory_space=pltpu.VMEM), pl.BlockSpec(memory_space=pl.ANY)
    dma = pltpu.SemaphoreType.DMA
    col = pltpu.VMEM((rows, LANES), BF)
    per_patch = pltpu.VMEM((npatch, LANES, PATCH), BF)
    half_f = pltpu.VMEM((PATCH, QH), F32)
    half_b = pltpu.VMEM((PATCH, QH), BF)
    masked = pltpu.VMEM((2 * LANES, QH), BF)
    coded = pltpu.VMEM((n, 16, cap), BF)
    full = pltpu.VMEM((m, rows, LANES), BF)
    hop_buf = pltpu.VMEM((npatch, PATCH // 2, LANES), BF)
    d_high, d_low, grad_all = (
        pl.pallas_call(
            layer_kernel,
            out_shape=[
                jax.ShapeDtypeStruct((rows, LANES), BF),
                jax.ShapeDtypeStruct((rows, LANES), BF),
                jax.ShapeDtypeStruct((4, band, LANES), F32),
            ],
            in_specs=[hbm, hbm] + [vmem] * 6,
            out_specs=[vmem] * 3,
            scratch_shapes=[
                pltpu.VMEM((rows, LANES), F32), col, col, col, pltpu.VMEM((n * cap, LANES), BF), coded,
                col, pltpu.VMEM((n * cap, LANES), BF), coded, pltpu.VMEM((blocks, BLK), jnp.int32), pltpu.VMEM((n, cap), F32),
                full, full, pltpu.VMEM((rows, feats), BF), col, col,
                pltpu.VMEM((npatch, 2 * LANES, PATCH), BF),
                per_patch, per_patch, per_patch, pltpu.VMEM((LANES, PATCH), BF),
                pltpu.VMEM((npatch, 4 * LANES, PATCH), BF),
                masked, masked, half_f, half_f,
                pltpu.VMEM((npatch * HEADS, PATCH, PATCH), BF),
                half_b, half_b,
                pltpu.VMEM((2, 1, QH), F32),
                pltpu.VMEM((npatch * HEADS, 1, PATCH), F32), pltpu.VMEM((2, QH, PATCH), BF), pltpu.VMEM((2, QH, PATCH), BF),
                pltpu.VMEM((feats, 4 * LANES), BF),
                pltpu.VMEM((npatch, 2 * PBLK, BLK), F32),
                pltpu.VMEM((rows, LANES), F32),
                hop_buf, hop_buf,
                pltpu.VMEM((npatch, m - 1, 2 * PBLK, BLK), F32),
                pltpu.VMEM((n, band, 4 * LANES), BF),
                dma((2,)), dma((3,)), dma((3,)), dma((2,)), dma((2, m, blocks)),
                dma((npatch, 6)), dma((npatch, 6)), dma((npatch, m - 1)), dma((npatch, m - 1)), dma(()), dma(()),
            ],
            compiler_params=pltpu.CompilerParams(
                collective_id=0, has_side_effects=True, vmem_limit_bytes=67043328
            ),
            name="layer",
        )(
            scan_points, voxel_grads,
            send_order.reshape(-1, LANES), arrive_order.reshape(-1, LANES), voxel_point.reshape(-1, LANES),
            voxel_shard.reshape(1, -1), jnp.transpose(qkv_weight, (1, 0, 2)), out_weight,
        )
    )
    return d_high.astype(F32) + d_low.astype(F32), jnp.transpose(grad_all[:3], (1, 0, 2)), grad_all[3]


def solution(mesh):
    in_specs = (
        P("seq", None), P("seq"), P("seq"), P(None, None, "mp"), P(None, "mp"),
        P("seq", None), P("seq", None), P("seq"),
    )
    out_specs = (P("seq", "mp"), P("seq", None, "mp"), P("seq", "mp"))
    return jax.shard_map(local, mesh=mesh, in_specs=in_specs, out_specs=out_specs, check_vma=False)
```

```python
import jax
import jax.numpy as jnp
from jax import lax
from jax.experimental import pallas as pl
from jax.experimental.pallas import tpu as pltpu
from jax.sharding import PartitionSpec as P

HD = 16
PATCH = 1024
LANES = 128
BLK = 256
HEADS = LANES // HD
PBLK = PATCH // BLK
QH = 512
CH = 256
EPSILON = 1e-05
LOG2E = 1.4426950408889634
BF = jnp.bfloat16
F32 = jnp.float32
MESH = pl.DeviceIdType.MESH


def dotf(a, b):
    return jnp.dot(a, b, preferred_element_type=F32)


def dot_nt(a, b):
    return lax.dot_general(a, b, (((1,), (1,)), ((), ())), preferred_element_type=F32)


def iota(shape, axis):
    return lax.broadcasted_iota(jnp.int32, shape, axis)


def as_mask(cond):
    return jnp.where(cond, 1.0, 0.0).astype(BF)


def small_iota(shape, axis):
    return iota(shape, axis).astype(F32).astype(BF)


def lane_copy(row):
    return jnp.broadcast_to(row.astype(F32), (LANES, BLK)).T


def block_row(ref, b):
    per = BLK // LANES
    return jnp.concatenate([ref[pl.ds(b * per + u, 1), :] for u in range(per)], axis=1)


def select_rows(order_row, count):
    want = lane_copy(order_row)
    high = jnp.floor(want * (1.0 / LANES))
    low = (want - high * LANES).astype(BF)
    high = high.astype(BF)
    zero = jnp.zeros((BLK, LANES), BF)
    here = jnp.where(low == small_iota((BLK, LANES), 1), jnp.ones((BLK, LANES), BF), zero)
    return jnp.concatenate([jnp.where(high == c, here, zero) for c in range(count // LANES)], axis=1)


def hits(position, b):
    shape = (BLK, position.shape[1])
    near = jnp.clip(position.astype(F32) - (b * BLK).astype(F32), -1.0, float(BLK)).astype(BF)
    return jnp.where(small_iota(shape, 0) == near, jnp.ones(shape, BF), jnp.zeros(shape, BF))


def lanes_of(ref, r):
    return jnp.concatenate([ref[j, r, :] for j in range(ref.shape[0])], axis=1)


def rows_of(block, size):
    return pl.ds(pl.multiple_of(block * size, size), size)


def remote(src, dst, send_sem, recv_sem, axis, to):
    return pltpu.make_async_remote_copy(
        src_ref=src, dst_ref=dst, send_sem=send_sem, recv_sem=recv_sem,
        device_id={axis: to}, device_id_type=MESH,
    )


def layer_kernel(
    scan, voxels, send_order, arrive_order, point, shard, w, wo,
    d_high, d_low, grad_all,
    normq, x, v, sendp, sendv, sendi, gotp, gotv, goti, place, at_all,
    pts, dout, hid, kn, vn, qhl, qt, kt, vt, dat, dpt, qm0, qm1, s0, s1, e_all, ds0, ds1, top, linv, dst, est,
    grads, stats, invb, rel_l, rel_r, got_s, got_g,
    in_sem, send_sem, recv_sem, ring_send, ring_recv, p_send, p_recv, s_send, s_recv, g_send, g_recv,
):
    seq, mp = lax.axis_index("seq"), lax.axis_index("mp")
    n, m = lax.axis_size("seq"), lax.axis_size("mp")
    rows = x.shape[0]
    npatch = rows // PATCH
    grp = rows // n
    cap = gotv.shape[0] // n
    blocks = rows // BLK
    right, left, opposite = lax.rem(mp + 1, m), lax.rem(mp + m - 1, m), lax.rem(mp + 2, m)
    part, got_l, got_r = pts, x, v

    mine = pl.ds(pl.multiple_of(mp * LANES, LANES), LANES)
    in_x = pltpu.make_async_copy(scan.at[:, mine], x, in_sem.at[0])
    in_v = pltpu.make_async_copy(voxels.at[:, mine], v, in_sem.at[1])
    in_x.start()
    in_v.start()
    barrier = pltpu.get_barrier_semaphore()
    for k in range(1, n):
        pl.semaphore_signal(barrier, inc=1, device_id={"seq": lax.rem(seq + k, n)}, device_id_type=MESH)
    for to in (right, left, opposite):
        pl.semaphore_signal(barrier, inc=1, device_id={"mp": to}, device_id_type=MESH)

    def send(src, dst, kind, peer):
        return remote(src, dst, send_sem.at[kind], recv_sem.at[kind], "seq", peer)

    tri = as_mask(iota((BLK, BLK), 0) < iota((BLK, BLK), 1))
    carry = jnp.zeros((n, 1), F32)
    codes = jnp.zeros((3 * n, cap), F32)
    for b in range(blocks):
        target = shard[:, b * BLK : (b + 1) * BLK]
        hot = jnp.where(iota((n, BLK), 0) == target, 1.0, 0.0)
        before = dotf(hot.astype(BF), tri) + carry
        rank = jnp.sum(before * hot, axis=0, keepdims=True)
        carry = carry + jnp.sum(hot, axis=1, keepdims=True)
        place[b : b + 1, :] = target * cap + rank.astype(jnp.int32)
        where_to = block_row(point, b)
        high = (where_to // 64).astype(F32)
        low = (where_to % 64).astype(F32)
        slot = as_mask(iota((cap, BLK), 0) == rank.astype(jnp.int32))
        coded = jnp.concatenate([hot * high, hot * low, hot], axis=0).astype(BF)
        codes = codes + dot_nt(coded, slot)
    sub16 = iota((16, cap), 0)
    for t in range(n):
        a, b, c = codes[t : t + 1], codes[n + t : n + t + 1], codes[2 * n + t : 2 * n + t + 1]
        sendi[t] = jnp.where(sub16 == 0, a, jnp.where(sub16 == 1, b, c)).astype(BF)
    in_x.wait()
    per = BLK // grp

    def ordered(i):
        return lax.rem(i + seq // per, blocks)

    def points_pick(i, _):
        b = ordered(i)
        hot = select_rows(block_row(send_order, b), rows)
        sendp[rows_of(b, BLK), :] = dotf(hot, x[...]).astype(BF)
        return 0

    def points_send(i, _):
        for u in range(per):
            peer = ordered(i) * per + u

            @pl.when(peer != seq)
            def _():
                send(sendp.at[rows_of(peer, grp)], gotp.at[rows_of(seq, grp)], 0, peer).start()

        return 0

    def points_out(i, _):
        points_pick(i, 0)
        points_send(i, 0)
        return 0

    lax.fori_loop(0, blocks // 2, points_pick, 0)
    pl.semaphore_wait(barrier, n + m - 2)
    lax.fori_loop(0, blocks // 2, points_send, 0)
    lax.fori_loop(blocks // 2, blocks, points_out, 0)
    gotp[rows_of(seq, grp), :] = sendp[rows_of(seq, grp), :]

    in_v.wait()
    per_v = BLK // cap
    vblocks = n // per_v

    def voxels_out(i, _):
        b = lax.rem(i + seq // per_v, vblocks)
        hot = jnp.concatenate([hits(place[c : c + 1, :], b) for c in range(blocks)], axis=1)
        sendv[rows_of(b, BLK), :] = dotf(hot, v[...]).astype(BF)
        for u in range(per_v):
            peer = b * per_v + u

            @pl.when(peer != seq)
            def _():
                send(sendv.at[rows_of(peer, cap)], gotv.at[rows_of(seq, cap)], 1, peer).start()
                send(sendi.at[peer], goti.at[seq], 2, peer).start()

        return 0

    lax.fori_loop(0, vblocks, voxels_out, 0)
    gotv[rows_of(seq, cap), :] = sendv[rows_of(seq, cap), :]
    goti[seq] = sendi[seq]

    def wait_all(kind, ref, size):
        other = ref.at[pl.ds(0, size)]
        send(other, other, kind, seq).wait_recv()
        send(other, other, kind, seq).wait_send()

    def ring(full, kind, owner, b, to):
        at = full.at[owner, rows_of(b, BLK)]
        return remote(at, at, ring_send.at[kind], ring_recv.at[kind, owner, b], "mp", to)

    def goes_right(b):
        return lax.rem(b, PBLK) < PBLK // 2

    def relay(full, kind, b):
        @pl.when(goes_right(b))
        def _():
            ring(full, kind, left, b, right).wait_recv()
            ring(full, kind, left, b, right).start()

        @pl.when(jnp.logical_not(goes_right(b)))
        def _():
            ring(full, kind, right, b, left).wait_recv()
            ring(full, kind, right, b, left).start()

    def arrived(full, kind, b):
        @pl.when(goes_right(b))
        def _():
            ring(full, kind, right, b, left).wait_recv()

        @pl.when(jnp.logical_not(goes_right(b)))
        def _():
            ring(full, kind, left, b, right).wait_recv()

        ring(full, kind, opposite, b, right).wait_recv()

    def ring_sent(full, kind):
        for _ in range(3):
            remote(full.at[0], full.at[0], ring_send.at[kind], ring_recv.at[kind, 0, 0], "mp", right).wait_send()

    wait_all(0, gotp, (n - 1) * grp)

    def points_in(b, _):
        hot = select_rows(block_row(arrive_order, b), rows)
        pts[mp, rows_of(b, BLK), :] = dotf(hot, gotp[...]).astype(BF)
        ring(pts, 0, mp, b, right).start()
        ring(pts, 0, mp, b, left).start()
        return 0

    lax.fori_loop(0, blocks, points_in, 0)
    wait_all(1, gotv, (n - 1) * cap)
    wait_all(2, goti, n - 1)
    for t in range(n):
        code = goti[t].astype(F32)
        at_all[t : t + 1, :] = jnp.where(code[2:3, :] > 0.5, code[0:1, :] * 64.0 + code[1:2, :], -1.0)

    def voxels_in(b, _):
        relay(pts, 0, b)
        hot = jnp.concatenate([hits(at_all[t : t + 1, :], b) for t in range(n)], axis=1)
        dout[mp, rows_of(b, BLK), :] = dotf(hot, gotv[...]).astype(BF)
        ring(dout, 1, mp, b, right).start()
        ring(dout, 1, mp, b, left).start()
        return 0

    lax.fori_loop(0, blocks, voxels_in, 0)

    wcat = jnp.concatenate([w[t] for t in range(3)], axis=1)
    ones_lane = as_mask(iota((PATCH, LANES), 1) < 3)
    halves = ((qm0, s0, ds0), (qm1, s1, ds1))

    def normalise(p):
        for b in range(PBLK):
            r = rows_of(p * PBLK + b, BLK)
            c = pl.ds(b * BLK, BLK)
            xb = lanes_of(pts, r).astype(F32)
            xb = xb - jnp.mean(xb, axis=1, keepdims=True)
            inv = lax.rsqrt(jnp.mean(xb * xb, axis=1, keepdims=True) + EPSILON)
            normed = xb * inv
            hidden = normed.astype(BF)
            hid[r, :] = hidden
            invb[r, :] = jnp.broadcast_to(inv, (BLK, LANES))
            own = normed[:, 0:LANES]
            for j in range(1, m):
                own = jnp.where(mp == j, normed[:, j * LANES : (j + 1) * LANES], own)
            normq[r, :] = own
            proj = dotf(hidden, wcat)
            q, k, val = (proj[:, t * LANES : (t + 1) * LANES].astype(BF) for t in range(3))
            kn[r, :] = k
            vn[r, :] = val
            qf = q.astype(F32).T
            qt[p, :, c] = qf.astype(BF)
            qs = qf * (0.25 * LOG2E)
            high = qs.astype(BF)
            qhl[p, 0:LANES, c] = high
            qhl[p, LANES : 2 * LANES, c] = (qs - high.astype(F32)).astype(BF)
            kt[p, :, c] = k.astype(F32).T.astype(BF)
            vt[p, :, c] = val.astype(F32).T.astype(BF)

    def head_rows(h, base=0):
        return pl.ds(pl.multiple_of(base * LANES + h * HD, HD), HD)

    def scores(p, h, half):
        qm, s = halves[half][:2]
        c = pl.ds(half * QH, QH)
        rmask = (iota((LANES, QH), 0) // HD) == h
        zero = jnp.zeros((LANES, QH), BF)
        qm[0:LANES, :] = jnp.where(rmask, qhl[p, 0:LANES, c], zero)
        qm[LANES : 2 * LANES, :] = jnp.where(rmask, qhl[p, LANES : 2 * LANES, c], zero)
        k = kn[rows_of(p, PATCH), :]
        val = dotf(jnp.concatenate([k, k], axis=1), qm[...])
        s[...] = val
        top[half] = jnp.max(val, axis=0, keepdims=True)

    def forward(p, h, half):
        s = halves[half][1]
        c = pl.ds(half * QH, QH)
        e = jnp.exp2(s[...] - top[half]).astype(BF)
        e_all[p * HEADS + h, :, c] = e
        vt1 = jnp.concatenate([vt[p, head_rows(h), :], jnp.ones((HD, PATCH), BF)], axis=0)
        av = dotf(vt1, e)
        inv = 1.0 / av[HD : HD + 1, :]
        linv[p * HEADS + h, :, c] = inv
        dpt[p, head_rows(h, 3), c] = (av[0:HD, :] * inv).astype(BF)

    def forward_patch(p, _):
        def ready(b, _):
            arrived(pts, 0, p * PBLK + b)
            return 0

        lax.fori_loop(0, PBLK, ready, 0)
        normalise(p)
        scores(p, 0, 0)

        def step(i, _):
            h = i // 2

            b = (p * 2 * HEADS + i - HEADS - 2) // 2

            @pl.when(jnp.logical_and(lax.rem(i, 2) == 0, jnp.logical_and(b >= 0, b < blocks)))
            def _():
                relay(dout, 1, b)

            @pl.when(lax.rem(i, 2) == 0)
            def _():
                scores(p, h, 1)
                forward(p, h, 0)

            @pl.when(jnp.logical_and(lax.rem(i, 2) == 1, h < HEADS - 1))
            def _():
                scores(p, h + 1, 0)
                forward(p, h, 1)

            @pl.when(i == 2 * HEADS - 1)
            def _():
                forward(p, HEADS - 1, 1)

            return 0

        lax.fori_loop(0, 2 * HEADS, step, 0)
        return 0

    lax.fori_loop(0, npatch, forward_patch, 0)

    def hop(p, sem, src, dst, to):
        return remote(src, dst, p_send.at[p, sem], p_recv.at[p, sem], "mp", to)

    def hops(p, *which):
        low, high = rows_of(2 * p, PATCH // 2), rows_of(2 * p + 1, PATCH // 2)
        ends = (
            (part.at[opposite, low], rel_l.at[p], right),
            (part.at[opposite, high], rel_r.at[p], left),
            (part.at[right, high], got_l.at[high], right),
            (part.at[left, low], got_r.at[low], left),
            (rel_l.at[p], got_l.at[low], right),
            (rel_r.at[p], got_r.at[high], left),
        )
        return [hop(p, w, *ends[w]) for w in which]

    def hand_on(p):
        low, high = rows_of(2 * p, PATCH // 2), rows_of(2 * p + 1, PATCH // 2)
        in_l, in_r, out_l, out_r = hops(p, 0, 1, 4, 5)
        in_l.wait()
        rel_l[p] = (rel_l[p].astype(F32) + part[right, low, :].astype(F32)).astype(BF)
        out_l.start()
        in_r.wait()
        rel_r[p] = (rel_r[p].astype(F32) + part[left, high, :].astype(F32)).astype(BF)
        out_r.start()

    def backward(p, h, half):
        ds_ref = halves[half][2]
        i = p * HEADS + h
        c = pl.ds(half * QH, QH)
        scaled = (dat[head_rows(h), c].astype(F32) * linv[i, :, c]).astype(BF)
        da = scaled.astype(F32)
        delta = jnp.sum(da * dpt[p, head_rows(h, 3), c].astype(F32), axis=0, keepdims=True)
        d1 = delta.astype(BF).astype(F32)
        d2 = (delta - d1).astype(BF).astype(F32)
        d3 = delta - d1 - d2
        sub = iota((LANES, QH), 0)
        tile = jnp.where(sub // HD == h, jnp.concatenate([da] * HEADS, axis=0), 0.0)
        tail = jnp.where(sub == 0, -d1, jnp.where(sub == 1, -d2, jnp.where(sub == 2, -d3, 0.0)))
        vv = jnp.concatenate([vn[rows_of(p, PATCH), :], ones_lane], axis=1)
        dp = dotf(vv, jnp.concatenate([tile, tail], axis=0).astype(BF))
        ds = e_all[i, :, c] * dp.astype(BF)
        ds_ref[...] = ds
        dpt[p, head_rows(h), c] = (dotf(kt[p, head_rows(h), :], ds) * 0.25).astype(BF)
        for u in range(PATCH // CH):
            r = pl.ds(u * CH, CH)
            dst[half, :, r] = ds_ref[r, :].T
        for u in range(PATCH // CH):
            r = pl.ds(u * CH, CH)
            est[half, :, r] = e_all[i, r, c].T
        return dotf(qt[p, head_rows(h), c], dst[half]), dotf(scaled, est[half])

    def dout_in(b, _):
        arrived(dout, 1, b)
        return 0

    lax.fori_loop(0, blocks, dout_in, 0)
    ring_sent(pts, 0)
    ring_sent(dout, 1)

    def stat_copy(p, i, to):
        return remote(stats.at[p], got_s.at[p, i], s_send.at[p, i], s_recv.at[p, i], "mp", to)

    def backward_patch(p, _):
        for b in range(PBLK):
            da = dotf(lanes_of(dout, rows_of(p * PBLK + b, BLK)), wo[...]).astype(BF)
            dat[:, b * BLK : (b + 1) * BLK] = da.astype(F32).T.astype(BF)

        def step(h, _):
            @pl.when(jnp.logical_and(p == 1, h == HEADS // 2))
            def _():
                hand_on(0)

            dk0, dv0 = backward(p, h, 0)
            dk1, dv1 = backward(p, h, 1)
            dpt[p, head_rows(h, 1), :] = ((dk0 + dk1) * 0.25).astype(BF)
            dpt[p, head_rows(h, 2), :] = (dv0 + dv1).astype(BF)
            return 0

        lax.fori_loop(0, HEADS, step, 0)
        for b in range(PBLK):
            r = rows_of(p * PBLK + b, BLK)
            dproj = dpt[p, 0 : 3 * LANES, pl.ds(b * BLK, BLK)].astype(F32).T.astype(BF)
            pd = dot_nt(dproj, wcat).astype(BF)
            for j in range(m):
                part[j, r, :] = pd[:, j * LANES : (j + 1) * LANES]
            if b % 2 == 1:
                for c in hops(p, *((0,), (1, 3, 2))[b // 2]):
                    c.start()
        for b in range(PBLK):
            r = rows_of(p * PBLK + b, BLK)
            pd = lanes_of(part, r)
            gram = dot_nt(pd, hid[r, :])
            cross = jnp.sum(jnp.where(iota((BLK, BLK), 0) == iota((BLK, BLK), 1), gram, 0.0), axis=0, keepdims=True)
            total = dot_nt(jnp.ones((8, pd.shape[1]), BF), pd)
            stats[p, 2 * b : 2 * b + 1, :] = total[0:1]
            stats[p, 2 * b + 1 : 2 * b + 2, :] = cross
        for i, to in enumerate((right, left, opposite)):
            stat_copy(p, i, to).start()
        return 0

    lax.fori_loop(0, npatch, backward_patch, 0)

    upper, lower = 0.0, 0.0
    for p in range(npatch):
        r = pl.ds(p * PATCH, PATCH)
        upper = upper + dotf(dpt[p, 0 : 3 * LANES, :], hid[r, :])
        lower = lower + dotf(dpt[p, 3 * LANES : 4 * LANES, :], lanes_of(dout, r))
    grads[:, 0 : 3 * LANES] = upper.T.astype(BF)
    grads[:, 3 * LANES : 4 * LANES] = lower.T.astype(BF)
    band = grads.shape[0] // n

    def grad_copy(src, dst, peer):
        return remote(src, dst, g_send, g_recv, "seq", peer)

    def grads_out(k, _):
        peer = lax.rem(seq + k, n)
        grad_copy(grads.at[rows_of(peer, band)], got_g.at[seq], peer).start()
        return 0

    lax.fori_loop(1, n, grads_out, 0)
    got_g[seq] = grads[rows_of(seq, band), :]
    hand_on(1)
    scale = 1.0 / (m * LANES)

    def finish(p):
        for i, to in enumerate((right, left, opposite)):
            stat_copy(p, i, to).wait()
        st = (stats[p] + got_s[p, 0] + got_s[p, 1] + got_s[p, 2]) * scale
        for b in range(PBLK):
            if b % 2 == 0:
                for c in hops(p, *((3, 4), (2, 5))[b // 2]):
                    c.wait()
            r = pl.ds(p * PATCH + b * BLK, BLK)
            mean_grad = lane_copy(st[2 * b : 2 * b + 1])
            mean_cross = lane_copy(st[2 * b + 1 : 2 * b + 2])
            d_hidden = part[mp, r, :].astype(F32) + got_l[r, :].astype(F32) + got_r[r, :].astype(F32)
            grad = dout[mp, r, :].astype(F32) + invb[r, :] * (
                d_hidden - mean_grad - normq[r, :] * mean_cross
            )
            high = grad.astype(BF)
            d_high[r, :] = high
            d_low[r, :] = (grad - high.astype(F32)).astype(BF)

    finish(0)
    others = got_g.at[pl.ds(0, n - 1)]
    grad_copy(others, others, seq).wait()
    total = jnp.zeros((band, grads.shape[1]), F32)
    for k in range(n):
        total = total + got_g[k].astype(F32)
    for t in range(4):
        grad_all[t] = total[:, t * LANES : (t + 1) * LANES]
    finish(1)


def local(
    scan_points, send_order, arrive_order, qkv_weight, out_weight, voxel_grads, voxel_shard, voxel_point
):
    n, m = lax.axis_size("seq"), lax.axis_size("mp")
    rows = scan_points.shape[0]
    feats = m * LANES
    grp, cap = rows // n, 2 * voxel_grads.shape[0] // n
    blocks, npatch, band = rows // BLK, rows // PATCH, feats // n
    vmem, hbm = pl.BlockSpec(memory_space=pltpu.VMEM), pl.BlockSpec(memory_space=pl.ANY)
    dma = pltpu.SemaphoreType.DMA
    col = pltpu.VMEM((rows, LANES), BF)
    per_patch = pltpu.VMEM((npatch, LANES, PATCH), BF)
    half_f = pltpu.VMEM((PATCH, QH), F32)
    half_b = pltpu.VMEM((PATCH, QH), BF)
    masked = pltpu.VMEM((2 * LANES, QH), BF)
    coded = pltpu.VMEM((n, 16, cap), BF)
    full = pltpu.VMEM((m, rows, LANES), BF)
    hop_buf = pltpu.VMEM((npatch, PATCH // 2, LANES), BF)
    d_high, d_low, grad_all = (
        pl.pallas_call(
            layer_kernel,
            out_shape=[
                jax.ShapeDtypeStruct((rows, LANES), BF),
                jax.ShapeDtypeStruct((rows, LANES), BF),
                jax.ShapeDtypeStruct((4, band, LANES), F32),
            ],
            in_specs=[hbm, hbm] + [vmem] * 6,
            out_specs=[vmem] * 3,
            scratch_shapes=[
                pltpu.VMEM((rows, LANES), F32), col, col, col, pltpu.VMEM((n * cap, LANES), BF), coded,
                col, pltpu.VMEM((n * cap, LANES), BF), coded, pltpu.VMEM((blocks, BLK), jnp.int32), pltpu.VMEM((n, cap), F32),
                full, full, pltpu.VMEM((rows, feats), BF), col, col,
                pltpu.VMEM((npatch, 2 * LANES, PATCH), BF),
                per_patch, per_patch, per_patch, pltpu.VMEM((LANES, PATCH), BF),
                pltpu.VMEM((npatch, 4 * LANES, PATCH), BF),
                masked, masked, half_f, half_f,
                pltpu.VMEM((npatch * HEADS, PATCH, PATCH), BF),
                half_b, half_b,
                pltpu.VMEM((2, 1, QH), F32),
                pltpu.VMEM((npatch * HEADS, 1, PATCH), F32), pltpu.VMEM((2, QH, PATCH), BF), pltpu.VMEM((2, QH, PATCH), BF),
                pltpu.VMEM((feats, 4 * LANES), BF),
                pltpu.VMEM((npatch, 2 * PBLK, BLK), F32),
                pltpu.VMEM((rows, LANES), F32),
                hop_buf, hop_buf,
                pltpu.VMEM((npatch, m - 1, 2 * PBLK, BLK), F32),
                pltpu.VMEM((n, band, 4 * LANES), BF),
                dma((2,)), dma((3,)), dma((3,)), dma((2,)), dma((2, m, blocks)),
                dma((npatch, 6)), dma((npatch, 6)), dma((npatch, m - 1)), dma((npatch, m - 1)), dma(()), dma(()),
            ],
            compiler_params=pltpu.CompilerParams(
                collective_id=0, has_side_effects=True, vmem_limit_bytes=67043328
            ),
            name="layer",
        )(
            scan_points, voxel_grads,
            send_order.reshape(-1, LANES), arrive_order.reshape(-1, LANES), voxel_point.reshape(-1, LANES),
            voxel_shard.reshape(1, -1), jnp.transpose(qkv_weight, (1, 0, 2)), out_weight,
        )
    )
    return d_high.astype(F32) + d_low.astype(F32), jnp.transpose(grad_all[:3], (1, 0, 2)), grad_all[3]


def solution(mesh):
    in_specs = (
        P("seq", None), P("seq"), P("seq"), P(None, None, "mp"), P(None, "mp"),
        P("seq", None), P("seq", None), P("seq"),
    )
    out_specs = (P("seq", "mp"), P("seq", None, "mp"), P("seq", "mp"))
    return jax.shard_map(local, mesh=mesh, in_specs=in_specs, out_specs=out_specs, check_vma=False)
```

```python
import jax
import jax.numpy as jnp
from jax import lax
from jax.experimental import pallas as pl
from jax.experimental.pallas import tpu as pltpu
from jax.sharding import PartitionSpec as P

HD = 16
PATCH = 1024
LANES = 128
BLK = 256
HEADS = LANES // HD
PBLK = PATCH // BLK
QH = 512
CH = 256
EPSILON = 1e-05
LOG2E = 1.4426950408889634
BF = jnp.bfloat16
F32 = jnp.float32
MESH = pl.DeviceIdType.MESH


def dotf(a, b):
    return jnp.dot(a, b, preferred_element_type=F32)


def dot_nt(a, b):
    return lax.dot_general(a, b, (((1,), (1,)), ((), ())), preferred_element_type=F32)


def iota(shape, axis):
    return lax.broadcasted_iota(jnp.int32, shape, axis)


def as_mask(cond):
    return jnp.where(cond, 1.0, 0.0).astype(BF)


def small_iota(shape, axis):
    return iota(shape, axis).astype(F32).astype(BF)


def lane_copy(row):
    return jnp.broadcast_to(row.astype(F32), (LANES, BLK)).T


def block_row(ref, b):
    per = BLK // LANES
    return jnp.concatenate([ref[pl.ds(b * per + u, 1), :] for u in range(per)], axis=1)


def select_rows(order_row, count):
    want = lane_copy(order_row)
    high = jnp.floor(want * (1.0 / LANES))
    low = (want - high * LANES).astype(BF)
    high = high.astype(BF)
    zero = jnp.zeros((BLK, LANES), BF)
    here = jnp.where(low == small_iota((BLK, LANES), 1), jnp.ones((BLK, LANES), BF), zero)
    return jnp.concatenate([jnp.where(high == c, here, zero) for c in range(count // LANES)], axis=1)


def hits(position, b):
    shape = (BLK, position.shape[1])
    near = jnp.clip(position.astype(F32) - (b * BLK).astype(F32), -1.0, float(BLK)).astype(BF)
    return jnp.where(small_iota(shape, 0) == near, jnp.ones(shape, BF), jnp.zeros(shape, BF))


def lanes_of(ref, r):
    return jnp.concatenate([ref[j, r, :] for j in range(ref.shape[0])], axis=1)


def rows_of(block, size):
    return pl.ds(pl.multiple_of(block * size, size), size)


def remote(src, dst, send_sem, recv_sem, axis, to):
    return pltpu.make_async_remote_copy(
        src_ref=src, dst_ref=dst, send_sem=send_sem, recv_sem=recv_sem,
        device_id={axis: to}, device_id_type=MESH,
    )


def layer_kernel(
    scan, voxels, send_order, arrive_order, point, shard, w, wo,
    d_high, d_low, grad_all,
    normq, x, v, sendp, sendv, sendi, gotp, gotv, goti, place, at_all,
    pts, dout, hid, kn, vn, qhl, qt, kt, vt, dat, dpt, qm0, qm1, s0, s1, e_all, ds0, ds1, top, linv, dst, est,
    grads, stats, invb, rel_l, rel_r, got_s, got_g,
    in_sem, send_sem, recv_sem, ring_send, ring_recv, p_send, p_recv, s_send, s_recv, g_send, g_recv,
):
    seq, mp = lax.axis_index("seq"), lax.axis_index("mp")
    n, m = lax.axis_size("seq"), lax.axis_size("mp")
    rows = x.shape[0]
    npatch = rows // PATCH
    grp = rows // n
    cap = gotv.shape[0] // n
    blocks = rows // BLK
    right, left, opposite = lax.rem(mp + 1, m), lax.rem(mp + m - 1, m), lax.rem(mp + 2, m)
    part, got_l, got_r = pts, x, v

    mine = pl.ds(pl.multiple_of(mp * LANES, LANES), LANES)
    in_x = pltpu.make_async_copy(scan.at[:, mine], x, in_sem.at[0])
    in_v = pltpu.make_async_copy(voxels.at[:, mine], v, in_sem.at[1])
    in_x.start()
    in_v.start()
    barrier = pltpu.get_barrier_semaphore()
    for k in range(1, n):
        pl.semaphore_signal(barrier, inc=1, device_id={"seq": lax.rem(seq + k, n)}, device_id_type=MESH)
    for to in (right, left, opposite):
        pl.semaphore_signal(barrier, inc=1, device_id={"mp": to}, device_id_type=MESH)

    def send(src, dst, kind, peer):
        return remote(src, dst, send_sem.at[kind], recv_sem.at[kind], "seq", peer)

    tri = as_mask(iota((BLK, BLK), 0) < iota((BLK, BLK), 1))
    carry = jnp.zeros((n, 1), F32)
    codes = jnp.zeros((3 * n, cap), F32)
    for b in range(blocks):
        target = shard[:, b * BLK : (b + 1) * BLK]
        hot = jnp.where(iota((n, BLK), 0) == target, 1.0, 0.0)
        before = dotf(hot.astype(BF), tri) + carry
        rank = jnp.sum(before * hot, axis=0, keepdims=True)
        carry = carry + jnp.sum(hot, axis=1, keepdims=True)
        place[b : b + 1, :] = target * cap + rank.astype(jnp.int32)
        where_to = block_row(point, b)
        high = (where_to // 64).astype(F32)
        low = (where_to % 64).astype(F32)
        slot = as_mask(iota((cap, BLK), 0) == rank.astype(jnp.int32))
        coded = jnp.concatenate([hot * high, hot * low, hot], axis=0).astype(BF)
        codes = codes + dot_nt(coded, slot)
    sub16 = iota((16, cap), 0)
    for t in range(n):
        a, b, c = codes[t : t + 1], codes[n + t : n + t + 1], codes[2 * n + t : 2 * n + t + 1]
        sendi[t] = jnp.where(sub16 == 0, a, jnp.where(sub16 == 1, b, c)).astype(BF)
    in_x.wait()
    per = BLK // grp

    def ordered(i):
        return lax.rem(i + seq // per, blocks)

    def points_pick(i, _):
        b = ordered(i)
        hot = select_rows(block_row(send_order, b), rows)
        sendp[rows_of(b, BLK), :] = dotf(hot, x[...]).astype(BF)
        return 0

    def points_send(i, _):
        for u in range(per):
            peer = ordered(i) * per + u

            @pl.when(peer != seq)
            def _():
                send(sendp.at[rows_of(peer, grp)], gotp.at[rows_of(seq, grp)], 0, peer).start()

        return 0

    def points_out(i, _):
        points_pick(i, 0)
        points_send(i, 0)
        return 0

    lax.fori_loop(0, blocks // 2, points_pick, 0)
    pl.semaphore_wait(barrier, n + m - 2)
    lax.fori_loop(0, blocks // 2, points_send, 0)
    lax.fori_loop(blocks // 2, blocks, points_out, 0)
    gotp[rows_of(seq, grp), :] = sendp[rows_of(seq, grp), :]

    in_v.wait()
    per_v = BLK // cap
    vblocks = n // per_v

    def voxels_out(i, _):
        b = lax.rem(i + seq // per_v, vblocks)
        hot = jnp.concatenate([hits(place[c : c + 1, :], b) for c in range(blocks)], axis=1)
        sendv[rows_of(b, BLK), :] = dotf(hot, v[...]).astype(BF)
        for u in range(per_v):
            peer = b * per_v + u

            @pl.when(peer != seq)
            def _():
                send(sendv.at[rows_of(peer, cap)], gotv.at[rows_of(seq, cap)], 1, peer).start()
                send(sendi.at[peer], goti.at[seq], 2, peer).start()

        return 0

    lax.fori_loop(0, vblocks, voxels_out, 0)
    gotv[rows_of(seq, cap), :] = sendv[rows_of(seq, cap), :]
    goti[seq] = sendi[seq]

    def wait_all(kind, ref, size):
        other = ref.at[pl.ds(0, size)]
        send(other, other, kind, seq).wait_recv()
        send(other, other, kind, seq).wait_send()

    def ring(full, kind, owner, b, to):
        at = full.at[owner, rows_of(b, BLK)]
        return remote(at, at, ring_send.at[kind], ring_recv.at[kind, owner, b], "mp", to)

    def goes_right(b):
        return lax.rem(b, PBLK) < PBLK // 2

    def relay(full, kind, b):
        @pl.when(goes_right(b))
        def _():
            ring(full, kind, left, b, right).wait_recv()
            ring(full, kind, left, b, right).start()

        @pl.when(jnp.logical_not(goes_right(b)))
        def _():
            ring(full, kind, right, b, left).wait_recv()
            ring(full, kind, right, b, left).start()

    def arrived(full, kind, b):
        @pl.when(goes_right(b))
        def _():
            ring(full, kind, right, b, left).wait_recv()

        @pl.when(jnp.logical_not(goes_right(b)))
        def _():
            ring(full, kind, left, b, right).wait_recv()

        ring(full, kind, opposite, b, right).wait_recv()

    def ring_sent(full, kind):
        for _ in range(3):
            remote(full.at[0], full.at[0], ring_send.at[kind], ring_recv.at[kind, 0, 0], "mp", right).wait_send()

    wait_all(0, gotp, (n - 1) * grp)

    def points_in(b, _):
        hot = select_rows(block_row(arrive_order, b), rows)
        pts[mp, rows_of(b, BLK), :] = dotf(hot, gotp[...]).astype(BF)
        ring(pts, 0, mp, b, right).start()
        ring(pts, 0, mp, b, left).start()
        return 0

    lax.fori_loop(0, blocks, points_in, 0)
    wait_all(1, gotv, (n - 1) * cap)
    wait_all(2, goti, n - 1)
    for t in range(n):
        code = goti[t].astype(F32)
        at_all[t : t + 1, :] = jnp.where(code[2:3, :] > 0.5, code[0:1, :] * 64.0 + code[1:2, :], -1.0)

    def voxels_in(b, _):
        relay(pts, 0, b)
        hot = jnp.concatenate([hits(at_all[t : t + 1, :], b) for t in range(n)], axis=1)
        dout[mp, rows_of(b, BLK), :] = dotf(hot, gotv[...]).astype(BF)
        ring(dout, 1, mp, b, right).start()
        ring(dout, 1, mp, b, left).start()
        return 0

    lax.fori_loop(0, blocks, voxels_in, 0)

    wcat = jnp.concatenate([w[t] for t in range(3)], axis=1)
    ones_lane = as_mask(iota((PATCH, LANES), 1) < 3)
    halves = ((qm0, s0, ds0), (qm1, s1, ds1))

    def normalise(p):
        for b in range(PBLK):
            r = rows_of(p * PBLK + b, BLK)
            c = pl.ds(b * BLK, BLK)
            xb = lanes_of(pts, r).astype(F32)
            xb = xb - jnp.mean(xb, axis=1, keepdims=True)
            inv = lax.rsqrt(jnp.mean(xb * xb, axis=1, keepdims=True) + EPSILON)
            normed = xb * inv
            hidden = normed.astype(BF)
            hid[r, :] = hidden
            invb[r, :] = jnp.broadcast_to(inv, (BLK, LANES))
            own = normed[:, 0:LANES]
            for j in range(1, m):
                own = jnp.where(mp == j, normed[:, j * LANES : (j + 1) * LANES], own)
            normq[r, :] = own
            proj = dotf(hidden, wcat)
            q, k, val = (proj[:, t * LANES : (t + 1) * LANES].astype(BF) for t in range(3))
            kn[r, :] = k
            vn[r, :] = val
            qf = q.astype(F32).T
            qt[p, :, c] = qf.astype(BF)
            qs = qf * (0.25 * LOG2E)
            high = qs.astype(BF)
            qhl[p, 0:LANES, c] = high
            qhl[p, LANES : 2 * LANES, c] = (qs - high.astype(F32)).astype(BF)
            kt[p, :, c] = k.astype(F32).T.astype(BF)
            vt[p, :, c] = val.astype(F32).T.astype(BF)

    def head_rows(h, base=0):
        return pl.ds(pl.multiple_of(base * LANES + h * HD, HD), HD)

    def scores(p, h, half):
        qm, s = halves[half][:2]
        c = pl.ds(half * QH, QH)
        rmask = (iota((LANES, QH), 0) // HD) == h
        zero = jnp.zeros((LANES, QH), BF)
        qm[0:LANES, :] = jnp.where(rmask, qhl[p, 0:LANES, c], zero)
        qm[LANES : 2 * LANES, :] = jnp.where(rmask, qhl[p, LANES : 2 * LANES, c], zero)
        k = kn[rows_of(p, PATCH), :]
        val = dotf(jnp.concatenate([k, k], axis=1), qm[...])
        s[...] = val
        top[half] = jnp.max(val, axis=0, keepdims=True)

    def forward(p, h, half):
        s = halves[half][1]
        c = pl.ds(half * QH, QH)
        e = jnp.exp2(s[...] - top[half]).astype(BF)
        e_all[p * HEADS + h, :, c] = e
        vt1 = jnp.concatenate([vt[p, head_rows(h), :], jnp.ones((HD, PATCH), BF)], axis=0)
        av = dotf(vt1, e)
        inv = 1.0 / av[HD : HD + 1, :]
        linv[p * HEADS + h, :, c] = inv
        dpt[p, head_rows(h, 3), c] = (av[0:HD, :] * inv).astype(BF)

    def forward_patch(p, _):
        def ready(b, _):
            arrived(pts, 0, p * PBLK + b)
            return 0

        lax.fori_loop(0, PBLK, ready, 0)
        normalise(p)
        scores(p, 0, 0)

        def step(i, _):
            h = i // 2

            b = (p * 2 * HEADS + i - HEADS - 4) // 2

            @pl.when(jnp.logical_and(lax.rem(i, 2) == 0, jnp.logical_and(b >= 0, b < blocks)))
            def _():
                relay(dout, 1, b)

            @pl.when(lax.rem(i, 2) == 0)
            def _():
                scores(p, h, 1)
                forward(p, h, 0)

            @pl.when(jnp.logical_and(lax.rem(i, 2) == 1, h < HEADS - 1))
            def _():
                scores(p, h + 1, 0)
                forward(p, h, 1)

            @pl.when(i == 2 * HEADS - 1)
            def _():
                forward(p, HEADS - 1, 1)

            return 0

        lax.fori_loop(0, 2 * HEADS, step, 0)
        return 0

    lax.fori_loop(0, npatch, forward_patch, 0)

    def hop(p, sem, src, dst, to):
        return remote(src, dst, p_send.at[p, sem], p_recv.at[p, sem], "mp", to)

    def hops(p, *which):
        low, high = rows_of(2 * p, PATCH // 2), rows_of(2 * p + 1, PATCH // 2)
        ends = (
            (part.at[opposite, low], rel_l.at[p], right),
            (part.at[opposite, high], rel_r.at[p], left),
            (part.at[right, high], got_l.at[high], right),
            (part.at[left, low], got_r.at[low], left),
            (rel_l.at[p], got_l.at[low], right),
            (rel_r.at[p], got_r.at[high], left),
        )
        return [hop(p, w, *ends[w]) for w in which]

    def hand_on(p):
        low, high = rows_of(2 * p, PATCH // 2), rows_of(2 * p + 1, PATCH // 2)
        in_l, in_r, out_l, out_r = hops(p, 0, 1, 4, 5)
        in_l.wait()
        rel_l[p] = (rel_l[p].astype(F32) + part[right, low, :].astype(F32)).astype(BF)
        out_l.start()
        in_r.wait()
        rel_r[p] = (rel_r[p].astype(F32) + part[left, high, :].astype(F32)).astype(BF)
        out_r.start()

    def backward(p, h, half):
        ds_ref = halves[half][2]
        i = p * HEADS + h
        c = pl.ds(half * QH, QH)
        scaled = (dat[head_rows(h), c].astype(F32) * linv[i, :, c]).astype(BF)
        da = scaled.astype(F32)
        delta = jnp.sum(da * dpt[p, head_rows(h, 3), c].astype(F32), axis=0, keepdims=True)
        d1 = delta.astype(BF).astype(F32)
        d2 = (delta - d1).astype(BF).astype(F32)
        d3 = delta - d1 - d2
        sub = iota((LANES, QH), 0)
        tile = jnp.where(sub // HD == h, jnp.concatenate([da] * HEADS, axis=0), 0.0)
        tail = jnp.where(sub == 0, -d1, jnp.where(sub == 1, -d2, jnp.where(sub == 2, -d3, 0.0)))
        vv = jnp.concatenate([vn[rows_of(p, PATCH), :], ones_lane], axis=1)
        dp = dotf(vv, jnp.concatenate([tile, tail], axis=0).astype(BF))
        ds = e_all[i, :, c] * dp.astype(BF)
        ds_ref[...] = ds
        dpt[p, head_rows(h), c] = (dotf(kt[p, head_rows(h), :], ds) * 0.25).astype(BF)
        for u in range(PATCH // CH):
            r = pl.ds(u * CH, CH)
            dst[half, :, r] = ds_ref[r, :].T
        for u in range(PATCH // CH):
            r = pl.ds(u * CH, CH)
            est[half, :, r] = e_all[i, r, c].T
        return dotf(qt[p, head_rows(h), c], dst[half]), dotf(scaled, est[half])

    def dout_in(b, _):
        arrived(dout, 1, b)
        return 0

    lax.fori_loop(0, blocks, dout_in, 0)
    ring_sent(pts, 0)
    ring_sent(dout, 1)

    def stat_copy(p, i, to):
        return remote(stats.at[p], got_s.at[p, i], s_send.at[p, i], s_recv.at[p, i], "mp", to)

    def backward_patch(p, _):
        for b in range(PBLK):
            da = dotf(lanes_of(dout, rows_of(p * PBLK + b, BLK)), wo[...]).astype(BF)
            dat[:, b * BLK : (b + 1) * BLK] = da.astype(F32).T.astype(BF)

        def step(h, _):
            @pl.when(jnp.logical_and(p == 1, h == HEADS // 2))
            def _():
                hand_on(0)

            dk0, dv0 = backward(p, h, 0)
            dk1, dv1 = backward(p, h, 1)
            dpt[p, head_rows(h, 1), :] = ((dk0 + dk1) * 0.25).astype(BF)
            dpt[p, head_rows(h, 2), :] = (dv0 + dv1).astype(BF)
            return 0

        lax.fori_loop(0, HEADS, step, 0)
        for b in range(PBLK):
            r = rows_of(p * PBLK + b, BLK)
            dproj = dpt[p, 0 : 3 * LANES, pl.ds(b * BLK, BLK)].astype(F32).T.astype(BF)
            pd = dot_nt(dproj, wcat).astype(BF)
            for j in range(m):
                part[j, r, :] = pd[:, j * LANES : (j + 1) * LANES]
            if b % 2 == 1:
                for c in hops(p, *((0,), (1, 3, 2))[b // 2]):
                    c.start()
        for b in range(PBLK):
            r = rows_of(p * PBLK + b, BLK)
            pd = lanes_of(part, r)
            gram = dot_nt(pd, hid[r, :])
            cross = jnp.sum(jnp.where(iota((BLK, BLK), 0) == iota((BLK, BLK), 1), gram, 0.0), axis=0, keepdims=True)
            total = dot_nt(jnp.ones((8, pd.shape[1]), BF), pd)
            stats[p, 2 * b : 2 * b + 1, :] = total[0:1]
            stats[p, 2 * b + 1 : 2 * b + 2, :] = cross
        for i, to in enumerate((right, left, opposite)):
            stat_copy(p, i, to).start()
        return 0

    lax.fori_loop(0, npatch, backward_patch, 0)

    upper, lower = 0.0, 0.0
    for p in range(npatch):
        r = pl.ds(p * PATCH, PATCH)
        upper = upper + dotf(dpt[p, 0 : 3 * LANES, :], hid[r, :])
        lower = lower + dotf(dpt[p, 3 * LANES : 4 * LANES, :], lanes_of(dout, r))
    grads[:, 0 : 3 * LANES] = upper.T.astype(BF)
    grads[:, 3 * LANES : 4 * LANES] = lower.T.astype(BF)
    band = grads.shape[0] // n

    def grad_copy(src, dst, peer):
        return remote(src, dst, g_send, g_recv, "seq", peer)

    def grads_out(k, _):
        peer = lax.rem(seq + k, n)
        grad_copy(grads.at[rows_of(peer, band)], got_g.at[seq], peer).start()
        return 0

    lax.fori_loop(1, n, grads_out, 0)
    got_g[seq] = grads[rows_of(seq, band), :]
    hand_on(1)
    scale = 1.0 / (m * LANES)

    def finish(p):
        for i, to in enumerate((right, left, opposite)):
            stat_copy(p, i, to).wait()
        st = (stats[p] + got_s[p, 0] + got_s[p, 1] + got_s[p, 2]) * scale
        for b in range(PBLK):
            if b % 2 == 0:
                for c in hops(p, *((3, 4), (2, 5))[b // 2]):
                    c.wait()
            r = pl.ds(p * PATCH + b * BLK, BLK)
            mean_grad = lane_copy(st[2 * b : 2 * b + 1])
            mean_cross = lane_copy(st[2 * b + 1 : 2 * b + 2])
            d_hidden = part[mp, r, :].astype(F32) + got_l[r, :].astype(F32) + got_r[r, :].astype(F32)
            grad = dout[mp, r, :].astype(F32) + invb[r, :] * (
                d_hidden - mean_grad - normq[r, :] * mean_cross
            )
            high = grad.astype(BF)
            d_high[r, :] = high
            d_low[r, :] = (grad - high.astype(F32)).astype(BF)

    finish(0)
    others = got_g.at[pl.ds(0, n - 1)]
    grad_copy(others, others, seq).wait()
    total = jnp.zeros((band, grads.shape[1]), F32)
    for k in range(n):
        total = total + got_g[k].astype(F32)
    for t in range(4):
        grad_all[t] = total[:, t * LANES : (t + 1) * LANES]
    finish(1)


def local(
    scan_points, send_order, arrive_order, qkv_weight, out_weight, voxel_grads, voxel_shard, voxel_point
):
    n, m = lax.axis_size("seq"), lax.axis_size("mp")
    rows = scan_points.shape[0]
    feats = m * LANES
    grp, cap = rows // n, 2 * voxel_grads.shape[0] // n
    blocks, npatch, band = rows // BLK, rows // PATCH, feats // n
    vmem, hbm = pl.BlockSpec(memory_space=pltpu.VMEM), pl.BlockSpec(memory_space=pl.ANY)
    dma = pltpu.SemaphoreType.DMA
    col = pltpu.VMEM((rows, LANES), BF)
    per_patch = pltpu.VMEM((npatch, LANES, PATCH), BF)
    half_f = pltpu.VMEM((PATCH, QH), F32)
    half_b = pltpu.VMEM((PATCH, QH), BF)
    masked = pltpu.VMEM((2 * LANES, QH), BF)
    coded = pltpu.VMEM((n, 16, cap), BF)
    full = pltpu.VMEM((m, rows, LANES), BF)
    hop_buf = pltpu.VMEM((npatch, PATCH // 2, LANES), BF)
    d_high, d_low, grad_all = (
        pl.pallas_call(
            layer_kernel,
            out_shape=[
                jax.ShapeDtypeStruct((rows, LANES), BF),
                jax.ShapeDtypeStruct((rows, LANES), BF),
                jax.ShapeDtypeStruct((4, band, LANES), F32),
            ],
            in_specs=[hbm, hbm] + [vmem] * 6,
            out_specs=[vmem] * 3,
            scratch_shapes=[
                pltpu.VMEM((rows, LANES), F32), col, col, col, pltpu.VMEM((n * cap, LANES), BF), coded,
                col, pltpu.VMEM((n * cap, LANES), BF), coded, pltpu.VMEM((blocks, BLK), jnp.int32), pltpu.VMEM((n, cap), F32),
                full, full, pltpu.VMEM((rows, feats), BF), col, col,
                pltpu.VMEM((npatch, 2 * LANES, PATCH), BF),
                per_patch, per_patch, per_patch, pltpu.VMEM((LANES, PATCH), BF),
                pltpu.VMEM((npatch, 4 * LANES, PATCH), BF),
                masked, masked, half_f, half_f,
                pltpu.VMEM((npatch * HEADS, PATCH, PATCH), BF),
                half_b, half_b,
                pltpu.VMEM((2, 1, QH), F32),
                pltpu.VMEM((npatch * HEADS, 1, PATCH), F32), pltpu.VMEM((2, QH, PATCH), BF), pltpu.VMEM((2, QH, PATCH), BF),
                pltpu.VMEM((feats, 4 * LANES), BF),
                pltpu.VMEM((npatch, 2 * PBLK, BLK), F32),
                pltpu.VMEM((rows, LANES), F32),
                hop_buf, hop_buf,
                pltpu.VMEM((npatch, m - 1, 2 * PBLK, BLK), F32),
                pltpu.VMEM((n, band, 4 * LANES), BF),
                dma((2,)), dma((3,)), dma((3,)), dma((2,)), dma((2, m, blocks)),
                dma((npatch, 6)), dma((npatch, 6)), dma((npatch, m - 1)), dma((npatch, m - 1)), dma(()), dma(()),
            ],
            compiler_params=pltpu.CompilerParams(
                collective_id=0, has_side_effects=True, vmem_limit_bytes=67043328
            ),
            name="layer",
        )(
            scan_points, voxel_grads,
            send_order.reshape(-1, LANES), arrive_order.reshape(-1, LANES), voxel_point.reshape(-1, LANES),
            voxel_shard.reshape(1, -1), jnp.transpose(qkv_weight, (1, 0, 2)), out_weight,
        )
    )
    return d_high.astype(F32) + d_low.astype(F32), jnp.transpose(grad_all[:3], (1, 0, 2)), grad_all[3]


def solution(mesh):
    in_specs = (
        P("seq", None), P("seq"), P("seq"), P(None, None, "mp"), P(None, "mp"),
        P("seq", None), P("seq", None), P("seq"),
    )
    out_specs = (P("seq", "mp"), P("seq", None, "mp"), P("seq", "mp"))
    return jax.shard_map(local, mesh=mesh, in_specs=in_specs, out_specs=out_specs, check_vma=False)
```
